32 devices in a mesh: fsdp: 32 (over z, y, x, core).
Axes of the slice: x: 2, y: 2, z: 4, core: 2. Of those that a mesh axis runs over, the one named last changes fastest.
Arguments:
- tokens: bfloat16 [8192, 2048], P('fsdp'), may hold values from -6 to 6
- seq_lengths: int32 [32, 2], P('fsdp'), may hold values from 0 to 256, as said below
- block_counts: int32 [32], P('fsdp'), may hold values from 1 to 2, as said below
- qkv_weight: bfloat16 [2048, 6144], P('fsdp'), may hold values from -0.125 to 0.125
- qkv_bias: bfloat16 [6144], P('fsdp'), may hold values from -3 to 3
- out_weight: bfloat16 [2048, 2048], P('fsdp'), may hold values from -0.5 to 0.5
- norm1_gain: bfloat16 [2048], P('fsdp'), may hold values from 0.5 to 1.5
- norm1_bias: bfloat16 [2048], P('fsdp'), may hold values from -2 to 2
- gate_weight: bfloat16 [2048, 5632], P('fsdp'), may hold values from -0.125 to 0.125
- up_weight: bfloat16 [2048, 5632], P('fsdp'), may hold values from -0.125 to 0.125
- down_weight: bfloat16 [2048, 5632], P('fsdp'), may hold values from -0.078125 to 0.078125
- norm2_gain: bfloat16 [2048], P('fsdp'), may hold values from 0.5 to 1.5
- norm2_bias: bfloat16 [2048], P('fsdp'), may hold values from -2 to 2
- out_grad: bfloat16 [8192, 2048], P('fsdp'), may hold values from -6 to 6
Outputs:
- layer_out: bfloat16 [8192, 2048], P('fsdp')
- tokens_grad: bfloat16 [8192, 2048], P('fsdp')
- qkv_weight_grad: float32 [2048, 6144], P('fsdp')
- qkv_bias_grad: float32 [6144], P('fsdp')
- out_weight_grad: float32 [2048, 2048], P('fsdp')
- norm1_gain_grad: float32 [2048], P('fsdp')
- norm1_bias_grad: float32 [2048], P('fsdp')
- gate_weight_grad: float32 [2048, 5632], P('fsdp')
- up_weight_grad: float32 [2048, 5632], P('fsdp')
- down_weight_grad: float32 [2048, 5632], P('fsdp')
- norm2_gain_grad: float32 [2048], P('fsdp')
- norm2_bias_grad: float32 [2048], P('fsdp')
The draws below stay inside these ranges and needn't reach their ends.
Inputs may be any that keep to these rules, and one draw needn't show every extreme that they name: `seq_lengths`: entry j of a device's row is the length of the sequence that begins at its block j, or 0; block 0 always begins one; a sequence of length L fills ceil(L / 128) blocks and the next one begins right after them, up to the device's used blocks; some device holds one sequence of 256 tokens. `block_counts`: used blocks of each device, consistent with seq_lengths; some device uses all of its blocks.
All inputs are finite; a program needn't handle non-finite values.
Results may differ from the reference program's by a relative error of at most 0.014.
Values may be sent and summed in bfloat16 or wider, within the bound.
No kernel may reach another device: no remote copies, remote signals or barrier semaphores. Data moves between devices by JAX's collectives and lax.ppermute only.
A program may use at most 448 MiB of HBM per device.

```python
import jax
import jax.numpy as jnp
from jax import lax

D = 2048
HEADS = 32
HEAD = 64
ROT = 16
FF = 5632
BLOCK = 128
BLK_DEV = 2
ROWS = 8192
N_FSDP = 32


def layout_draw(key):
    count_key, full_key, cut_key, tail_key = jax.random.split(key, 4)
    block_index = jnp.arange(BLK_DEV, dtype=jnp.int32)
    devices = jnp.arange(N_FSDP, dtype=jnp.int32)
    used_blocks = jax.random.randint(count_key, (N_FSDP,), 1, BLK_DEV + 1)
    chosen = jax.random.randint(full_key, (), 0, N_FSDP)
    is_full = devices == chosen
    used_blocks = jnp.where(is_full, BLK_DEV, used_blocks).astype(jnp.int32)
    cut_flags = jax.random.randint(cut_key, (N_FSDP, BLK_DEV), 0, 2)
    begins = (block_index[None, :] == 0) | (cut_flags == 1) & (block_index[None, :] < used_blocks[:, None])
    begins = jnp.where(is_full[:, None], block_index[None, :] == 0, begins)
    later_begin = begins[:, None, :] & (block_index[None, None, :] > block_index[None, :, None])
    following = jnp.min(jnp.where(later_begin, block_index[None, None, :], used_blocks[:, None, None]), axis=2)
    span_blocks = following - block_index[None, :]
    tail_rows = jax.random.randint(tail_key, (N_FSDP, BLK_DEV), BLOCK // 2, BLOCK + 1)
    tail_rows = jnp.where(is_full[:, None], BLOCK, tail_rows)
    lengths = jnp.where(begins, BLOCK * (span_blocks - 1) + tail_rows, 0).astype(jnp.int32)
    return (lengths, used_blocks)


def draw_seq_lengths(key, part):
    return layout_draw(jax.random.fold_in(key, 11))[0]


def draw_block_counts(key, part):
    return layout_draw(jax.random.fold_in(key, 11))[1]


def steps_of(rng, dims, pieces, low, top_value):
    level, own = 1.0, jax.random.fold_in(rng, 6)
    for dim, blocks in pieces:
        draws = jnp.exp(jax.random.uniform(jax.random.fold_in(own, dim), (blocks,), jnp.float32, low / len(pieces), top_value / len(pieces)))
        level = level * jnp.repeat(draws, dims[dim] // blocks).reshape([-1 if axis == dim else 1 for axis in range(len(dims))])
    return level


def normal_values(rng, extent, width, bound, shards=(), kind=jnp.bfloat16):
    level = steps_of(rng, extent, shards, -0.22, 0.18) if shards else 1.0
    entries = jax.random.normal(rng, extent, jnp.float32) * width * level
    return jnp.minimum(jnp.maximum(entries, -bound), bound).astype(kind)


def setup_inputs(seed: int = 0) -> dict:
    seeds = jax.random.split(jax.random.key(seed), 15)
    tokens = normal_values(seeds[0], (ROWS, D), 1.0, 6.0, ((0, 32),))
    seq_lengths = draw_seq_lengths(jax.random.fold_in(seeds[14], 71), 0)
    block_counts = draw_block_counts(jax.random.fold_in(seeds[14], 71), 0)
    qkv_weight = normal_values(seeds[3], (D, 3 * D), D ** -0.5, 0.125, ((0, 32),))
    qkv_bias = normal_values(seeds[4], (3 * D,), 0.5, 3.0, ((0, 32),))
    out_weight = normal_values(seeds[5], (D, D), (D // 16) ** -0.5, 0.5, ((0, 32),))
    norm1_gain = jnp.clip(1.0 + 0.1 * jax.random.normal(seeds[6], (D,), jnp.float32), 0.5, 1.5).astype(jnp.bfloat16)
    norm1_bias = normal_values(seeds[7], (D,), 0.3, 2.0, ((0, 32),))
    gate_weight = normal_values(seeds[8], (D, FF), D ** -0.5, 0.125, ((0, 32),))
    up_weight = normal_values(seeds[9], (D, FF), D ** -0.5, 0.125, ((0, 32),))
    down_weight = normal_values(seeds[10], (D, FF), FF ** -0.5, 0.078125, ((0, 32),))
    norm2_gain = jnp.clip(1.0 + 0.1 * jax.random.normal(seeds[11], (D,), jnp.float32), 0.5, 1.5).astype(jnp.bfloat16)
    norm2_bias = normal_values(seeds[12], (D,), 0.3, 2.0, ((0, 32),))
    out_grad = normal_values(seeds[13], (ROWS, D), 1.0, 6.0, ((0, 32),))
    return {"tokens": tokens, "seq_lengths": seq_lengths, "block_counts": block_counts, "qkv_weight": qkv_weight, "qkv_bias": qkv_bias, "out_weight": out_weight, "norm1_gain": norm1_gain, "norm1_bias": norm1_bias, "gate_weight": gate_weight, "up_weight": up_weight, "down_weight": down_weight, "norm2_gain": norm2_gain, "norm2_bias": norm2_bias, "out_grad": out_grad}


@jax.custom_vjp
def low(v):
    return lax.optimization_barrier(v.astype(jnp.bfloat16)).astype(jnp.float32)

@jax.custom_vjp
def low_back(v):
    return v

def low_keep(v):
    return (low(v), None)

def low_pass(kept, grad):
    return (grad,)

def back_keep(v):
    return (v, None)

def back_low(kept, grad):
    return (low(grad),)
low.defvjp(low_keep, low_pass)
low_back.defvjp(back_keep, back_low)
eps_norm = 1e-05

def matmul(left, right):
    return jnp.dot(left, right, precision=lax.Precision.HIGHEST, preferred_element_type=jnp.float32)

def layer_norm(values, gain, shift):
    centre = values - lax.optimization_barrier(jnp.mean(values, axis=1, keepdims=True))
    spread = lax.optimization_barrier(jnp.mean(centre * centre, axis=1, keepdims=True))
    return centre * lax.rsqrt(spread + eps_norm) * gain + shift

def row_layout(lengths, used_blocks, row_count):
    block_index = jnp.arange(lengths.shape[0], dtype=jnp.int32)
    row_index = jnp.arange(row_count, dtype=jnp.int32)
    row_block = row_index // BLOCK
    began = lax.optimization_barrier(jnp.max(jnp.where((lengths[None, :] > 0) & (block_index[None, :] <= row_block[:, None]), block_index[None, :], 0), axis=1))
    position = row_index - began * BLOCK
    limit = lax.optimization_barrier(jnp.sum(jnp.where(block_index[None, :] == began[:, None], lengths[None, :], 0), axis=1))
    valid = (position < limit) & (row_block < used_blocks)
    same = (began[:, None] == began[None, :]) & (row_index[None, :] <= row_index[:, None])
    allowed = same & valid[:, None] & valid[None, :] | (row_index[:, None] == row_index[None, :])
    return (position, valid, allowed)

def rotate(values, position, direction):
    half_rot = ROT // 2
    freqs = 10000.0 ** (-2.0 * jnp.arange(half_rot, dtype=jnp.float32) / ROT)
    angle = position.astype(jnp.float32)[:, None] * freqs[None, :]
    cosine = jnp.cos(angle)[:, None, :]
    sine = direction * jnp.sin(angle)[:, None, :]
    first = values[:, :, :half_rot]
    second = values[:, :, half_rot:ROT]
    return jnp.concatenate([first * cosine - second * sine, second * cosine + first * sine, values[:, :, ROT:]], axis=2)

def one_device(inputs, lengths, used_blocks, weights):
    qkv_weight, qkv_bias, out_weight, gain_one, shift_one, gate_weight, up_weight, down_weight, gain_two, shift_two = weights
    row_count = inputs.shape[0]
    position, valid, allowed = row_layout(lengths, used_blocks, row_count)
    normed_one = low(layer_norm(inputs, gain_one, shift_one))
    qkv = low_back(matmul(normed_one, qkv_weight) + qkv_bias)
    query = low(rotate(qkv[:, :D].reshape(row_count, HEADS, HEAD), position, 1.0))
    key_rows = low(rotate(qkv[:, D:2 * D].reshape(row_count, HEADS, HEAD), position, 1.0))
    value = low(qkv[:, 2 * D:].reshape(row_count, HEADS, HEAD))
    scores = low_back(jnp.einsum('qhd,khd->hqk', query, key_rows, precision=lax.Precision.HIGHEST) * HEAD ** (-0.5))
    scores = jnp.where(allowed[None, :, :], scores, -1e+30)
    probs = low(jax.nn.softmax(scores, axis=2))
    mixed = jnp.einsum('hqk,khd->qhd', probs, value, precision=lax.Precision.HIGHEST).reshape(row_count, D)
    mixed = low(low_back(mixed))
    middle = inputs + low_back(matmul(mixed, out_weight))
    normed_two = low(layer_norm(middle, gain_two, shift_two))
    gate = low_back(matmul(normed_two, gate_weight))
    upward = low_back(matmul(normed_two, up_weight))
    hidden = low(jax.nn.silu(gate) * upward)
    down = low_back(matmul(hidden, down_weight.T))
    return jnp.where(valid[:, None], middle + down, 0.0)

def reference(tokens, seq_lengths, block_counts, qkv_weight, qkv_bias, out_weight, norm1_gain, norm1_bias, gate_weight, up_weight, down_weight, norm2_gain, norm2_bias, out_grad):
    row_count = BLOCK * BLK_DEV
    inputs = tokens.astype(jnp.float32).reshape(N_FSDP, row_count, D)
    weights = tuple((weight.astype(jnp.float32) for weight in (qkv_weight, qkv_bias, out_weight, norm1_gain, norm1_bias, gate_weight, up_weight, down_weight, norm2_gain, norm2_bias)))
    device_fn = jax.checkpoint(one_device)

    def forward(inputs, weights):

        def step(carry, element):
            return (carry, device_fn(element[0], element[1], element[2], weights))
        unused, result = lax.scan(step, jnp.zeros((), jnp.float32), (inputs, seq_lengths, block_counts))
        return result
    result, pullback = jax.vjp(forward, inputs, weights)
    input_grad, weight_grads = pullback(out_grad.astype(jnp.float32).reshape(N_FSDP, row_count, D))
    layer_out = result.reshape(N_FSDP * row_count, D).astype(jnp.bfloat16)
    tokens_grad = input_grad.reshape(N_FSDP * row_count, D).astype(jnp.bfloat16)
    return (layer_out, tokens_grad, weight_grads[0], weight_grads[1], weight_grads[2], weight_grads[3], weight_grads[4], weight_grads[5], weight_grads[6], weight_grads[7], weight_grads[8], weight_grads[9])
```

```python
import jax
import jax.numpy as jnp
from jax import lax
from jax.sharding import Mesh, PartitionSpec as P

HEAD = 64
ROT = 16
BLOCK = 128
PARTS = 8
LINE = 4

AXES = ("z", "y", "x", "c", "s")
PLANE = ("y", "x", "c")
SWAP = ((0, 1), (1, 0))
NEAR = ((0, 1), (1, 0), (2, 3), (3, 2))
FAR = ((0, 2), (1, 3), (2, 0), (3, 1))

eps_norm = 1e-05
f32 = jnp.float32
bf16 = jnp.bfloat16


def mat_rows(left, right, kind=f32):
    return lax.dot_general(
        left, right, (((0,), (0,)), ((), ())), preferred_element_type=f32
    ).astype(kind)


def mat_cols(left, right):
    return lax.dot_general(left, right, (((1,), (1,)), ((), ())), preferred_element_type=f32)


def mat(left, right):
    return jnp.dot(left, right, preferred_element_type=f32)


def over_x(values):
    return lax.ppermute(values, "x", SWAP)


def over_y(values):
    return lax.ppermute(values, "y", SWAP)


def over_c(values):
    return lax.ppermute(values, "c", SWAP)


def gather_plane(own):
    half = own.shape[0] // 2
    from_x = over_x(own)
    from_y = over_y(own)
    far_low = over_x(from_y[:half])
    far_high = over_y(from_x[half:])
    line = [own, from_x, from_y, far_low, far_high]
    return jnp.concatenate(line + [over_c(part) for part in line], axis=0)


def scatter_plane(kept, sent, rows):
    width = kept.shape[1]
    half = rows // 2
    joined = kept.reshape(4, rows, width) + over_c(sent).reshape(4, rows, width).astype(f32)
    far = joined[3].astype(bf16)
    low = over_x(far[:half]).astype(f32)
    high = over_y(far[half:]).astype(f32)
    for_x = jnp.concatenate([joined[1, :half], joined[1, half:] + high], axis=0).astype(bf16)
    for_y = jnp.concatenate([joined[2, :half] + low, joined[2, half:]], axis=0).astype(bf16)
    return joined[0] + over_x(for_x).astype(f32) + over_y(for_y).astype(f32)


def exchange(blocks, me):
    result = blocks
    for mask in range(1, PARTS):
        there = me ^ mask
        piece = lax.dynamic_index_in_dim(blocks, there, 0, keepdims=True)
        came = lax.ppermute(piece, PLANE, [(i, i ^ mask) for i in range(PARTS)])
        result = lax.dynamic_update_slice_in_dim(result, came, there, 0)
    return result


def doubled(values, axis, perm, upper):
    other = lax.ppermute(values, axis, perm)
    return jnp.where(
        upper,
        jnp.concatenate([other, values], axis=0),
        jnp.concatenate([values, other], axis=0),
    )


def halved(values, axis, perm, upper):
    half = values.shape[0] // 2
    low, high = values[:half], values[half:]
    came = lax.ppermute(jnp.where(upper, low, high), axis, perm)
    return jnp.where(upper, high, low) + came


def standardize(values):
    centre = values - jnp.mean(values, axis=1, keepdims=True)
    inverse = lax.rsqrt(jnp.mean(centre * centre, axis=1, keepdims=True) + eps_norm)
    return (centre * inverse, inverse)


def norm_back(grad_out, standard, inverse, gain):
    scaled = grad_out * gain
    inner = jnp.mean(scaled, axis=1, keepdims=True)
    along = jnp.mean(scaled * standard, axis=1, keepdims=True)
    return (
        inverse * (scaled - inner - standard * along),
        jnp.sum(grad_out * standard, axis=0),
        jnp.sum(grad_out, axis=0),
    )


def row_layout(lengths, used_blocks, row_count):
    block_index = jnp.arange(lengths.shape[0], dtype=jnp.int32)
    row_index = jnp.arange(row_count, dtype=jnp.int32)
    row_block = row_index // BLOCK
    began = jnp.max(
        jnp.where(
            (lengths[None, :] > 0) & (block_index[None, :] <= row_block[:, None]),
            block_index[None, :],
            0,
        ),
        axis=1,
    )
    position = row_index - began * BLOCK
    limit = jnp.sum(jnp.where(block_index[None, :] == began[:, None], lengths[None, :], 0), axis=1)
    valid = (position < limit) & (row_block < used_blocks)
    same = (began[:, None] == began[None, :]) & (row_index[None, :] <= row_index[:, None])
    allowed = same & valid[:, None] & valid[None, :] | (row_index[:, None] == row_index[None, :])
    return (position, valid, allowed)


def rotate(values, position, direction):
    half_rot = ROT // 2
    freqs = 10000.0 ** (-2.0 * jnp.arange(half_rot, dtype=f32) / ROT)
    angle = position.astype(f32)[..., None] * freqs
    cosine = jnp.cos(angle)[:, :, None, :]
    sine = direction * jnp.sin(angle)[:, :, None, :]
    first = values[..., :half_rot]
    second = values[..., half_rot:ROT]
    return jnp.concatenate(
        [first * cosine - second * sine, second * cosine + first * sine, values[..., ROT:]], axis=3
    )


def per_device(
    tokens,
    seq_lengths,
    block_counts,
    qkv_weight,
    qkv_bias,
    out_weight,
    norm1_gain,
    norm1_bias,
    gate_weight,
    up_weight,
    down_weight,
    norm2_gain,
    norm2_bias,
    out_grad,
):
    rows, width = tokens.shape
    share = norm1_gain.shape[0]
    bias_share = qkv_bias.shape[0]
    hidden_share = gate_weight.shape[1] // PARTS
    heads = width // HEAD // PARTS
    head_cols = heads * HEAD
    spread = lax.axis_size("s")
    factor = HEAD ** (-0.5)
    iz = lax.axis_index("z")
    iy = lax.axis_index("y")
    ix = lax.axis_index("x")
    ic = lax.axis_index("c")
    me = iy * 4 + ix * 2 + ic

    def spread_gather(values, axis):
        return lax.all_gather(values, "s", axis=axis, tiled=True) if spread > 1 else values

    def spread_scatter(values, axis):
        if spread == 1:
            return values
        return lax.psum_scatter(values, "s", scatter_dimension=axis, tiled=True)

    def line_gather(values):
        return lax.all_gather(values, "z", axis=0, tiled=True)

    def line_scatter(values):
        return lax.psum_scatter(values, "z", scatter_dimension=0, tiled=True)

    out_full = line_gather(spread_gather(out_weight, 0))

    position, valid, _ = row_layout(seq_lengths[0], block_counts[0], rows)
    packed = jnp.concatenate(
        [
            norm1_gain,
            norm1_bias,
            norm2_gain,
            norm2_bias,
            qkv_bias,
            seq_lengths[0].astype(bf16),
            block_counts.astype(bf16),
        ]
    )
    packed_size = packed.shape[0]
    packed = jnp.pad(packed, (0, -packed_size % 128))[None, :]

    qkv_blocks = (
        qkv_weight.reshape(share, 3 * heads, PARTS, HEAD)
        .transpose(2, 0, 1, 3)
        .reshape(PARTS, share, 3 * head_cols)
    )
    qkv_rows = spread_gather(exchange(qkv_blocks, me), 1)
    qkv_full = line_gather(qkv_rows.reshape(-1, 3 * head_cols))

    tokens_all = gather_plane(tokens)

    plane_pack = doubled(packed, "c", SWAP, ic == 1)
    plane_pack = doubled(plane_pack, "x", SWAP, ix == 1)
    plane_pack = doubled(plane_pack, "y", SWAP, iy == 1)
    all_pack = spread_gather(plane_pack[:, None], 1).reshape(PARTS * spread, -1)
    all_pack = doubled(all_pack, "z", NEAR, iz % 2 == 1)
    all_pack = doubled(all_pack, "z", FAR, iz >= 2)

    def vector(index):
        return all_pack[:, index * share : (index + 1) * share].reshape(width).astype(f32)

    gain_one, shift_one, gain_two, shift_two = (vector(index) for index in range(4))
    bias_full = all_pack[:, 4 * share : 4 * share + bias_share].reshape(3 * heads, PARTS, HEAD)
    bias_mine = lax.dynamic_index_in_dim(bias_full, me, 1, keepdims=False).reshape(3 * head_cols)

    relative = [core + 4 * dy + 2 * dx for core in (0, 1) for dy in (0, 1) for dx in (0, 1)]
    marks = plane_pack[:, 4 * share + bias_share : 4 * share + bias_share + 3].astype(jnp.int32)
    marks = jnp.stack(
        [lax.dynamic_index_in_dim(marks, me ^ mask, 0, keepdims=False) for mask in relative]
    )
    position_all, _, allowed_all = jax.vmap(lambda lengths, used: row_layout(lengths, used, rows))(
        marks[:, :2], marks[:, 2]
    )

    mlp_blocks = jnp.stack(
        [
            weight.reshape(share, PARTS, hidden_share).transpose(1, 0, 2)
            for weight in (gate_weight, up_weight, down_weight)
        ],
        axis=1,
    )
    mlp_rows = spread_gather(exchange(mlp_blocks, me), 2)
    gate_full, up_full, down_full = (
        line_gather(mlp_rows[:, index].reshape(-1, hidden_share)) for index in range(3)
    )

    standard_all, inverse_all = standardize(tokens_all.astype(f32))
    normed_one = (standard_all * gain_one + shift_one).astype(bf16)
    qkv = mat(normed_one, qkv_full) + bias_mine.astype(f32)

    def split_heads(values):
        return values.reshape(PARTS, rows, heads, HEAD)

    query = rotate(split_heads(qkv[:, :head_cols]), position_all, 1.0).astype(bf16)
    key_rows = rotate(
        split_heads(qkv[:, head_cols : 2 * head_cols]), position_all, 1.0
    ).astype(bf16)
    value = split_heads(qkv[:, 2 * head_cols :]).astype(bf16)
    scores = jnp.einsum("gqhd,gkhd->ghqk", query, key_rows, preferred_element_type=f32) * factor
    scores = jnp.where(allowed_all[:, None], scores, -1e30)
    expo = jnp.exp(scores - jnp.max(scores, axis=3, keepdims=True))
    probs = expo / jnp.sum(expo, axis=3, keepdims=True)
    probs_low = probs.astype(bf16)
    mixed = (
        jnp.einsum("ghqk,gkhd->gqhd", probs_low, value, preferred_element_type=f32)
        .reshape(PARTS * rows, head_cols)
        .astype(bf16)
    )
    half_rows = 4 * rows
    out_kept = mat(mixed[:half_rows], out_full)
    out_sent = mat(mixed[half_rows:], out_full).astype(bf16)
    middle = tokens.astype(f32) + scatter_plane(out_kept, out_sent, rows)

    standard_two, inverse_two = standardize(middle)
    normed_two = gather_plane((standard_two * gain_two + shift_two).astype(bf16))

    grad_top = jnp.where(valid[:, None], out_grad.astype(f32), 0.0)
    grad_low = gather_plane(grad_top.astype(bf16))

    gate = mat(normed_two, gate_full)
    upward = mat(normed_two, up_full)
    sigma = jax.nn.sigmoid(gate)
    hidden = (gate * sigma * upward).astype(bf16)
    down_grad = line_scatter(mat_rows(grad_low, hidden, bf16))
    grad_hidden = mat(grad_low, down_full)
    grad_gate = (grad_hidden * upward * sigma * (1.0 + gate * (1.0 - sigma))).astype(bf16)
    grad_up = (grad_hidden * gate * sigma).astype(bf16)

    def back_two(low, high):
        return mat_cols(grad_gate[low:high], gate_full) + mat_cols(grad_up[low:high], up_full)

    grad_normed_two = scatter_plane(
        back_two(0, half_rows), back_two(half_rows, 2 * half_rows).astype(bf16), rows
    )
    gate_grad = line_scatter(mat_rows(normed_two, grad_gate, bf16))
    up_grad = line_scatter(mat_rows(normed_two, grad_up, bf16))

    down = scatter_plane(
        mat_cols(hidden[:half_rows], down_full),
        mat_cols(hidden[half_rows:], down_full).astype(bf16),
        rows,
    )
    layer_out = jnp.where(valid[:, None], middle + down, 0.0).astype(bf16)

    grad_middle_norm, gain_two_grad, shift_two_grad = norm_back(
        grad_normed_two, standard_two, inverse_two, gain_two
    )
    grad_middle = grad_top + grad_middle_norm
    grad_branch = gather_plane(grad_middle.astype(bf16))
    out_grad_weight = line_scatter(mat_rows(mixed, grad_branch, bf16))

    grad_mixed = split_heads(mat_cols(grad_branch, out_full).astype(bf16))
    grad_probs = jnp.einsum("gqhd,gkhd->ghqk", grad_mixed, value, preferred_element_type=f32)
    row_inner = jnp.sum(grad_probs * probs, axis=3, keepdims=True)
    grad_scores = (probs * (grad_probs - row_inner)).astype(bf16)
    grad_query = (
        jnp.einsum("ghqk,gkhd->gqhd", grad_scores, key_rows, preferred_element_type=f32) * factor
    )
    grad_key = (
        jnp.einsum("ghqk,gqhd->gkhd", grad_scores, query, preferred_element_type=f32) * factor
    )
    grad_value = jnp.einsum("ghqk,gqhd->gkhd", probs_low, grad_mixed, preferred_element_type=f32)

    def join_heads(values):
        return values.reshape(PARTS * rows, head_cols)

    grad_qkv = jnp.concatenate(
        [
            join_heads(rotate(grad_query, position_all, -1.0)),
            join_heads(rotate(grad_key, position_all, -1.0)),
            join_heads(grad_value),
        ],
        axis=1,
    ).astype(bf16)
    qkv_grad = line_scatter(mat_rows(normed_one, grad_qkv, bf16))
    bias_part = jnp.sum(grad_qkv.astype(f32), axis=0).reshape(3 * heads, 1, HEAD)
    bias_grad = jnp.where(
        lax.broadcasted_iota(jnp.int32, (3 * heads, PARTS, HEAD), 1) == me, bias_part, 0.0
    )

    grad_normed_one = scatter_plane(
        mat_cols(grad_qkv[:half_rows], qkv_full),
        mat_cols(grad_qkv[half_rows:], qkv_full).astype(bf16),
        rows,
    )
    grad_input_norm, gain_one_grad, shift_one_grad = norm_back(
        grad_normed_one, standard_all[:rows], inverse_all[:rows], gain_one
    )
    tokens_grad = (grad_middle + grad_input_norm).astype(bf16)

    devices = LINE * PARTS * spread
    small = jnp.concatenate(
        [
            part.reshape(devices, -1)
            for part in (gain_one_grad, shift_one_grad, gain_two_grad, shift_two_grad, bias_grad)
        ],
        axis=1,
    )
    small = halved(small, "z", FAR, iz >= 2)
    small = halved(small, "z", NEAR, iz % 2 == 1)
    small = halved(small, "y", SWAP, iy == 1)
    small = halved(small, "x", SWAP, ix == 1)
    small = halved(small, "c", SWAP, ic == 1)
    small = spread_scatter(small, 0)[0]

    mlp_back = jnp.stack(
        [part.reshape(PARTS, -1, hidden_share) for part in (gate_grad, up_grad, down_grad)], axis=1
    )
    mlp_back = exchange(spread_scatter(mlp_back, 2), me)
    gate_share, up_share, down_share = (
        mlp_back[:, index].transpose(1, 0, 2).reshape(share, -1).astype(f32) for index in range(3)
    )
    qkv_back = exchange(spread_scatter(qkv_grad.reshape(PARTS, -1, 3 * head_cols), 1), me)
    qkv_share = (
        qkv_back.reshape(PARTS, share, 3 * heads, HEAD)
        .transpose(1, 2, 0, 3)
        .reshape(share, 3 * width)
        .astype(f32)
    )
    out_share = spread_scatter(out_grad_weight, 0).astype(f32)
    return (
        layer_out,
        tokens_grad,
        qkv_share,
        small[4 * share :],
        out_share,
        small[:share],
        small[share : 2 * share],
        gate_share,
        up_share,
        down_share,
        small[2 * share : 3 * share],
        small[3 * share : 4 * share],
    )


def solution(mesh):
    devices = mesh.devices.reshape(LINE, 2, 2, 2, -1)
    rows, flat = P(AXES, None), P(AXES)
    return jax.shard_map(
        per_device,
        mesh=Mesh(devices, AXES),
        in_specs=(
            rows,
            rows,
            flat,
            rows,
            flat,
            rows,
            flat,
            flat,
            rows,
            rows,
            rows,
            flat,
            flat,
            rows,
        ),
        out_specs=(rows, rows, rows, flat, rows, flat, flat, rows, rows, rows, flat, flat),
        check_vma=False,
    )
```

```python
import functools

import jax
import jax.numpy as jnp
from jax import lax
from jax.experimental import pallas as pl
from jax.experimental.pallas import tpu as pltpu
from jax.sharding import Mesh, PartitionSpec as P

HEAD = 64
ROT = 16
BLOCK = 128
PARTS = 8
LINE = 4
GROUPS = 4

AXES = ("z", "y", "x", "c", "s")
PLANE = ("y", "x", "c")
SWAP = ((0, 1), (1, 0))
NEAR = ((0, 1), (1, 0), (2, 3), (3, 2))
FAR = ((0, 2), (1, 3), (2, 0), (3, 1))
INNER = ((1, 2), (2, 1))
OUTWARD = ((2, 3), (1, 0))
INWARD = ((3, 2), (0, 1))

eps_norm = 1e-05
f32 = jnp.float32
bf16 = jnp.bfloat16
VMEM_BYTES = 56 * 1024 * 1024
ANYWHERE = pl.BlockSpec(memory_space=pl.ANY)


def mat_rows(left, right):
    return lax.dot_general(left, right, (((0,), (0,)), ((), ())), preferred_element_type=f32)


def mat_cols(left, right):
    return lax.dot_general(left, right, (((1,), (1,)), ((), ())), preferred_element_type=f32)


def mat(left, right):
    return jnp.dot(left, right, preferred_element_type=f32)


def over_x(values):
    return lax.ppermute(values, "x", SWAP)


def over_y(values):
    return lax.ppermute(values, "y", SWAP)


def over_c(values):
    return lax.ppermute(values, "c", SWAP)


def along_z(values, perm):
    return lax.ppermute(values, "z", perm)


def after(values, *earlier):
    return lax.optimization_barrier((values, *earlier))[0]


def gather_plane(own):
    half = own.shape[0] // 2
    from_x = over_x(own)
    from_y = over_y(own)
    line = [own, from_x, from_y, over_x(from_y[:half]), over_y(from_x[half:])]
    return line, [over_c(part) for part in line]


def scatter_plane(kept, sent, rows):
    half = rows // 2
    came = over_c(sent)

    def joined(low, high):
        return kept[low:high].astype(f32) + came[low:high].astype(f32)

    low = over_x(joined(3 * rows, 3 * rows + half).astype(bf16))
    high = over_y(joined(3 * rows + half, 4 * rows).astype(bf16))
    near_x = jnp.concatenate(
        [joined(rows, rows + half), joined(rows + half, 2 * rows) + high.astype(f32)], axis=0
    )
    near_y = jnp.concatenate(
        [joined(2 * rows, 2 * rows + half) + low.astype(f32), joined(2 * rows + half, 3 * rows)],
        axis=0,
    )
    return (
        joined(0, rows)
        + over_x(near_x.astype(bf16)).astype(f32)
        + over_y(near_y.astype(bf16)).astype(f32)
    )


def exchange(blocks, me):
    result = blocks
    for mask in range(1, PARTS):
        there = me ^ mask
        piece = lax.dynamic_index_in_dim(blocks, there, 0, keepdims=True)
        came = lax.ppermute(piece, PLANE, [(i, i ^ mask) for i in range(PARTS)])
        result = lax.dynamic_update_slice_in_dim(result, came, there, 0)
    return result


def gather_line(own):
    far = along_z(own, FAR)
    return (own, along_z(own, NEAR), far, along_z(own, INNER), along_z(far, OUTWARD))


def scatter_line(full, iz):
    blocks = full.reshape(LINE, -1, full.shape[1])

    def block(mask):
        return lax.dynamic_index_in_dim(blocks, iz ^ mask, 0, keepdims=False)

    last = block(3)
    inward = along_z(last, INWARD)
    inner = along_z(last, INNER)
    near = along_z(block(1), NEAR)
    far = along_z((block(2).astype(f32) + inward.astype(f32)).astype(bf16), FAR)
    return block(0).astype(f32) + inner.astype(f32) + near.astype(f32) + far.astype(f32)


def doubled(values, axis, perm, upper):
    other = lax.ppermute(values, axis, perm)
    return jnp.where(
        upper,
        jnp.concatenate([other, values], axis=0),
        jnp.concatenate([values, other], axis=0),
    )


def halved(values, axis, perm, upper):
    half = values.shape[0] // 2
    low, high = values[:half], values[half:]
    came = lax.ppermute(jnp.where(upper, low, high), axis, perm)
    return jnp.where(upper, high, low) + came


def standardize(values):
    centre = values - jnp.mean(values, axis=1, keepdims=True)
    inverse = lax.rsqrt(jnp.mean(centre * centre, axis=1, keepdims=True) + eps_norm)
    return (centre * inverse, inverse)


def norm_back(grad_out, standard, inverse, gain):
    scaled = grad_out * gain
    inner = jnp.mean(scaled, axis=1, keepdims=True)
    along = jnp.mean(scaled * standard, axis=1, keepdims=True)
    return (
        inverse * (scaled - inner - standard * along),
        jnp.sum(grad_out * standard, axis=0),
        jnp.sum(grad_out, axis=0),
    )


def block_marks(lengths, used_blocks):
    index = jnp.arange(lengths.shape[0], dtype=jnp.int32)
    began = jnp.max(
        jnp.where((lengths[None, :] > 0) & (index[None, :] <= index[:, None]), index[None, :], 0),
        axis=1,
    )
    limit = jnp.sum(jnp.where(index[None, :] == began[:, None], lengths[None, :], 0), axis=1)
    return jnp.stack([began, limit, (index < used_blocks).astype(jnp.int32)], axis=1).reshape(-1)


def valid_rows(marks, row_count):
    marks = marks.reshape(-1, 3)
    row = jnp.arange(row_count, dtype=jnp.int32)
    began, limit, used = (jnp.repeat(marks[:, index], BLOCK) for index in range(3))
    return (row - began * BLOCK < limit) & (used > 0)


def rotary_tables(row_count, heads):
    half_rot = ROT // 2
    freqs = 10000.0 ** (-2.0 * jnp.arange(half_rot, dtype=f32) / ROT)
    angle = jnp.arange(row_count, dtype=f32)[:, None] * freqs[None, :]
    cosine, sine = jnp.cos(angle), jnp.sin(angle)
    zero = jnp.zeros((row_count, HEAD - ROT), f32)
    none = jnp.zeros_like(sine)
    return tuple(
        jnp.tile(jnp.concatenate(parts, axis=1), (1, heads))
        for parts in (
            [cosine, cosine, zero + 1.0],
            [-sine, none, zero],
            [none, sine, zero],
        )
    )


def line_copies(pieces, target, sems):
    copies, offset = [], 0
    for index, piece in enumerate(pieces):
        size = piece.shape[0]
        copies.append(
            pltpu.make_async_copy(piece, target.at[pl.ds(offset, size)], sems.at[index])
        )
        offset += size
    return copies


def block_target(target, z, mask, size):
    return target.at[pl.ds(pl.multiple_of(jnp.bitwise_xor(z, mask) * size, size), size)]


def start_blocks(pieces, target, sems, z):
    size = pieces[0].shape[0]
    for mask in range(3):
        pltpu.make_async_copy(
            pieces[mask], block_target(target, z, mask, size), sems.at[mask]
        ).start()
    inner = jnp.logical_or(z == 1, z == 2)

    @pl.when(inner)
    def _():
        pltpu.make_async_copy(pieces[3], block_target(target, z, 3, size), sems.at[3]).start()

    @pl.when(jnp.logical_not(inner))
    def _():
        pltpu.make_async_copy(pieces[4], block_target(target, z, 3, size), sems.at[3]).start()


def wait_blocks(pieces, target, sems, z):
    size = pieces[0].shape[0]
    for mask in range(4):
        pltpu.make_async_copy(
            pieces[mask], block_target(target, z, mask, size), sems.at[mask]
        ).wait()


def begin_lines(step, lines):
    @pl.when(step == 0)
    def _():
        for copies in lines:
            for copy in copies:
                copy.start()


def await_lines(step, lines):
    for index in range(GROUPS):

        @pl.when(step == index)
        def _(index=index):
            for copies in lines:
                for copy in copies[index:] if index == GROUPS - 1 else copies[index : index + 1]:
                    copy.wait()


def row_marks(marks, group, shape, axis):
    place = lax.broadcasted_iota(jnp.int32, shape, axis)
    key = jnp.zeros(shape, jnp.int32)
    for index in range(shape[axis] // BLOCK):
        began = marks[group, 3 * index]
        limit = marks[group, 3 * index + 1]
        used = marks[group, 3 * index + 2]
        inside = jnp.logical_and(place >= index * BLOCK, place < (index + 1) * BLOCK)
        last = jnp.where(used > 0, began * BLOCK + limit, 0)
        seen = jnp.where(place < last, began, -1 - axis)
        key = jnp.where(inside, seen, key)
    return place, key


def allowed_pairs(marks, group, rows):
    row, row_key = row_marks(marks, group, (rows, 1), 0)
    column, column_key = row_marks(marks, group, (1, rows), 1)
    row = jnp.broadcast_to(row, (rows, rows))
    column = jnp.broadcast_to(column, (rows, rows))
    same = jnp.broadcast_to(row_key, (rows, rows)) == jnp.broadcast_to(column_key, (rows, rows))
    return jnp.logical_or(jnp.logical_and(same, column <= row), row == column)


def placed_table(table, marks, group, rows):
    parts = []
    for index in range(rows // BLOCK):
        start = pl.multiple_of((index - marks[group, 3 * index]) * BLOCK, BLOCK)
        parts.append(table[pl.ds(start, BLOCK), :])
    return jnp.concatenate(parts, axis=0)


def rotate(values, cosine, ahead, behind):
    width = values.shape[1]
    half_rot = ROT // 2
    return (
        values * cosine
        + pltpu.roll(values, width - half_rot, 1) * ahead
        + pltpu.roll(values, half_rot, 1) * behind
    )


def head_masks(shape, heads):
    lane = lax.broadcasted_iota(jnp.int32, shape, 1)
    return [
        jnp.logical_and(lane >= index * HEAD, lane < (index + 1) * HEAD) for index in range(heads)
    ]


def softmax_of(query, key_rows, allowed):
    scores = mat_cols(query, key_rows) * HEAD ** (-0.5)
    scores = jnp.where(allowed, scores, -1e30)
    expo = jnp.exp(scores - jnp.max(scores, axis=1, keepdims=True))
    return expo / jnp.sum(expo, axis=1, keepdims=True)


def attend_forward(first, heads, rows, half, z_ref, marks_ref, *refs):
    tokens, qkv_pieces, out_pieces = refs[0:5], refs[5:10], refs[10:15]
    gain, shift, bias, cos_ref, ahead_ref, behind_ref = refs[15:21]
    refs = refs[21 if first else 24 :]
    normed_ref, qkv_ref, mixed_ref, part_ref = refs[:4]
    token_rows, qkv_weight, out_weight, line_sems, qkv_sems, out_sems = refs[4:]
    step = pl.program_id(0)
    group = half * GROUPS + step
    z = z_ref[0]
    line = line_copies(tokens, token_rows, line_sems)
    begin_lines(step, [line])

    @pl.when(step == 0)
    def _():
        start_blocks(qkv_pieces, qkv_weight, qkv_sems, z)
        start_blocks(out_pieces, out_weight, out_sems, z)

    await_lines(step, [line])
    values = token_rows[pl.ds(pl.multiple_of(step * rows, rows), rows), :].astype(f32)
    centre = values - jnp.mean(values, axis=1, keepdims=True)
    inverse = lax.rsqrt(jnp.mean(centre * centre, axis=1, keepdims=True) + eps_norm)
    normed = (centre * inverse * gain[...] + shift[...]).astype(bf16)
    normed_ref[...] = normed

    @pl.when(step == 0)
    def _():
        wait_blocks(qkv_pieces, qkv_weight, qkv_sems, z)
        wait_blocks(out_pieces, out_weight, out_sems, z)

    width = heads * HEAD
    qkv = mat(normed, qkv_weight[...]) + bias[...]
    tables = [placed_table(ref, marks_ref, group, rows) for ref in (cos_ref, ahead_ref, behind_ref)]
    query = rotate(qkv[:, :width], *tables).astype(bf16)
    key_rows = rotate(qkv[:, width : 2 * width], *tables).astype(bf16)
    value = qkv[:, 2 * width :].astype(bf16)
    qkv_ref[:, :width] = query
    qkv_ref[:, width : 2 * width] = key_rows
    qkv_ref[:, 2 * width :] = value
    allowed = allowed_pairs(marks_ref, group, rows)
    mixed = jnp.zeros((rows, width), f32)
    for mask in head_masks((rows, width), heads):
        probs = softmax_of(jnp.where(mask, query, 0), key_rows, allowed).astype(bf16)
        mixed = jnp.where(mask, mat(probs, value), mixed)
    mixed = mixed.astype(bf16)
    mixed_ref[...] = mixed
    part_ref[...] = mat(mixed, out_weight[...]).astype(bf16)


def feed_both(first, rows, z_ref, *refs):
    normed, grads = refs[0:5], refs[5:10]
    gate_pieces, up_pieces, down_pieces = refs[10:15], refs[15:20], refs[20:25]
    refs = refs[25 if first else 30 :]
    normed_ref, grad_ref, hidden_ref, gate_ref, up_ref, back_ref, down_ref = refs[:7]
    normed_rows, grad_rows, gate_weight, up_weight, down_weight = refs[7:12]
    normed_sems, grad_sems, gate_sems, up_sems, down_sems = refs[12:]
    step = pl.program_id(0)
    z = z_ref[0]
    lines = [
        line_copies(normed, normed_rows, normed_sems),
        line_copies(grads, grad_rows, grad_sems),
    ]

    @pl.when(step == 0)
    def _():
        start_blocks(gate_pieces, gate_weight, gate_sems, z)

    begin_lines(step, lines)

    @pl.when(step == 0)
    def _():
        start_blocks(up_pieces, up_weight, up_sems, z)
        start_blocks(down_pieces, down_weight, down_sems, z)
        wait_blocks(gate_pieces, gate_weight, gate_sems, z)

    await_lines(step, lines)
    here = pl.ds(pl.multiple_of(step * rows, rows), rows)
    values = normed_rows[here, :]
    normed_ref[...] = values
    gate = mat(values, gate_weight[...])

    @pl.when(step == 0)
    def _():
        wait_blocks(up_pieces, up_weight, up_sems, z)
        wait_blocks(down_pieces, down_weight, down_sems, z)

    upward = mat(values, up_weight[...])
    sigma = jax.nn.sigmoid(gate)
    gated = gate * sigma
    hidden = (gated * upward).astype(bf16)
    hidden_ref[...] = hidden
    grad_low = grad_rows[here, :]
    grad_ref[...] = grad_low
    grad_hidden = mat(grad_low, down_weight[...])
    grad_gate = (grad_hidden * upward * sigma * (1.0 + gate * (1.0 - sigma))).astype(bf16)
    grad_up = (grad_hidden * gated).astype(bf16)
    gate_ref[...] = grad_gate
    up_ref[...] = grad_up
    back_ref[...] = (
        mat_cols(grad_gate, gate_weight[...]) + mat_cols(grad_up, up_weight[...])
    ).astype(bf16)
    down_ref[...] = mat_cols(hidden, down_weight[...]).astype(bf16)


def attend_backward(first, heads, rows, half, z_ref, marks_ref, *refs):
    branch, qkv_pieces, out_pieces = refs[0:5], refs[5:10], refs[10:15]
    saved, cos_ref, ahead_ref, behind_ref = refs[15:19]
    refs = refs[19 if first else 21 :]
    branch_ref, grad_ref, part_ref = refs[:3]
    branch_rows, qkv_weight, out_weight, line_sems, qkv_sems, out_sems = refs[3:]
    step = pl.program_id(0)
    group = half * GROUPS + step
    z = z_ref[0]
    line = line_copies(branch, branch_rows, line_sems)

    @pl.when(step == 0)
    def _():
        start_blocks(out_pieces, out_weight, out_sems, z)

    begin_lines(step, [line])

    @pl.when(step == 0)
    def _():
        start_blocks(qkv_pieces, qkv_weight, qkv_sems, z)
        wait_blocks(out_pieces, out_weight, out_sems, z)

    await_lines(step, [line])
    values = branch_rows[pl.ds(pl.multiple_of(step * rows, rows), rows), :]
    branch_ref[...] = values
    width = heads * HEAD
    factor = HEAD ** (-0.5)
    grad_mixed = mat_cols(values, out_weight[...]).astype(bf16)
    query = saved[:, :width]
    key_rows = saved[:, width : 2 * width]
    value = saved[:, 2 * width :]
    allowed = allowed_pairs(marks_ref, group, rows)
    zero = jnp.zeros((rows, width), f32)
    grad_query, grad_key, grad_value = zero, zero, zero
    for mask in head_masks((rows, width), heads):
        probs = softmax_of(jnp.where(mask, query, 0), key_rows, allowed)
        grad_probs = mat_cols(jnp.where(mask, grad_mixed, 0), value)
        inner = jnp.sum(grad_probs * probs, axis=1, keepdims=True)
        grad_scores = (probs * (grad_probs - inner)).astype(bf16)
        grad_query = jnp.where(mask, mat(grad_scores, key_rows), grad_query)
        grad_key = jnp.where(mask, mat_rows(grad_scores, query), grad_key)
        grad_value = jnp.where(mask, mat_rows(probs.astype(bf16), grad_mixed), grad_value)
    cosine, ahead, behind = (
        placed_table(ref, marks_ref, group, rows) for ref in (cos_ref, ahead_ref, behind_ref)
    )
    grads = jnp.concatenate(
        [
            rotate(grad_query * factor, cosine, -ahead, -behind),
            rotate(grad_key * factor, cosine, -ahead, -behind),
            grad_value,
        ],
        axis=1,
    ).astype(bf16)
    grad_ref[...] = grads

    @pl.when(step == 0)
    def _():
        wait_blocks(qkv_pieces, qkv_weight, qkv_sems, z)

    part_ref[...] = mat_cols(grads, qkv_weight[...]).astype(bf16)


def run_half(body, scalars, loose, blocked, whole, outputs, scratch, half, rows, prior, flops):
    loose, blocked, whole = list(loose), list(blocked), list(whole)
    kept = list(prior or [])
    out_shape, out_specs = [], []
    for width, shared in outputs:
        total = 2 * GROUPS if shared else GROUPS
        offset = half * GROUPS if shared else 0
        out_shape.append(jax.ShapeDtypeStruct((total * rows, width), bf16))
        out_specs.append(pl.BlockSpec((rows, width), lambda i, *_, offset=offset: (i + offset, 0)))
    in_specs = [ANYWHERE] * len(loose)
    for values in blocked:
        in_specs.append(
            pl.BlockSpec((rows, values.shape[1]), lambda i, *_: (i + half * GROUPS, 0))
        )
    for values in whole:
        in_specs.append(pl.BlockSpec(values.shape, lambda i, *_: (0, 0)))
    in_specs += [ANYWHERE] * len(kept)
    before = len(scalars) + len(loose) + len(blocked) + len(whole)
    moved = sum(values.size * values.dtype.itemsize for values in loose + blocked + whole)
    moved += sum(width * rows * GROUPS * 2 for width, _ in outputs)
    return pl.pallas_call(
        body,
        grid_spec=pltpu.PrefetchScalarGridSpec(
            num_scalar_prefetch=len(scalars),
            grid=(GROUPS,),
            in_specs=in_specs,
            out_specs=out_specs,
            scratch_shapes=scratch,
        ),
        out_shape=out_shape,
        input_output_aliases={before + index: index for index in range(len(kept))},
        compiler_params=pltpu.CompilerParams(
            dimension_semantics=("arbitrary",), vmem_limit_bytes=VMEM_BYTES
        ),
        cost_estimate=pl.CostEstimate(flops=flops, bytes_accessed=moved, transcendentals=0),
    )(*scalars, *loose, *blocked, *whole, *kept)


def per_device(
    tokens,
    seq_lengths,
    block_counts,
    qkv_weight,
    qkv_bias,
    out_weight,
    norm1_gain,
    norm1_bias,
    gate_weight,
    up_weight,
    down_weight,
    norm2_gain,
    norm2_bias,
    out_grad,
):
    rows, width = tokens.shape
    share = norm1_gain.shape[0]
    bias_share = qkv_bias.shape[0]
    hidden_share = gate_weight.shape[1] // PARTS
    heads = width // HEAD // PARTS
    head_cols = heads * HEAD
    spread = lax.axis_size("s")
    iz = lax.axis_index("z")
    iy = lax.axis_index("y")
    ix = lax.axis_index("x")
    ic = lax.axis_index("c")
    me = iy * 4 + ix * 2 + ic
    z_scalar = iz.astype(jnp.int32).reshape(1)

    def spread_gather(values, axis):
        return lax.all_gather(values, "s", axis=axis, tiled=True) if spread > 1 else values

    def spread_scatter(values, axis):
        if spread == 1:
            return values
        return lax.psum_scatter(values, "s", scatter_dimension=axis, tiled=True)

    out_blocks = gather_line(spread_gather(out_weight, 0))

    own_marks = block_marks(seq_lengths[0], block_counts[0])
    packed = jnp.concatenate(
        [
            norm1_gain,
            norm1_bias,
            norm2_gain,
            norm2_bias,
            qkv_bias,
            seq_lengths[0].astype(bf16),
            block_counts.astype(bf16),
        ]
    )
    packed = jnp.pad(packed, (0, -packed.shape[0] % 128))[None, :]

    qkv_parts = (
        qkv_weight.reshape(share, 3 * heads, PARTS, HEAD)
        .transpose(2, 0, 1, 3)
        .reshape(PARTS, share, 3 * head_cols)
    )
    qkv_rows = spread_gather(exchange(qkv_parts, me), 1).reshape(-1, 3 * head_cols)
    qkv_blocks = gather_line(qkv_rows)

    token_lines = gather_plane(tokens)

    plane_pack = doubled(packed, "c", SWAP, ic == 1)
    plane_pack = doubled(plane_pack, "x", SWAP, ix == 1)
    plane_pack = doubled(plane_pack, "y", SWAP, iy == 1)
    all_pack = spread_gather(plane_pack[:, None], 1).reshape(PARTS * spread, -1)
    all_pack = doubled(all_pack, "z", NEAR, iz % 2 == 1)
    all_pack = doubled(all_pack, "z", FAR, iz >= 2)

    def vector(index):
        return all_pack[:, index * share : (index + 1) * share].reshape(1, width).astype(f32)

    gain_one, shift_one, gain_two, shift_two = (vector(index) for index in range(4))
    bias_full = all_pack[:, 4 * share : 4 * share + bias_share].reshape(3 * heads, PARTS, HEAD)
    bias_mine = (
        lax.dynamic_index_in_dim(bias_full, me, 1, keepdims=False)
        .reshape(1, 3 * head_cols)
        .astype(f32)
    )

    relative = [core + 4 * dy + 2 * dx for core in (0, 1) for dy in (0, 1) for dx in (0, 1)]
    marks = plane_pack[:, 4 * share + bias_share : 4 * share + bias_share + 3].astype(jnp.int32)
    marks = jnp.stack(
        [lax.dynamic_index_in_dim(marks, me ^ mask, 0, keepdims=False) for mask in relative]
    )
    marks = jax.vmap(block_marks)(marks[:, :2], marks[:, 2])
    tables = rotary_tables(rows, heads)

    mlp_parts = jnp.stack(
        [
            weight.reshape(share, PARTS, hidden_share).transpose(1, 0, 2)
            for weight in (gate_weight, up_weight, down_weight)
        ],
        axis=1,
    )
    mlp_rows = spread_gather(exchange(mlp_parts, me), 2)
    gate_blocks, up_blocks, down_blocks = (
        gather_line(mlp_rows[:, index].reshape(-1, hidden_share)) for index in range(3)
    )

    dma = pltpu.SemaphoreType.DMA
    line_rows = GROUPS * rows

    def attention(half, prior):
        return run_half(
            functools.partial(attend_forward, prior is None, heads, rows, half),
            (z_scalar, marks),
            token_lines[half] + list(qkv_blocks) + list(out_blocks),
            (),
            (gain_one, shift_one, bias_mine) + tables,
            ((width, True), (3 * head_cols, True), (head_cols, True), (width, False)),
            [
                pltpu.VMEM((line_rows, width), bf16),
                pltpu.VMEM((width, 3 * head_cols), bf16),
                pltpu.VMEM((head_cols, width), bf16),
                dma((5,)),
                dma((4,)),
                dma((4,)),
            ],
            half,
            rows,
            prior,
            2 * line_rows * width * 4 * head_cols,
        )

    *shared, out_sent = attention(1, None)
    normed_one, saved, mixed, out_kept = attention(0, shared)
    inputs = tokens.astype(f32)
    middle = inputs + scatter_plane(out_kept, out_sent, rows)

    standard_two, inverse_two = standardize(middle)
    normed_lines = gather_plane((standard_two * gain_two + shift_two).astype(bf16))

    valid = valid_rows(own_marks, rows)[:, None]
    grad_top = jnp.where(valid, out_grad.astype(f32), 0.0)
    grad_lines = gather_plane(grad_top.astype(bf16))

    def feed(half, prior):
        return run_half(
            functools.partial(feed_both, prior is None, rows),
            (z_scalar,),
            normed_lines[half]
            + grad_lines[half]
            + list(gate_blocks)
            + list(up_blocks)
            + list(down_blocks),
            (),
            (),
            ((width, True),) * 2 + ((hidden_share, True),) * 3 + ((width, False),) * 2,
            [pltpu.VMEM((line_rows, width), bf16)] * 2
            + [pltpu.VMEM((width, hidden_share), bf16)] * 3
            + [dma((5,))] * 2
            + [dma((4,))] * 3,
            half,
            rows,
            prior,
            12 * line_rows * width * hidden_share,
        )

    *shared, back_sent, down_sent = feed(1, None)
    normed_two, grad_low, hidden, grad_gate, grad_up, back_kept, down_kept = feed(0, shared)
    grad_normed_two = scatter_plane(back_kept, back_sent, rows)
    down_grad = scatter_line(mat_rows(grad_low, hidden).astype(bf16), iz)
    gate_grad = scatter_line(mat_rows(normed_two, grad_gate).astype(bf16), iz)
    up_grad = scatter_line(mat_rows(normed_two, grad_up).astype(bf16), iz)

    grad_middle_norm, gain_two_grad, shift_two_grad = norm_back(
        grad_normed_two, standard_two, inverse_two, gain_two
    )
    grad_middle = grad_top + grad_middle_norm
    branch_lines = gather_plane(grad_middle.astype(bf16))

    down = scatter_plane(down_kept, down_sent, rows)
    layer_out = jnp.where(valid, middle + down, 0.0).astype(bf16)

    def attention_back(half, prior):
        return run_half(
            functools.partial(attend_backward, prior is None, heads, rows, half),
            (z_scalar, marks),
            branch_lines[half] + list(qkv_blocks) + list(out_blocks),
            (saved,),
            tables,
            ((width, True), (3 * head_cols, True), (width, False)),
            [
                pltpu.VMEM((line_rows, width), bf16),
                pltpu.VMEM((width, 3 * head_cols), bf16),
                pltpu.VMEM((head_cols, width), bf16),
                dma((5,)),
                dma((4,)),
                dma((4,)),
            ],
            half,
            rows,
            prior,
            2 * line_rows * width * 4 * head_cols,
        )

    *shared, input_sent = attention_back(1, None)
    grad_branch, grad_qkv, input_kept = attention_back(0, shared)
    qkv_grad = scatter_line(mat_rows(normed_one, grad_qkv).astype(bf16), iz)
    out_grad_weight = scatter_line(mat_rows(mixed, grad_branch).astype(bf16), iz)
    bias_part = jnp.sum(grad_qkv.astype(f32), axis=0).reshape(3 * heads, 1, HEAD)
    bias_grad = jnp.where(
        lax.broadcasted_iota(jnp.int32, (3 * heads, PARTS, HEAD), 1) == me, bias_part, 0.0
    )

    grad_normed_one = scatter_plane(input_kept, input_sent, rows)
    standard_one, inverse_one = standardize(inputs)
    grad_input_norm, gain_one_grad, shift_one_grad = norm_back(
        grad_normed_one, standard_one, inverse_one, gain_one
    )
    tokens_grad = (grad_middle + grad_input_norm).astype(bf16)

    devices = LINE * PARTS * spread
    small = jnp.concatenate(
        [
            part.reshape(devices, -1)
            for part in (gain_one_grad, shift_one_grad, gain_two_grad, shift_two_grad, bias_grad)
        ],
        axis=1,
    )
    small = halved(small, "z", FAR, iz >= 2)
    small = halved(small, "z", NEAR, iz % 2 == 1)
    small = halved(small, "y", SWAP, iy == 1)
    small = halved(small, "x", SWAP, ix == 1)
    small = halved(small, "c", SWAP, ic == 1)
    small = spread_scatter(small, 0)[0]

    mlp_back = jnp.stack(
        [part.reshape(PARTS, -1, hidden_share) for part in (gate_grad, up_grad, down_grad)], axis=1
    )
    mlp_back = exchange(spread_scatter(mlp_back, 2).astype(bf16), me)
    gate_share, up_share, down_share = (
        mlp_back[:, index].transpose(1, 0, 2).reshape(share, -1).astype(f32) for index in range(3)
    )
    qkv_back = spread_scatter(qkv_grad.reshape(PARTS, -1, 3 * head_cols), 1)
    qkv_back = exchange(qkv_back.astype(bf16), me)
    qkv_share = (
        qkv_back.reshape(PARTS, share, 3 * heads, HEAD)
        .transpose(1, 2, 0, 3)
        .reshape(share, 3 * width)
        .astype(f32)
    )
    out_share = spread_scatter(out_grad_weight, 0)
    return (
        layer_out,
        tokens_grad,
        qkv_share,
        small[4 * share :],
        out_share,
        small[:share],
        small[share : 2 * share],
        gate_share,
        up_share,
        down_share,
        small[2 * share : 3 * share],
        small[3 * share : 4 * share],
    )


def solution(mesh):
    devices = mesh.devices.reshape(LINE, 2, 2, 2, -1)
    rows, flat = P(AXES, None), P(AXES)
    return jax.shard_map(
        per_device,
        mesh=Mesh(devices, AXES),
        in_specs=(
            rows,
            rows,
            flat,
            rows,
            flat,
            rows,
            flat,
            flat,
            rows,
            rows,
            rows,
            flat,
            flat,
            rows,
        ),
        out_specs=(rows, rows, rows, flat, rows, flat, flat, rows, rows, rows, flat, flat),
        check_vma=False,
    )
```

```python
import functools

import jax
import jax.numpy as jnp
from jax import lax
from jax.experimental import pallas as pl
from jax.experimental.pallas import tpu as pltpu
from jax.sharding import Mesh, PartitionSpec as P

HEAD = 64
ROT = 16
BLOCK = 128
PARTS = 8
LINE = 4
GROUPS = 4

AXES = ("z", "y", "x", "c", "s")
PLANE = ("y", "x", "c")
SWAP = ((0, 1), (1, 0))
NEAR = ((0, 1), (1, 0), (2, 3), (3, 2))
FAR = ((0, 2), (1, 3), (2, 0), (3, 1))

eps_norm = 1e-05
f32 = jnp.float32
bf16 = jnp.bfloat16
VMEM_BYTES = 56 * 1024 * 1024
ANYWHERE = pl.BlockSpec(memory_space=pl.ANY)


def mat_rows(left, right):
    return lax.dot_general(left, right, (((0,), (0,)), ((), ())), preferred_element_type=f32)


def mat_cols(left, right):
    return lax.dot_general(left, right, (((1,), (1,)), ((), ())), preferred_element_type=f32)


def mat(left, right):
    return jnp.dot(left, right, preferred_element_type=f32)


def over_x(values):
    return lax.ppermute(values, "x", SWAP)


def over_y(values):
    return lax.ppermute(values, "y", SWAP)


def over_c(values):
    return lax.ppermute(values, "c", SWAP)


def gather_line(values):
    return lax.all_gather(values, "z", axis=0, tiled=True)


def scatter_line(values):
    return lax.psum_scatter(values.astype(bf16), "z", scatter_dimension=0, tiled=True)


def after(values, *earlier):
    return lax.optimization_barrier((values, *earlier))[0]


def gather_plane(own, *earlier):
    half = own.shape[0] // 2
    from_x = over_x(own)
    from_y = over_y(own)
    low, high = from_y[:half], from_x[half:]
    if earlier:
        low, high, *_ = lax.optimization_barrier((low, high, *earlier))
    line = [own, from_x, from_y, over_x(low), over_y(high)]
    return line, [over_c(part) for part in line]


def scatter_plane(kept, sent, rows, first=None, second=None):
    half = rows // 2
    came = over_c(sent)

    def joined(low, high):
        return kept[low:high].astype(f32) + came[low:high].astype(f32)

    far_low = joined(3 * rows, 3 * rows + half).astype(bf16)
    far_high = joined(3 * rows + half, 4 * rows).astype(bf16)
    done = []
    if first is not None:
        done.append(first(far_low, far_high))
    low, high = over_x(far_low), over_y(far_high)
    if done:
        low, high, _ = lax.optimization_barrier((low, high, done[0]))
    near_x = jnp.concatenate(
        [joined(rows, rows + half), joined(rows + half, 2 * rows) + high.astype(f32)], axis=0
    ).astype(bf16)
    near_y = jnp.concatenate(
        [joined(2 * rows, 2 * rows + half) + low.astype(f32), joined(2 * rows + half, 3 * rows)],
        axis=0,
    ).astype(bf16)
    if second is not None:
        done.append(second(near_x, near_y))
    last_x, last_y = over_x(near_x), over_y(near_y)
    if second is not None:
        last_x, last_y, _ = lax.optimization_barrier((last_x, last_y, done[-1]))
    total = joined(0, rows) + last_x.astype(f32) + last_y.astype(f32)
    return (total, *done) if done else total


def place_pieces(stacks, me_ref, *refs):
    result = refs[PARTS]
    for mask, piece in enumerate(refs[:PARTS]):
        there = jnp.bitwise_xor(me_ref[0], mask)
        if stacks:
            for index in range(result.shape[0]):
                result[index, there] = piece[index]
        else:
            result[there] = piece[...]


def pieces_for(blocks, me, axis=0):
    return [
        lax.dynamic_index_in_dim(blocks, me ^ mask, axis, keepdims=False) for mask in range(PARTS)
    ]


def exchange(pieces, me, shape):
    stacks = len(shape) == 4
    pieces = [
        lax.ppermute(piece, PLANE, [(i, i ^ mask) for i in range(PARTS)]) if mask else piece
        for mask, piece in enumerate(pieces)
    ]
    size = 2 * pieces[0].dtype.itemsize * PARTS * pieces[0].size
    return pl.pallas_call(
        functools.partial(place_pieces, stacks),
        in_specs=[pl.BlockSpec(memory_space=pltpu.SMEM)]
        + [pl.BlockSpec(memory_space=pltpu.VMEM)] * PARTS,
        out_specs=pl.BlockSpec(memory_space=pltpu.VMEM),
        compiler_params=pltpu.CompilerParams(vmem_limit_bytes=16 * 1024 * 1024),
        out_shape=jax.ShapeDtypeStruct(shape, pieces[0].dtype),
        cost_estimate=pl.CostEstimate(flops=0, bytes_accessed=size, transcendentals=0),
    )(me.astype(jnp.int32).reshape(1), *pieces)


def doubled(values, axis, perm, upper):
    other = lax.ppermute(values, axis, perm)
    return jnp.where(
        upper,
        jnp.concatenate([other, values], axis=0),
        jnp.concatenate([values, other], axis=0),
    )


def halved(values, axis, perm, upper):
    half = values.shape[0] // 2
    low, high = values[:half], values[half:]
    came = lax.ppermute(jnp.where(upper, low, high), axis, perm)
    return jnp.where(upper, high, low) + came


def standardize(values):
    centre = values - jnp.mean(values, axis=1, keepdims=True)
    inverse = lax.rsqrt(jnp.mean(centre * centre, axis=1, keepdims=True) + eps_norm)
    return (centre * inverse, inverse)


def norm_back(grad_out, standard, inverse, gain):
    scaled = grad_out * gain
    inner = jnp.mean(scaled, axis=1, keepdims=True)
    along = jnp.mean(scaled * standard, axis=1, keepdims=True)
    return (
        inverse * (scaled - inner - standard * along),
        jnp.sum(grad_out * standard, axis=0),
        jnp.sum(grad_out, axis=0),
    )


def block_marks(lengths, used_blocks):
    index = jnp.arange(lengths.shape[0], dtype=jnp.int32)
    began = jnp.max(
        jnp.where((lengths[None, :] > 0) & (index[None, :] <= index[:, None]), index[None, :], 0),
        axis=1,
    )
    limit = jnp.sum(jnp.where(index[None, :] == began[:, None], lengths[None, :], 0), axis=1)
    return jnp.stack([began, limit, (index < used_blocks).astype(jnp.int32)], axis=1).reshape(-1)


def valid_rows(marks, row_count):
    marks = marks.reshape(-1, 3)
    row = jnp.arange(row_count, dtype=jnp.int32)
    began, limit, used = (jnp.repeat(marks[:, index], BLOCK) for index in range(3))
    return (row - began * BLOCK < limit) & (used > 0)


def rotary_tables(row_count, heads):
    half_rot = ROT // 2
    freqs = 10000.0 ** (-2.0 * jnp.arange(half_rot, dtype=f32) / ROT)
    angle = jnp.arange(row_count, dtype=f32)[:, None] * freqs[None, :]
    cosine, sine = jnp.cos(angle), jnp.sin(angle)
    zero = jnp.zeros((row_count, HEAD - ROT), f32)
    none = jnp.zeros_like(sine)
    return tuple(
        jnp.tile(jnp.concatenate(parts, axis=1), (1, heads))
        for parts in (
            [cosine, cosine, zero + 1.0],
            [-sine, none, zero],
            [none, sine, zero],
        )
    )


def line_copies(pieces, target, sems):
    copies, offset = [], 0
    for index, piece in enumerate(pieces):
        size = piece.shape[0]
        copies.append(
            pltpu.make_async_copy(piece, target.at[pl.ds(offset, size)], sems.at[index])
        )
        offset += size
    return copies


def begin_lines(step, lines):
    @pl.when(step == 0)
    def _():
        for copies in lines:
            for copy in copies:
                copy.start()


def await_lines(step, lines, groups=1):
    steps = GROUPS // groups
    for index in range(steps):

        @pl.when(step == index)
        def _(index=index):
            for copies in lines:
                last = None if index == steps - 1 else (index + 1) * groups
                for copy in copies[index * groups : last]:
                    copy.wait()


def keep_rows(step, steps, pairs):
    @pl.when(step == steps - 1)
    def _():
        for copy in pairs:
            copy.start()


def await_kept(step, steps, pairs):
    @pl.when(step == steps - 1)
    def _():
        for copy in pairs:
            copy.wait()


def row_marks(marks, group, shape, axis):
    place = lax.broadcasted_iota(jnp.int32, shape, axis)
    key = jnp.zeros(shape, jnp.int32)
    for index in range(shape[axis] // BLOCK):
        began = marks[group, 3 * index]
        limit = marks[group, 3 * index + 1]
        used = marks[group, 3 * index + 2]
        inside = jnp.logical_and(place >= index * BLOCK, place < (index + 1) * BLOCK)
        last = jnp.where(used > 0, began * BLOCK + limit, 0)
        seen = jnp.where(place < last, began, -1 - axis)
        key = jnp.where(inside, seen, key)
    return place, key


def allowed_pairs(marks, group, rows):
    row, row_key = row_marks(marks, group, (rows, 1), 0)
    column, column_key = row_marks(marks, group, (1, rows), 1)
    row = jnp.broadcast_to(row, (rows, rows))
    column = jnp.broadcast_to(column, (rows, rows))
    same = jnp.broadcast_to(row_key, (rows, rows)) == jnp.broadcast_to(column_key, (rows, rows))
    return jnp.logical_or(jnp.logical_and(same, column <= row), row == column)


def placed_table(table, marks, group, rows):
    parts = []
    for index in range(rows // BLOCK):
        start = pl.multiple_of((index - marks[group, 3 * index]) * BLOCK, BLOCK)
        parts.append(table[pl.ds(start, BLOCK), :])
    return jnp.concatenate(parts, axis=0)


def rotate(values, cosine, ahead, behind):
    width = values.shape[1]
    half_rot = ROT // 2
    return (
        values * cosine
        + pltpu.roll(values, width - half_rot, 1) * ahead
        + pltpu.roll(values, half_rot, 1) * behind
    )


def head_masks(shape, heads):
    lane = lax.broadcasted_iota(jnp.int32, shape, 1)
    return [
        jnp.logical_and(lane >= index * HEAD, lane < (index + 1) * HEAD) for index in range(heads)
    ]


def softmax_of(query, key_rows, allowed):
    scores = mat_cols(query, key_rows) * HEAD ** (-0.5)
    scores = jnp.where(allowed, scores, -1e30)
    expo = jnp.exp(scores - jnp.max(scores, axis=1, keepdims=True))
    return expo / jnp.sum(expo, axis=1, keepdims=True)


def attend_forward(first, heads, rows, half, marks_ref, *refs):
    tokens = refs[0:5]
    qkv_weight, out_weight, gain, shift, bias, cos_ref, ahead_ref, behind_ref = refs[5:13]
    refs = refs[13 if first else 16 :]
    normed_ref, qkv_ref, mixed_ref, part_ref, token_rows, line_sems = refs
    step = pl.program_id(0)
    group = half * GROUPS + step
    line = line_copies(tokens, token_rows, line_sems)
    begin_lines(step, [line])
    await_lines(step, [line])
    values = token_rows[pl.ds(pl.multiple_of(step * rows, rows), rows), :].astype(f32)
    centre = values - jnp.mean(values, axis=1, keepdims=True)
    inverse = lax.rsqrt(jnp.mean(centre * centre, axis=1, keepdims=True) + eps_norm)
    normed = (centre * inverse * gain[...] + shift[...]).astype(bf16)
    normed_ref[...] = normed
    width = heads * HEAD
    qkv = mat(normed, qkv_weight[...]) + bias[...]
    tables = [placed_table(ref, marks_ref, group, rows) for ref in (cos_ref, ahead_ref, behind_ref)]
    query = rotate(qkv[:, :width], *tables).astype(bf16)
    key_rows = rotate(qkv[:, width : 2 * width], *tables).astype(bf16)
    value = qkv[:, 2 * width :].astype(bf16)
    qkv_ref[:, :width] = query
    qkv_ref[:, width : 2 * width] = key_rows
    qkv_ref[:, 2 * width :] = value
    allowed = allowed_pairs(marks_ref, group, rows)
    mixed = jnp.zeros((rows, width), f32)
    for mask in head_masks((rows, width), heads):
        probs = softmax_of(jnp.where(mask, query, 0), key_rows, allowed).astype(bf16)
        mixed = jnp.where(mask, mat(probs, value), mixed)
    mixed = mixed.astype(bf16)
    mixed_ref[...] = mixed
    part_ref[...] = mat(mixed, out_weight[...]).astype(bf16)


def feed_both(first, rows, half, *refs):
    normed, grads, weights = refs[0:5], refs[5:10], refs[10]
    refs = refs[11 if first else 15 :]
    normed_ref, grad_ref, hidden_ref, both_ref, back_ref, down_ref = refs[:6]
    normed_rows, grad_rows, gate_weight, up_weight, down_weight = refs[6:11]
    normed_sems, grad_sems, weight_sems, keep_sems = refs[11:]
    step = pl.program_id(0)
    groups = rows * GROUPS // normed_rows.shape[0]
    steps = GROUPS // groups
    place = pl.ds(half * normed_rows.shape[0], normed_rows.shape[0])
    kept = [
        pltpu.make_async_copy(normed_rows, normed_ref.at[place], keep_sems.at[0]),
        pltpu.make_async_copy(grad_rows, grad_ref.at[place], keep_sems.at[1]),
    ]
    size = gate_weight.shape[0] // LINE
    loads = [
        [
            pltpu.make_async_copy(
                weights.at[place, index],
                target.at[pl.ds(place * size, size)],
                weight_sems.at[LINE * index + place],
            )
            for place in range(LINE)
        ]
        for index, target in enumerate((gate_weight, up_weight, down_weight))
    ]
    lines = [
        line_copies(normed, normed_rows, normed_sems),
        line_copies(grads, grad_rows, grad_sems),
    ]

    @pl.when(step == 0)
    def _():
        for copy in loads[0]:
            copy.start()

    begin_lines(step, lines)

    @pl.when(step == 0)
    def _():
        for copy in loads[1] + loads[2]:
            copy.start()
        for copy in loads[0]:
            copy.wait()

    await_lines(step, lines, groups)
    keep_rows(step, steps, kept)
    here = pl.ds(pl.multiple_of(step * rows, rows), rows)
    values = normed_rows[here, :]
    gate = mat(values, gate_weight[...])

    @pl.when(step == 0)
    def _():
        for copy in loads[1] + loads[2]:
            copy.wait()

    upward = mat(values, up_weight[...])
    sigma = jax.nn.sigmoid(gate)
    gated = gate * sigma
    hidden = (gated * upward).astype(bf16)
    hidden_ref[...] = hidden
    grad_low = grad_rows[here, :]
    grad_hidden = mat(grad_low, down_weight[...])
    grad_gate = (grad_hidden * upward * sigma * (1.0 + gate * (1.0 - sigma))).astype(bf16)
    grad_up = (grad_hidden * gated).astype(bf16)
    columns = hidden.shape[1]
    both_ref[:, :columns] = grad_gate
    both_ref[:, columns:] = grad_up
    back_ref[...] = (
        mat_cols(grad_gate, gate_weight[...]) + mat_cols(grad_up, up_weight[...])
    ).astype(bf16)
    down_ref[...] = mat_cols(hidden, down_weight[...]).astype(bf16)
    await_kept(step, steps, kept)


def attend_backward(first, heads, rows, half, marks_ref, *refs):
    branch = refs[0:5]
    saved, qkv_weight, out_weight, cos_ref, ahead_ref, behind_ref = refs[5:11]
    refs = refs[11 if first else 13 :]
    branch_ref, grad_ref, part_ref, branch_rows, line_sems, keep_sems = refs
    step = pl.program_id(0)
    group = half * GROUPS + step
    line = line_copies(branch, branch_rows, line_sems)
    place = pl.ds(half * GROUPS * rows, GROUPS * rows)
    kept = [pltpu.make_async_copy(branch_rows, branch_ref.at[place], keep_sems.at[0])]
    begin_lines(step, [line])
    await_lines(step, [line])
    keep_rows(step, GROUPS, kept)
    values = branch_rows[pl.ds(pl.multiple_of(step * rows, rows), rows), :]
    width = heads * HEAD
    factor = HEAD ** (-0.5)
    grad_mixed = mat_cols(values, out_weight[...]).astype(bf16)
    query = saved[:, :width]
    key_rows = saved[:, width : 2 * width]
    value = saved[:, 2 * width :]
    allowed = allowed_pairs(marks_ref, group, rows)
    zero = jnp.zeros((rows, width), f32)
    grad_query, grad_key, grad_value = zero, zero, zero
    for mask in head_masks((rows, width), heads):
        probs = softmax_of(jnp.where(mask, query, 0), key_rows, allowed)
        grad_probs = mat_cols(jnp.where(mask, grad_mixed, 0), value)
        inner = jnp.sum(grad_probs * probs, axis=1, keepdims=True)
        grad_scores = (probs * (grad_probs - inner)).astype(bf16)
        grad_query = jnp.where(mask, mat(grad_scores, key_rows), grad_query)
        grad_key = jnp.where(mask, mat_rows(grad_scores, query), grad_key)
        grad_value = jnp.where(mask, mat_rows(probs.astype(bf16), grad_mixed), grad_value)
    cosine, ahead, behind = (
        placed_table(ref, marks_ref, group, rows) for ref in (cos_ref, ahead_ref, behind_ref)
    )
    grads = jnp.concatenate(
        [
            rotate(grad_query * factor, cosine, -ahead, -behind),
            rotate(grad_key * factor, cosine, -ahead, -behind),
            grad_value,
        ],
        axis=1,
    ).astype(bf16)
    grad_ref[...] = grads
    part_ref[...] = mat_cols(grads, qkv_weight[...]).astype(bf16)
    await_kept(step, GROUPS, kept)


def run_half(body, scalars, loose, blocked, whole, outputs, scratch, half, rows, prior, steps=GROUPS):
    loose, blocked, whole = list(loose), list(blocked), list(whole)
    kept = list(prior or [])
    out_shape, out_specs = [], []
    for width, shared, by_copy in outputs:
        total = 2 * steps if shared else steps
        offset = half * steps if shared else 0
        out_shape.append(jax.ShapeDtypeStruct((total * rows, width), bf16))
        block = pl.BlockSpec((rows, width), lambda i, *_, offset=offset: (i + offset, 0))
        out_specs.append(ANYWHERE if by_copy else block)
    in_specs = [ANYWHERE] * len(loose)
    for values in blocked:
        in_specs.append(pl.BlockSpec((rows, values.shape[1]), lambda i, *_: (i + half * steps, 0)))
    for values in whole:
        in_specs.append(
            pl.BlockSpec(values.shape, lambda i, *_: (0, 0), pipeline_mode=pl.Buffered(1))
        )
    in_specs += [ANYWHERE] * len(kept)
    before = len(scalars) + len(loose) + len(blocked) + len(whole)
    return pl.pallas_call(
        body,
        grid_spec=pltpu.PrefetchScalarGridSpec(
            num_scalar_prefetch=len(scalars),
            grid=(steps,),
            in_specs=in_specs,
            out_specs=out_specs,
            scratch_shapes=scratch,
        ),
        out_shape=out_shape,
        input_output_aliases={before + index: index for index in range(len(kept))},
        compiler_params=pltpu.CompilerParams(
            dimension_semantics=("arbitrary",), vmem_limit_bytes=VMEM_BYTES
        ),
        cost_estimate=pl.CostEstimate(flops=1, bytes_accessed=1, transcendentals=0),
    )(*scalars, *loose, *blocked, *whole, *kept)


def per_device(
    tokens,
    seq_lengths,
    block_counts,
    qkv_weight,
    qkv_bias,
    out_weight,
    norm1_gain,
    norm1_bias,
    gate_weight,
    up_weight,
    down_weight,
    norm2_gain,
    norm2_bias,
    out_grad,
):
    rows, width = tokens.shape
    share = norm1_gain.shape[0]
    bias_share = qkv_bias.shape[0]
    hidden_share = gate_weight.shape[1] // PARTS
    heads = width // HEAD // PARTS
    head_cols = heads * HEAD
    spread = lax.axis_size("s")
    iz = lax.axis_index("z")
    iy = lax.axis_index("y")
    ix = lax.axis_index("x")
    ic = lax.axis_index("c")
    me = iy * 4 + ix * 2 + ic

    def spread_gather(values, axis):
        return lax.all_gather(values, "s", axis=axis, tiled=True) if spread > 1 else values

    def spread_scatter(values, axis):
        if spread == 1:
            return values
        return lax.psum_scatter(values, "s", scatter_dimension=axis, tiled=True)

    own_marks = block_marks(seq_lengths[0], block_counts[0])
    packed = jnp.concatenate(
        [
            norm1_gain,
            norm1_bias,
            norm2_gain,
            norm2_bias,
            qkv_bias,
            seq_lengths[0].astype(bf16),
            block_counts.astype(bf16),
        ]
    )
    packed = jnp.pad(packed, (0, -packed.shape[0] % 128))[None, :]

    qkv_parts = (
        qkv_weight.reshape(share, 3 * heads, PARTS, HEAD)
        .transpose(2, 0, 1, 3)
        .reshape(PARTS, share, 3 * head_cols)
    )
    qkv_rows = exchange(pieces_for(qkv_parts, me), me, qkv_parts.shape)
    qkv_rows = spread_gather(qkv_rows, 1).reshape(-1, 3 * head_cols)
    qkv_full = gather_line(qkv_rows)
    out_full = gather_line(spread_gather(out_weight, 0))

    plane_pack = doubled(packed, "c", SWAP, ic == 1)
    plane_pack = doubled(plane_pack, "x", SWAP, ix == 1)
    plane_pack = doubled(plane_pack, "y", SWAP, iy == 1)
    all_pack = spread_gather(plane_pack[:, None], 1).reshape(PARTS * spread, -1)
    all_pack = doubled(all_pack, "z", NEAR, iz % 2 == 1)
    all_pack = doubled(all_pack, "z", FAR, iz >= 2)

    def vector(index):
        return all_pack[:, index * share : (index + 1) * share].reshape(1, width).astype(f32)

    gain_one, shift_one, gain_two, shift_two = (vector(index) for index in range(4))
    bias_full = all_pack[:, 4 * share : 4 * share + bias_share].reshape(3 * heads, PARTS, HEAD)
    bias_mine = (
        lax.dynamic_index_in_dim(bias_full, me, 1, keepdims=False)
        .reshape(1, 3 * head_cols)
        .astype(f32)
    )

    relative = [core + 4 * dy + 2 * dx for core in (0, 1) for dy in (0, 1) for dx in (0, 1)]
    marks = plane_pack[:, 4 * share + bias_share : 4 * share + bias_share + 3].astype(jnp.int32)
    marks = jnp.stack(
        [lax.dynamic_index_in_dim(marks, me ^ mask, 0, keepdims=False) for mask in relative]
    )
    marks = jax.vmap(block_marks)(marks[:, :2], marks[:, 2])
    tables = rotary_tables(rows, heads)

    mlp_parts = jnp.stack(
        [
            weight.reshape(share, PARTS, hidden_share).transpose(1, 0, 2)
            for weight in (gate_weight, up_weight, down_weight)
        ]
    )
    mlp_pieces = pieces_for(mlp_parts, me, 1)
    token_lines = gather_plane(tokens, *mlp_pieces)
    mlp_rows = spread_gather(exchange(mlp_pieces, me, mlp_parts.shape), 2)
    mlp_full = gather_line(mlp_rows.reshape(-1, hidden_share))
    mlp_full = mlp_full.reshape(LINE, 3, -1, hidden_share)

    valid = valid_rows(own_marks, rows)[:, None]
    grad_top = jnp.where(valid, out_grad.astype(f32), 0.0)
    grad_lines = gather_plane(after(grad_top.astype(bf16), token_lines[0][3], token_lines[0][4]))

    dma = pltpu.SemaphoreType.DMA
    line_rows = GROUPS * rows

    def attention(half, prior):
        return run_half(
            functools.partial(attend_forward, prior is None, heads, rows, half),
            (after(marks, mlp_rows, *grad_lines[0][:3]) if prior is None else marks,),
            token_lines[half],
            (),
            (qkv_full, out_full, gain_one, shift_one, bias_mine) + tables,
            (
                (width, True, False),
                (3 * head_cols, True, False),
                (head_cols, True, False),
                (width, False, False),
            ),
            [
                pltpu.VMEM((line_rows, width), bf16),
                dma((5,)),
            ],
            half,
            rows,
            prior,
        )

    *shared, out_sent = attention(1, None)
    normed_one, saved, mixed, out_kept = attention(0, shared)
    out_sent = after(out_sent, *grad_lines[0])
    inputs = tokens.astype(f32)
    middle = inputs + scatter_plane(out_kept, out_sent, rows)

    standard_two, inverse_two = standardize(middle)
    normed_lines = gather_plane((standard_two * gain_two + shift_two).astype(bf16))

    def feed(half, prior):
        return run_half(
            functools.partial(feed_both, prior is None, 2 * rows, half),
            (),
            normed_lines[half] + grad_lines[half] + [mlp_full],
            (),
            (),
            ((width, True, True),) * 2
            + ((hidden_share, True, False), (2 * hidden_share, True, False))
            + ((width, False, False),) * 2,
            [pltpu.VMEM((line_rows, width), bf16)] * 2
            + [pltpu.VMEM((width, hidden_share), bf16)] * 3
            + [dma((5,)), dma((5,)), dma((3 * LINE,)), dma((2,))],
            half,
            2 * rows,
            prior,
            GROUPS // 2,
        )

    *shared, back_sent, down_sent = feed(1, None)
    normed_two, grad_low, hidden, grad_both, back_kept, down_kept = feed(0, shared)
    grad_normed_two, down_part, both_part = scatter_plane(
        back_kept,
        back_sent,
        rows,
        lambda *far: mat_rows(after(grad_low, *far), hidden).astype(bf16),
        lambda *near: mat_rows(after(normed_two, *near), grad_both).astype(bf16),
    )
    down_grad = scatter_line(down_part)
    both_grad = scatter_line(both_part)

    grad_middle_norm, gain_two_grad, shift_two_grad = norm_back(
        grad_normed_two, standard_two, inverse_two, gain_two
    )
    grad_middle = grad_top + grad_middle_norm
    branch_lines = gather_plane(grad_middle.astype(bf16))

    def attention_back(half, prior, *earlier):
        return run_half(
            functools.partial(attend_backward, prior is None, heads, rows, half),
            (after(marks, *earlier),),
            branch_lines[half],
            (saved,),
            (qkv_full, out_full) + tables,
            ((width, True, True), (3 * head_cols, True, False), (width, False, False)),
            [
                pltpu.VMEM((line_rows, width), bf16),
                dma((5,)),
                dma((1,)),
            ],
            half,
            rows,
            prior,
        )

    backs = []

    def back_first(*far):
        backs.append(attention_back(1, None, down_grad, *far))
        return backs[0][2]

    def back_second(*near):
        backs.append(attention_back(0, backs[0][:2], *near))
        return backs[1][2]

    down, input_sent, input_kept = scatter_plane(
        down_kept, after(down_sent, grad_middle), rows, back_first, back_second
    )
    layer_out = jnp.where(valid, middle + down, 0.0).astype(bf16)
    grad_branch, grad_qkv, _ = backs[1]
    grad_normed_one, qkv_part, out_part = scatter_plane(
        input_kept,
        input_sent,
        rows,
        lambda *far: mat_rows(after(normed_one, *far), grad_qkv).astype(bf16),
        lambda *near: mat_rows(after(mixed, *near), grad_branch).astype(bf16),
    )
    qkv_grad = scatter_line(qkv_part)
    grad_normed_one = after(grad_normed_one, both_grad)
    bias_part = jnp.sum(grad_qkv.astype(f32), axis=0).reshape(3 * heads, 1, HEAD)
    bias_grad = jnp.where(
        lax.broadcasted_iota(jnp.int32, (3 * heads, PARTS, HEAD), 1) == me, bias_part, 0.0
    )

    standard_one, inverse_one = standardize(inputs)
    grad_input_norm, gain_one_grad, shift_one_grad = norm_back(
        grad_normed_one, standard_one, inverse_one, gain_one
    )
    tokens_grad = (grad_middle + grad_input_norm).astype(bf16)

    devices = LINE * PARTS * spread
    small = jnp.concatenate(
        [
            part.reshape(devices, -1)
            for part in (gain_one_grad, shift_one_grad, gain_two_grad, shift_two_grad, bias_grad)
        ],
        axis=1,
    )
    small = halved(small, "z", FAR, iz >= 2)
    small = halved(small, "z", NEAR, iz % 2 == 1)
    small = halved(small, "y", SWAP, iy == 1)
    small = halved(small, "x", SWAP, ix == 1)
    small = halved(small, "c", SWAP, ic == 1)
    small = spread_scatter(small, 0)[0]

    def back_blocks(values):
        return spread_scatter(values.reshape(PARTS, -1, values.shape[1]), 1)

    def send_back(blocks):
        return exchange(pieces_for(blocks, me), me, blocks.shape)

    def in_rows(blocks):
        return blocks.transpose(1, 0, 2).astype(f32)

    down_back = send_back(back_blocks(after(down_grad, grad_normed_one)))
    both_back = send_back(back_blocks(after(both_grad, grad_normed_one)))
    qkv_blocks = back_blocks(after(qkv_grad, down_back, both_back))
    qkv_pieces = pieces_for(qkv_blocks, me)
    down_back, both_back, *_ = lax.optimization_barrier((down_back, both_back, *qkv_pieces))
    down_share = in_rows(down_back).reshape(share, -1)
    both_back = in_rows(both_back)
    gate_share = both_back[:, :, :hidden_share].reshape(share, -1)
    up_share = both_back[:, :, hidden_share:].reshape(share, -1)
    qkv_back = in_rows(exchange(qkv_pieces, me, qkv_blocks.shape))
    out_grad_weight = scatter_line(after(out_part, qkv_grad))
    qkv_share = (
        qkv_back.reshape(share, PARTS, 3 * heads, HEAD).transpose(0, 2, 1, 3).reshape(share, 3 * width)
    )
    out_share = spread_scatter(out_grad_weight, 0).astype(f32)
    return (
        layer_out,
        tokens_grad,
        qkv_share,
        small[4 * share :],
        out_share,
        small[:share],
        small[share : 2 * share],
        gate_share,
        up_share,
        down_share,
        small[2 * share : 3 * share],
        small[3 * share : 4 * share],
    )


def solution(mesh):
    devices = mesh.devices.reshape(LINE, 2, 2, 2, -1)
    rows, flat = P(AXES, None), P(AXES)
    return jax.shard_map(
        per_device,
        mesh=Mesh(devices, AXES),
        in_specs=(
            rows,
            rows,
            flat,
            rows,
            flat,
            rows,
            flat,
            flat,
            rows,
            rows,
            rows,
            flat,
            flat,
            rows,
        ),
        out_specs=(rows, rows, rows, flat, rows, flat, flat, rows, rows, rows, flat, flat),
        check_vma=False,
    )
```

```python
import functools

import jax
import jax.numpy as jnp
from jax import lax
from jax.experimental import pallas as pl
from jax.experimental.pallas import tpu as pltpu
from jax.sharding import Mesh, PartitionSpec as P

HEAD = 64
ROT = 16
BLOCK = 128
PARTS = 8
LINE = 4
GROUPS = 4

AXES = ("z", "y", "x", "c", "s")
PLANE = ("y", "x", "c")
SWAP = ((0, 1), (1, 0))
NEAR = ((0, 1), (1, 0), (2, 3), (3, 2))
FAR = ((0, 2), (1, 3), (2, 0), (3, 1))

eps_norm = 1e-05
f32 = jnp.float32
bf16 = jnp.bfloat16
VMEM_BYTES = 56 * 1024 * 1024
ANYWHERE = pl.BlockSpec(memory_space=pl.ANY)


def mat_rows(left, right):
    return lax.dot_general(left, right, (((0,), (0,)), ((), ())), preferred_element_type=f32)


def mat_cols(left, right):
    return lax.dot_general(left, right, (((1,), (1,)), ((), ())), preferred_element_type=f32)


def mat(left, right):
    return jnp.dot(left, right, preferred_element_type=f32)


def over_x(values):
    return lax.ppermute(values, "x", SWAP)


def over_y(values):
    return lax.ppermute(values, "y", SWAP)


def over_c(values):
    return lax.ppermute(values, "c", SWAP)


def gather_line(values):
    return lax.all_gather(values, "z", axis=0, tiled=True)


def scatter_line(values):
    return lax.psum_scatter(values.astype(bf16), "z", scatter_dimension=0, tiled=True)


def after(values, *earlier):
    return lax.optimization_barrier((values, *earlier))[0]


def gather_plane(own, *earlier):
    half = own.shape[0] // 2
    from_x = over_x(own)
    from_y = over_y(own)
    low, high = from_y[:half], from_x[half:]
    if earlier:
        low, high, *_ = lax.optimization_barrier((low, high, *earlier))
    line = [own, from_x, from_y, over_x(low), over_y(high)]
    return line, [over_c(part) for part in line]


def scatter_plane(kept, sent, rows, first=None, second=None):
    half = rows // 2
    came = over_c(sent)

    def joined(low, high):
        return kept[low:high].astype(f32) + came[low:high].astype(f32)

    far_low = joined(3 * rows, 3 * rows + half).astype(bf16)
    far_high = joined(3 * rows + half, 4 * rows).astype(bf16)
    done = []
    if first is not None:
        done.append(first(far_low, far_high))
    low, high = over_x(far_low), over_y(far_high)
    if done:
        low, high, _ = lax.optimization_barrier((low, high, done[0]))
    near_x = jnp.concatenate(
        [joined(rows, rows + half), joined(rows + half, 2 * rows) + high.astype(f32)], axis=0
    ).astype(bf16)
    near_y = jnp.concatenate(
        [joined(2 * rows, 2 * rows + half) + low.astype(f32), joined(2 * rows + half, 3 * rows)],
        axis=0,
    ).astype(bf16)
    if second is not None:
        done.append(second(near_x, near_y))
    last_x, last_y = over_x(near_x), over_y(near_y)
    if second is not None:
        last_x, last_y, _ = lax.optimization_barrier((last_x, last_y, done[-1]))
    total = joined(0, rows) + last_x.astype(f32) + last_y.astype(f32)
    return (total, *done) if done else total


def place_pieces(me_ref, *refs):
    result = refs[PARTS]
    for mask, piece in enumerate(refs[:PARTS]):
        there = jnp.bitwise_xor(me_ref[0], mask)
        if len(result.shape) == 4:
            for index in range(result.shape[0]):
                result[index, there] = piece[index]
        else:
            result[there] = piece[...]


def place_columns(chunks, me_ref, *refs):
    results, held = refs[PARTS:-1], refs[-1]
    for mask, piece in enumerate(refs[:PARTS]):
        held[jnp.bitwise_xor(me_ref[0], mask)] = piece[...]
    offset = 0
    for result in results:
        size = result.shape[1] // (PARTS * chunks)
        for chunk in range(chunks):
            parts = [held[member, :, offset : offset + size] for member in range(PARTS)]
            joined = jnp.concatenate(parts, axis=1).astype(f32)
            result[:, chunk * PARTS * size : (chunk + 1) * PARTS * size] = joined
            offset += size


def pieces_for(blocks, me, axis=0):
    return [
        lax.dynamic_index_in_dim(blocks, me ^ mask, axis, keepdims=False) for mask in range(PARTS)
    ]


def send_pieces(pieces):
    return [
        lax.ppermute(piece, PLANE, [(i, i ^ mask) for i in range(PARTS)]) if mask else piece
        for mask, piece in enumerate(pieces)
    ]


def collect(body, pieces, me, shapes, scratch=()):
    pieces = send_pieces(pieces)
    whole = pl.BlockSpec(memory_space=pltpu.VMEM)
    size = 3 * pieces[0].dtype.itemsize * PARTS * pieces[0].size
    return pl.pallas_call(
        body,
        in_specs=[pl.BlockSpec(memory_space=pltpu.SMEM)] + [whole] * PARTS,
        out_specs=[whole] * len(shapes),
        scratch_shapes=scratch,
        compiler_params=pltpu.CompilerParams(vmem_limit_bytes=24 * 1024 * 1024),
        out_shape=shapes,
        cost_estimate=pl.CostEstimate(flops=0, bytes_accessed=size, transcendentals=0),
    )(me.astype(jnp.int32).reshape(1), *pieces)


def exchange(pieces, me, shape):
    return collect(place_pieces, pieces, me, [jax.ShapeDtypeStruct(shape, pieces[0].dtype)])[0]


def exchange_columns(pieces, me, shapes, chunks=1):
    return collect(
        functools.partial(place_columns, chunks),
        pieces,
        me,
        [jax.ShapeDtypeStruct(shape, f32) for shape in shapes],
        [pltpu.VMEM((PARTS,) + pieces[0].shape, pieces[0].dtype)],
    )


def doubled(values, axis, perm, upper):
    other = lax.ppermute(values, axis, perm)
    return jnp.where(
        upper,
        jnp.concatenate([other, values], axis=0),
        jnp.concatenate([values, other], axis=0),
    )


def halved(values, axis, perm, upper):
    half = values.shape[0] // 2
    low, high = values[:half], values[half:]
    came = lax.ppermute(jnp.where(upper, low, high), axis, perm)
    return jnp.where(upper, high, low) + came


def standardize(values):
    centre = values - jnp.mean(values, axis=1, keepdims=True)
    inverse = lax.rsqrt(jnp.mean(centre * centre, axis=1, keepdims=True) + eps_norm)
    return (centre * inverse, inverse)


def norm_back(grad_out, standard, inverse, gain):
    scaled = grad_out * gain
    inner = jnp.mean(scaled, axis=1, keepdims=True)
    along = jnp.mean(scaled * standard, axis=1, keepdims=True)
    return (
        inverse * (scaled - inner - standard * along),
        jnp.sum(grad_out * standard, axis=0),
        jnp.sum(grad_out, axis=0),
    )


def block_marks(lengths, used_blocks):
    index = jnp.arange(lengths.shape[0], dtype=jnp.int32)
    began = jnp.max(
        jnp.where((lengths[None, :] > 0) & (index[None, :] <= index[:, None]), index[None, :], 0),
        axis=1,
    )
    limit = jnp.sum(jnp.where(index[None, :] == began[:, None], lengths[None, :], 0), axis=1)
    return jnp.stack([began, limit, (index < used_blocks).astype(jnp.int32)], axis=1).reshape(-1)


def valid_rows(marks, row_count):
    marks = marks.reshape(-1, 3)
    row = jnp.arange(row_count, dtype=jnp.int32)
    began, limit, used = (jnp.repeat(marks[:, index], BLOCK) for index in range(3))
    return (row - began * BLOCK < limit) & (used > 0)


def rotary_tables(row_count, heads):
    half_rot = ROT // 2
    freqs = 10000.0 ** (-2.0 * jnp.arange(half_rot, dtype=f32) / ROT)
    angle = jnp.arange(row_count, dtype=f32)[:, None] * freqs[None, :]
    cosine, sine = jnp.cos(angle), jnp.sin(angle)
    zero = jnp.zeros((row_count, HEAD - ROT), f32)
    none = jnp.zeros_like(sine)
    return tuple(
        jnp.tile(jnp.concatenate(parts, axis=1), (1, heads))
        for parts in (
            [cosine, cosine, zero + 1.0],
            [-sine, none, zero],
            [none, sine, zero],
        )
    )


def line_copies(pieces, target, sems):
    copies, offset = [], 0
    for index, piece in enumerate(pieces):
        size = piece.shape[0]
        copies.append(
            pltpu.make_async_copy(piece, target.at[pl.ds(offset, size)], sems.at[index])
        )
        offset += size
    return copies


def begin_lines(step, lines):
    @pl.when(step == 0)
    def _():
        for copies in lines:
            for copy in copies:
                copy.start()


def await_lines(step, lines, groups=1):
    steps = GROUPS // groups
    for index in range(steps):

        @pl.when(step == index)
        def _(index=index):
            for copies in lines:
                last = None if index == steps - 1 else (index + 1) * groups
                for copy in copies[index * groups : last]:
                    copy.wait()


def keep_rows(step, steps, pairs):
    @pl.when(step == steps - 1)
    def _():
        for copy in pairs:
            copy.start()


def await_kept(step, steps, pairs):
    @pl.when(step == steps - 1)
    def _():
        for copy in pairs:
            copy.wait()


def row_marks(marks, group, shape, axis):
    place = lax.broadcasted_iota(jnp.int32, shape, axis)
    key = jnp.zeros(shape, jnp.int32)
    for index in range(shape[axis] // BLOCK):
        began = marks[group, 3 * index]
        limit = marks[group, 3 * index + 1]
        used = marks[group, 3 * index + 2]
        inside = jnp.logical_and(place >= index * BLOCK, place < (index + 1) * BLOCK)
        last = jnp.where(used > 0, began * BLOCK + limit, 0)
        seen = jnp.where(place < last, began, -1 - axis)
        key = jnp.where(inside, seen, key)
    return place, key


def allowed_pairs(marks, group, rows):
    row, row_key = row_marks(marks, group, (rows, 1), 0)
    column, column_key = row_marks(marks, group, (1, rows), 1)
    row = jnp.broadcast_to(row, (rows, rows))
    column = jnp.broadcast_to(column, (rows, rows))
    same = jnp.broadcast_to(row_key, (rows, rows)) == jnp.broadcast_to(column_key, (rows, rows))
    return jnp.logical_or(jnp.logical_and(same, column <= row), row == column)


def placed_table(table, marks, group, rows):
    parts = []
    for index in range(rows // BLOCK):
        start = pl.multiple_of((index - marks[group, 3 * index]) * BLOCK, BLOCK)
        parts.append(table[pl.ds(start, BLOCK), :])
    return jnp.concatenate(parts, axis=0)


def rotate(values, cosine, ahead, behind):
    width = values.shape[1]
    half_rot = ROT // 2
    return (
        values * cosine
        + pltpu.roll(values, width - half_rot, 1) * ahead
        + pltpu.roll(values, half_rot, 1) * behind
    )


def head_masks(shape, heads):
    lane = lax.broadcasted_iota(jnp.int32, shape, 1)
    return [
        jnp.logical_and(lane >= index * HEAD, lane < (index + 1) * HEAD) for index in range(heads)
    ]


def softmax_of(query, key_rows, allowed):
    scores = mat_cols(query, key_rows) * HEAD ** (-0.5)
    scores = jnp.where(allowed, scores, -1e30)
    expo = jnp.exp(scores - jnp.max(scores, axis=1, keepdims=True))
    return expo / jnp.sum(expo, axis=1, keepdims=True)


def attend_forward(first, heads, rows, half, marks_ref, *refs):
    tokens = refs[0:5]
    qkv_weight, out_weight, gain, shift, bias, cos_ref, ahead_ref, behind_ref = refs[5:13]
    refs = refs[13 if first else 16 :]
    normed_ref, qkv_ref, mixed_ref, part_ref, token_rows, line_sems = refs
    step = pl.program_id(0)
    group = half * GROUPS + step
    line = line_copies(tokens, token_rows, line_sems)
    begin_lines(step, [line])
    await_lines(step, [line])
    values = token_rows[pl.ds(pl.multiple_of(step * rows, rows), rows), :].astype(f32)
    centre = values - jnp.mean(values, axis=1, keepdims=True)
    inverse = lax.rsqrt(jnp.mean(centre * centre, axis=1, keepdims=True) + eps_norm)
    normed = (centre * inverse * gain[...] + shift[...]).astype(bf16)
    normed_ref[...] = normed
    width = heads * HEAD
    qkv = mat(normed, qkv_weight[...]) + bias[...]
    tables = [placed_table(ref, marks_ref, group, rows) for ref in (cos_ref, ahead_ref, behind_ref)]
    query = rotate(qkv[:, :width], *tables).astype(bf16)
    key_rows = rotate(qkv[:, width : 2 * width], *tables).astype(bf16)
    value = qkv[:, 2 * width :].astype(bf16)
    qkv_ref[:, :width] = query
    qkv_ref[:, width : 2 * width] = key_rows
    qkv_ref[:, 2 * width :] = value
    allowed = allowed_pairs(marks_ref, group, rows)
    mixed = jnp.zeros((rows, width), f32)
    for mask in head_masks((rows, width), heads):
        probs = softmax_of(jnp.where(mask, query, 0), key_rows, allowed).astype(bf16)
        mixed = jnp.where(mask, mat(probs, value), mixed)
    mixed = mixed.astype(bf16)
    mixed_ref[...] = mixed
    part_ref[...] = mat(mixed, out_weight[...]).astype(bf16)


def feed_both(first, rows, half, *refs):
    normed, grads, weights = refs[0:5], refs[5:10], refs[10]
    refs = refs[11 if first else 15 :]
    normed_ref, grad_ref, hidden_ref, both_ref, back_ref, down_ref = refs[:6]
    normed_rows, grad_rows, gate_weight, up_weight, down_weight = refs[6:11]
    normed_sems, grad_sems, weight_sems, keep_sems = refs[11:]
    step = pl.program_id(0)
    groups = rows * GROUPS // normed_rows.shape[0]
    steps = GROUPS // groups
    place = pl.ds(half * normed_rows.shape[0], normed_rows.shape[0])
    kept = [
        pltpu.make_async_copy(normed_rows, normed_ref.at[place], keep_sems.at[0]),
        pltpu.make_async_copy(grad_rows, grad_ref.at[place], keep_sems.at[1]),
    ]
    size = gate_weight.shape[0] // LINE
    loads = [
        [
            pltpu.make_async_copy(
                weights.at[place, index],
                target.at[pl.ds(place * size, size)],
                weight_sems.at[LINE * index + place],
            )
            for place in range(LINE)
        ]
        for index, target in enumerate((gate_weight, up_weight, down_weight))
    ]
    lines = [
        line_copies(normed, normed_rows, normed_sems),
        line_copies(grads, grad_rows, grad_sems),
    ]

    @pl.when(step == 0)
    def _():
        for copy in loads[0]:
            copy.start()

    begin_lines(step, lines)

    @pl.when(step == 0)
    def _():
        for copy in loads[1] + loads[2]:
            copy.start()
        for copy in loads[0]:
            copy.wait()

    await_lines(step, lines, groups)
    keep_rows(step, steps, kept)
    here = pl.ds(pl.multiple_of(step * rows, rows), rows)
    values = normed_rows[here, :]
    gate = mat(values, gate_weight[...])

    @pl.when(step == 0)
    def _():
        for copy in loads[1] + loads[2]:
            copy.wait()

    upward = mat(values, up_weight[...])
    sigma = jax.nn.sigmoid(gate)
    gated = gate * sigma
    hidden = (gated * upward).astype(bf16)
    hidden_ref[...] = hidden
    grad_low = grad_rows[here, :]
    grad_hidden = mat(grad_low, down_weight[...])
    grad_gate = (grad_hidden * upward * sigma * (1.0 + gate * (1.0 - sigma))).astype(bf16)
    grad_up = (grad_hidden * gated).astype(bf16)
    columns = hidden.shape[1]
    both_ref[:, :columns] = grad_gate
    both_ref[:, columns:] = grad_up
    back_ref[...] = (
        mat_cols(grad_gate, gate_weight[...]) + mat_cols(grad_up, up_weight[...])
    ).astype(bf16)
    down_ref[...] = mat_cols(hidden, down_weight[...]).astype(bf16)
    await_kept(step, steps, kept)


def attend_backward(first, heads, rows, half, marks_ref, *refs):
    branch = refs[0:5]
    saved, qkv_weight, out_weight, cos_ref, ahead_ref, behind_ref = refs[5:11]
    refs = refs[11 if first else 13 :]
    branch_ref, grad_ref, part_ref, branch_rows, line_sems, keep_sems = refs
    step = pl.program_id(0)
    group = half * GROUPS + step
    line = line_copies(branch, branch_rows, line_sems)
    place = pl.ds(half * GROUPS * rows, GROUPS * rows)
    kept = [pltpu.make_async_copy(branch_rows, branch_ref.at[place], keep_sems.at[0])]
    begin_lines(step, [line])
    await_lines(step, [line])
    keep_rows(step, GROUPS, kept)
    values = branch_rows[pl.ds(pl.multiple_of(step * rows, rows), rows), :]
    width = heads * HEAD
    factor = HEAD ** (-0.5)
    grad_mixed = mat_cols(values, out_weight[...]).astype(bf16)
    query = saved[:, :width]
    key_rows = saved[:, width : 2 * width]
    value = saved[:, 2 * width :]
    allowed = allowed_pairs(marks_ref, group, rows)
    zero = jnp.zeros((rows, width), f32)
    grad_query, grad_key, grad_value = zero, zero, zero
    for mask in head_masks((rows, width), heads):
        probs = softmax_of(jnp.where(mask, query, 0), key_rows, allowed)
        grad_probs = mat_cols(jnp.where(mask, grad_mixed, 0), value)
        inner = jnp.sum(grad_probs * probs, axis=1, keepdims=True)
        grad_scores = (probs * (grad_probs - inner)).astype(bf16)
        grad_query = jnp.where(mask, mat(grad_scores, key_rows), grad_query)
        grad_key = jnp.where(mask, mat_rows(grad_scores, query), grad_key)
        grad_value = jnp.where(mask, mat_rows(probs.astype(bf16), grad_mixed), grad_value)
    cosine, ahead, behind = (
        placed_table(ref, marks_ref, group, rows) for ref in (cos_ref, ahead_ref, behind_ref)
    )
    grads = jnp.concatenate(
        [
            rotate(grad_query * factor, cosine, -ahead, -behind),
            rotate(grad_key * factor, cosine, -ahead, -behind),
            grad_value,
        ],
        axis=1,
    ).astype(bf16)
    grad_ref[...] = grads
    part_ref[...] = mat_cols(grads, qkv_weight[...]).astype(bf16)
    await_kept(step, GROUPS, kept)


def run_half(body, scalars, loose, blocked, whole, outputs, scratch, half, rows, prior, steps=GROUPS):
    loose, blocked, whole = list(loose), list(blocked), list(whole)
    kept = list(prior or [])
    out_shape, out_specs = [], []
    for width, shared, by_copy in outputs:
        total = 2 * steps if shared else steps
        offset = half * steps if shared else 0
        out_shape.append(jax.ShapeDtypeStruct((total * rows, width), bf16))
        block = pl.BlockSpec((rows, width), lambda i, *_, offset=offset: (i + offset, 0))
        out_specs.append(ANYWHERE if by_copy else block)
    in_specs = [ANYWHERE] * len(loose)
    for values in blocked:
        in_specs.append(pl.BlockSpec((rows, values.shape[1]), lambda i, *_: (i + half * steps, 0)))
    for values in whole:
        in_specs.append(
            pl.BlockSpec(values.shape, lambda i, *_: (0, 0), pipeline_mode=pl.Buffered(1))
        )
    in_specs += [ANYWHERE] * len(kept)
    before = len(scalars) + len(loose) + len(blocked) + len(whole)
    return pl.pallas_call(
        body,
        grid_spec=pltpu.PrefetchScalarGridSpec(
            num_scalar_prefetch=len(scalars),
            grid=(steps,),
            in_specs=in_specs,
            out_specs=out_specs,
            scratch_shapes=scratch,
        ),
        out_shape=out_shape,
        input_output_aliases={before + index: index for index in range(len(kept))},
        compiler_params=pltpu.CompilerParams(
            dimension_semantics=("arbitrary",), vmem_limit_bytes=VMEM_BYTES
        ),
        cost_estimate=pl.CostEstimate(flops=1, bytes_accessed=1, transcendentals=0),
    )(*scalars, *loose, *blocked, *whole, *kept)


def per_device(
    tokens,
    seq_lengths,
    block_counts,
    qkv_weight,
    qkv_bias,
    out_weight,
    norm1_gain,
    norm1_bias,
    gate_weight,
    up_weight,
    down_weight,
    norm2_gain,
    norm2_bias,
    out_grad,
):
    rows, width = tokens.shape
    share = norm1_gain.shape[0]
    bias_share = qkv_bias.shape[0]
    hidden_share = gate_weight.shape[1] // PARTS
    heads = width // HEAD // PARTS
    head_cols = heads * HEAD
    spread = lax.axis_size("s")
    iz = lax.axis_index("z")
    iy = lax.axis_index("y")
    ix = lax.axis_index("x")
    ic = lax.axis_index("c")
    me = iy * 4 + ix * 2 + ic

    def spread_gather(values, axis):
        return lax.all_gather(values, "s", axis=axis, tiled=True) if spread > 1 else values

    def spread_scatter(values, axis):
        if spread == 1:
            return values
        return lax.psum_scatter(values, "s", scatter_dimension=axis, tiled=True)

    own_marks = block_marks(seq_lengths[0], block_counts[0])
    packed = jnp.concatenate(
        [
            norm1_gain,
            norm1_bias,
            norm2_gain,
            norm2_bias,
            qkv_bias,
            seq_lengths[0].astype(bf16),
            block_counts.astype(bf16),
        ]
    )
    packed = jnp.pad(packed, (0, -packed.shape[0] % 128))[None, :]

    qkv_parts = (
        qkv_weight.reshape(share, 3 * heads, PARTS, HEAD)
        .transpose(2, 0, 1, 3)
        .reshape(PARTS, share, 3 * head_cols)
    )
    qkv_rows = exchange(pieces_for(qkv_parts, me), me, qkv_parts.shape)
    qkv_rows = spread_gather(qkv_rows, 1).reshape(-1, 3 * head_cols)
    qkv_full = gather_line(qkv_rows)
    out_full = gather_line(spread_gather(out_weight, 0))

    plane_pack = doubled(packed, "c", SWAP, ic == 1)
    plane_pack = doubled(plane_pack, "x", SWAP, ix == 1)
    plane_pack = doubled(plane_pack, "y", SWAP, iy == 1)
    all_pack = spread_gather(plane_pack[:, None], 1).reshape(PARTS * spread, -1)
    all_pack = doubled(all_pack, "z", NEAR, iz % 2 == 1)
    all_pack = doubled(all_pack, "z", FAR, iz >= 2)

    def vector(index):
        return all_pack[:, index * share : (index + 1) * share].reshape(1, width).astype(f32)

    gain_one, shift_one, gain_two, shift_two = (vector(index) for index in range(4))
    bias_full = all_pack[:, 4 * share : 4 * share + bias_share].reshape(3 * heads, PARTS, HEAD)
    bias_mine = (
        lax.dynamic_index_in_dim(bias_full, me, 1, keepdims=False)
        .reshape(1, 3 * head_cols)
        .astype(f32)
    )

    relative = [core + 4 * dy + 2 * dx for core in (0, 1) for dy in (0, 1) for dx in (0, 1)]
    marks = plane_pack[:, 4 * share + bias_share : 4 * share + bias_share + 3].astype(jnp.int32)
    marks = jnp.stack(
        [lax.dynamic_index_in_dim(marks, me ^ mask, 0, keepdims=False) for mask in relative]
    )
    marks = jax.vmap(block_marks)(marks[:, :2], marks[:, 2])
    tables = rotary_tables(rows, heads)

    mlp_parts = jnp.stack(
        [
            weight.reshape(share, PARTS, hidden_share).transpose(1, 0, 2)
            for weight in (gate_weight, up_weight, down_weight)
        ]
    )
    mlp_pieces = pieces_for(mlp_parts, me, 1)
    token_lines = gather_plane(tokens, *mlp_pieces)
    mlp_rows = spread_gather(exchange(mlp_pieces, me, mlp_parts.shape), 2)
    mlp_full = gather_line(mlp_rows.reshape(-1, hidden_share))
    mlp_full = mlp_full.reshape(LINE, 3, -1, hidden_share)

    valid = valid_rows(own_marks, rows)[:, None]
    grad_top = jnp.where(valid, out_grad.astype(f32), 0.0)
    grad_lines = gather_plane(after(grad_top.astype(bf16), token_lines[0][3], token_lines[0][4]))

    dma = pltpu.SemaphoreType.DMA
    line_rows = GROUPS * rows

    def attention(half, prior):
        return run_half(
            functools.partial(attend_forward, prior is None, heads, rows, half),
            (after(marks, mlp_rows, *grad_lines[0][:3]) if prior is None else marks,),
            token_lines[half],
            (),
            (qkv_full, out_full, gain_one, shift_one, bias_mine) + tables,
            (
                (width, True, False),
                (3 * head_cols, True, False),
                (head_cols, True, False),
                (width, False, False),
            ),
            [
                pltpu.VMEM((line_rows, width), bf16),
                dma((5,)),
            ],
            half,
            rows,
            prior,
        )

    *shared, out_sent = attention(1, None)
    normed_one, saved, mixed, out_kept = attention(0, shared)
    out_sent = after(out_sent, *grad_lines[0])
    inputs = tokens.astype(f32)
    middle = inputs + scatter_plane(out_kept, out_sent, rows)

    standard_two, inverse_two = standardize(middle)
    normed_lines = gather_plane((standard_two * gain_two + shift_two).astype(bf16))

    def feed(half, prior):
        return run_half(
            functools.partial(feed_both, prior is None, 2 * rows, half),
            (),
            normed_lines[half] + grad_lines[half] + [mlp_full],
            (),
            (),
            ((width, True, True),) * 2
            + ((hidden_share, True, False), (2 * hidden_share, True, False))
            + ((width, False, False),) * 2,
            [pltpu.VMEM((line_rows, width), bf16)] * 2
            + [pltpu.VMEM((width, hidden_share), bf16)] * 3
            + [dma((5,)), dma((5,)), dma((3 * LINE,)), dma((2,))],
            half,
            2 * rows,
            prior,
            GROUPS // 2,
        )

    *shared, back_sent, down_sent = feed(1, None)
    normed_two, grad_low, hidden, grad_both, back_kept, down_kept = feed(0, shared)
    grad_normed_two, down_part, both_part = scatter_plane(
        back_kept,
        back_sent,
        rows,
        lambda *far: mat_rows(after(grad_low, *far), hidden).astype(bf16),
        lambda *near: mat_rows(after(normed_two, *near), grad_both).astype(bf16),
    )
    down_grad = scatter_line(down_part)
    both_grad = scatter_line(both_part)

    grad_middle_norm, gain_two_grad, shift_two_grad = norm_back(
        grad_normed_two, standard_two, inverse_two, gain_two
    )
    grad_middle = grad_top + grad_middle_norm
    branch_lines = gather_plane(grad_middle.astype(bf16))

    def attention_back(half, prior, *earlier):
        return run_half(
            functools.partial(attend_backward, prior is None, heads, rows, half),
            (after(marks, *earlier),),
            branch_lines[half],
            (saved,),
            (qkv_full, out_full) + tables,
            ((width, True, True), (3 * head_cols, True, False), (width, False, False)),
            [
                pltpu.VMEM((line_rows, width), bf16),
                dma((5,)),
                dma((1,)),
            ],
            half,
            rows,
            prior,
        )

    *shared, input_sent = attention_back(1, None, down_grad)
    grad_branch, grad_qkv, input_kept = attention_back(0, shared)
    grad_normed_one, qkv_part, out_part = scatter_plane(
        input_kept,
        input_sent,
        rows,
        lambda *far: mat_rows(after(normed_one, *far), grad_qkv).astype(bf16),
        lambda *near: mat_rows(after(mixed, *near), grad_branch).astype(bf16),
    )
    qkv_grad = scatter_line(qkv_part)
    grad_normed_one = after(grad_normed_one, both_grad)
    down = scatter_plane(down_kept, after(down_sent, input_sent), rows)
    layer_out = jnp.where(valid, middle + down, 0.0).astype(bf16)
    bias_part = jnp.sum(grad_qkv.astype(f32), axis=0).reshape(3 * heads, 1, HEAD)
    bias_grad = jnp.where(
        lax.broadcasted_iota(jnp.int32, (3 * heads, PARTS, HEAD), 1) == me, bias_part, 0.0
    )

    standard_one, inverse_one = standardize(inputs)
    grad_input_norm, gain_one_grad, shift_one_grad = norm_back(
        grad_normed_one, standard_one, inverse_one, gain_one
    )
    tokens_grad = (grad_middle + grad_input_norm).astype(bf16)

    devices = LINE * PARTS * spread
    small = jnp.concatenate(
        [
            part.reshape(devices, -1)
            for part in (gain_one_grad, shift_one_grad, gain_two_grad, shift_two_grad, bias_grad)
        ],
        axis=1,
    )
    small = halved(small, "z", FAR, iz >= 2)
    small = halved(small, "z", NEAR, iz % 2 == 1)
    small = halved(small, "y", SWAP, iy == 1)
    small = halved(small, "x", SWAP, ix == 1)
    small = halved(small, "c", SWAP, ic == 1)
    small = spread_scatter(small, 0)[0]

    def back_blocks(values):
        return spread_scatter(values.reshape(PARTS, -1, values.shape[1]), 1)

    columns = PARTS * hidden_share
    mlp_blocks = (back_blocks(after(down_grad, grad_normed_one)), back_blocks(both_grad))
    mlp_pieces = [
        jnp.concatenate(parts, axis=1) for parts in zip(*(pieces_for(b, me) for b in mlp_blocks))
    ]
    down_share, gate_share, up_share = exchange_columns(mlp_pieces, me, [(share, columns)] * 3)
    qkv_pieces = pieces_for(back_blocks(after(qkv_grad, *mlp_pieces)), me)
    (qkv_share,) = exchange_columns(qkv_pieces, me, [(share, 3 * width)], 3 * heads)
    out_grad_weight = scatter_line(after(out_part, qkv_grad))
    out_share = spread_scatter(out_grad_weight, 0).astype(f32)
    return (
        layer_out,
        tokens_grad,
        qkv_share,
        small[4 * share :],
        out_share,
        small[:share],
        small[share : 2 * share],
        gate_share,
        up_share,
        down_share,
        small[2 * share : 3 * share],
        small[3 * share : 4 * share],
    )


def solution(mesh):
    devices = mesh.devices.reshape(LINE, 2, 2, 2, -1)
    rows, flat = P(AXES, None), P(AXES)
    return jax.shard_map(
        per_device,
        mesh=Mesh(devices, AXES),
        in_specs=(
            rows,
            rows,
            flat,
            rows,
            flat,
            rows,
            flat,
            flat,
            rows,
            rows,
            rows,
            flat,
            flat,
            rows,
        ),
        out_specs=(rows, rows, rows, flat, rows, flat, flat, rows, rows, rows, flat, flat),
        check_vma=False,
    )
```

```python
import functools

import jax
import jax.numpy as jnp
from jax import lax
from jax.experimental import pallas as pl
from jax.experimental.pallas import tpu as pltpu
from jax.sharding import Mesh, PartitionSpec as P

HEAD = 64
ROT = 16
BLOCK = 128
PARTS = 8
LINE = 4
GROUPS = 4

AXES = ("z", "y", "x", "c", "s")
PLANE = ("y", "x", "c")
SWAP = ((0, 1), (1, 0))
NEAR = ((0, 1), (1, 0), (2, 3), (3, 2))
FAR = ((0, 2), (1, 3), (2, 0), (3, 1))

eps_norm = 1e-05
f32 = jnp.float32
bf16 = jnp.bfloat16
VMEM_BYTES = 56 * 1024 * 1024
ANYWHERE = pl.BlockSpec(memory_space=pl.ANY)


def mat_rows(left, right):
    return lax.dot_general(left, right, (((0,), (0,)), ((), ())), preferred_element_type=f32)


def mat_cols(left, right):
    return lax.dot_general(left, right, (((1,), (1,)), ((), ())), preferred_element_type=f32)


def mat(left, right):
    return jnp.dot(left, right, preferred_element_type=f32)


def over_x(values):
    return lax.ppermute(values, "x", SWAP)


def over_y(values):
    return lax.ppermute(values, "y", SWAP)


def over_c(values):
    return lax.ppermute(values, "c", SWAP)


def gather_line(values):
    return lax.all_gather(values, "z", axis=0, tiled=True)


def scatter_line(values):
    return lax.psum_scatter(values.astype(bf16), "z", scatter_dimension=0, tiled=True)


def after(values, *earlier):
    return lax.optimization_barrier((values, *earlier))[0]


def gather_plane(own, *earlier):
    half = own.shape[0] // 2
    from_x = over_x(own)
    from_y = over_y(own)
    low, high = from_y[:half], from_x[half:]
    if earlier:
        low, high, *_ = lax.optimization_barrier((low, high, *earlier))
    line = [own, from_x, from_y, over_x(low), over_y(high)]
    return line, [over_c(part) for part in line]


def scatter_plane(kept, sent, rows, first=None, second=None):
    half = rows // 2
    kept, sent = (parts if isinstance(parts, list) else [parts] for parts in (kept, sent))
    came = [over_c(part) for part in sent]

    def rows_of(parts, low, high):
        size = parts[0].shape[0]
        return parts[low // size][low % size : low % size + high - low].astype(f32)

    def joined(low, high):
        return rows_of(kept, low, high) + rows_of(came, low, high)

    far_low = joined(3 * rows, 3 * rows + half).astype(bf16)
    far_high = joined(3 * rows + half, 4 * rows).astype(bf16)
    done = []
    if first is not None:
        done.append(first(far_low, far_high))
    low, high = over_x(far_low), over_y(far_high)
    if done:
        low, high, _ = lax.optimization_barrier((low, high, done[0]))
    near_x = jnp.concatenate(
        [joined(rows, rows + half), joined(rows + half, 2 * rows) + high.astype(f32)], axis=0
    ).astype(bf16)
    near_y = jnp.concatenate(
        [joined(2 * rows, 2 * rows + half) + low.astype(f32), joined(2 * rows + half, 3 * rows)],
        axis=0,
    ).astype(bf16)
    if second is not None:
        done.append(second(near_x, near_y))
    last_x, last_y = over_x(near_x), over_y(near_y)
    if second is not None:
        last_x, last_y, _ = lax.optimization_barrier((last_x, last_y, done[-1]))
    total = joined(0, rows) + last_x.astype(f32) + last_y.astype(f32)
    return (total, *done) if done else total


def place_pieces(me_ref, *refs):
    result = refs[PARTS]
    for mask, piece in enumerate(refs[:PARTS]):
        there = jnp.bitwise_xor(me_ref[0], mask)
        if len(result.shape) == 4:
            for index in range(result.shape[0]):
                result[index, there] = piece[index]
        else:
            result[there] = piece[...]


def place_columns(chunks, me_ref, *refs):
    results, held = refs[PARTS:-1], refs[-1]
    for mask, piece in enumerate(refs[:PARTS]):
        held[jnp.bitwise_xor(me_ref[0], mask)] = piece[...]
    offset = 0
    for result in results:
        size = result.shape[1] // (PARTS * chunks)
        for chunk in range(chunks):
            parts = [held[member, :, offset : offset + size] for member in range(PARTS)]
            joined = jnp.concatenate(parts, axis=1).astype(f32)
            result[:, chunk * PARTS * size : (chunk + 1) * PARTS * size] = joined
            offset += size


def pieces_for(blocks, me, axis=0):
    return [
        lax.dynamic_index_in_dim(blocks, me ^ mask, axis, keepdims=False) for mask in range(PARTS)
    ]


def send_pieces(pieces):
    return [
        lax.ppermute(piece, PLANE, [(i, i ^ mask) for i in range(PARTS)]) if mask else piece
        for mask, piece in enumerate(pieces)
    ]


def collect(body, pieces, me, shapes, scratch=()):
    pieces = send_pieces(pieces)
    whole = pl.BlockSpec(memory_space=pltpu.VMEM)
    size = 3 * pieces[0].dtype.itemsize * PARTS * pieces[0].size
    return pl.pallas_call(
        body,
        in_specs=[pl.BlockSpec(memory_space=pltpu.SMEM)] + [whole] * PARTS,
        out_specs=[whole] * len(shapes),
        scratch_shapes=scratch,
        compiler_params=pltpu.CompilerParams(vmem_limit_bytes=24 * 1024 * 1024),
        out_shape=shapes,
        cost_estimate=pl.CostEstimate(flops=0, bytes_accessed=size, transcendentals=0),
    )(me.astype(jnp.int32).reshape(1), *pieces)


def exchange(pieces, me, shape):
    return collect(place_pieces, pieces, me, [jax.ShapeDtypeStruct(shape, pieces[0].dtype)])[0]


def exchange_columns(pieces, me, shapes, chunks=1):
    return collect(
        functools.partial(place_columns, chunks),
        pieces,
        me,
        [jax.ShapeDtypeStruct(shape, f32) for shape in shapes],
        [pltpu.VMEM((PARTS,) + pieces[0].shape, pieces[0].dtype)],
    )


def doubled(values, axis, perm, upper):
    other = lax.ppermute(values, axis, perm)
    return jnp.where(
        upper,
        jnp.concatenate([other, values], axis=0),
        jnp.concatenate([values, other], axis=0),
    )


def halved(values, axis, perm, upper):
    half = values.shape[0] // 2
    low, high = values[:half], values[half:]
    came = lax.ppermute(jnp.where(upper, low, high), axis, perm)
    return jnp.where(upper, high, low) + came


def standardize(values):
    centre = values - jnp.mean(values, axis=1, keepdims=True)
    inverse = lax.rsqrt(jnp.mean(centre * centre, axis=1, keepdims=True) + eps_norm)
    return (centre * inverse, inverse)


def norm_back(grad_out, standard, inverse, gain):
    scaled = grad_out * gain
    inner = jnp.mean(scaled, axis=1, keepdims=True)
    along = jnp.mean(scaled * standard, axis=1, keepdims=True)
    return (
        inverse * (scaled - inner - standard * along),
        jnp.sum(grad_out * standard, axis=0),
        jnp.sum(grad_out, axis=0),
    )


def block_marks(lengths, used_blocks):
    index = jnp.arange(lengths.shape[0], dtype=jnp.int32)
    began = jnp.max(
        jnp.where((lengths[None, :] > 0) & (index[None, :] <= index[:, None]), index[None, :], 0),
        axis=1,
    )
    limit = jnp.sum(jnp.where(index[None, :] == began[:, None], lengths[None, :], 0), axis=1)
    return jnp.stack([began, limit, (index < used_blocks).astype(jnp.int32)], axis=1).reshape(-1)


def valid_rows(marks, row_count):
    marks = marks.reshape(-1, 3)
    row = jnp.arange(row_count, dtype=jnp.int32)
    began, limit, used = (jnp.repeat(marks[:, index], BLOCK) for index in range(3))
    return (row - began * BLOCK < limit) & (used > 0)


def rotary_tables(row_count, heads):
    half_rot = ROT // 2
    freqs = 10000.0 ** (-2.0 * jnp.arange(half_rot, dtype=f32) / ROT)
    angle = jnp.arange(row_count, dtype=f32)[:, None] * freqs[None, :]
    cosine, sine = jnp.cos(angle), jnp.sin(angle)
    zero = jnp.zeros((row_count, HEAD - ROT), f32)
    none = jnp.zeros_like(sine)
    return tuple(
        jnp.tile(jnp.concatenate(parts, axis=1), (1, heads))
        for parts in (
            [cosine, cosine, zero + 1.0],
            [-sine, none, zero],
            [none, sine, zero],
        )
    )


def line_copies(pieces, target, sems):
    copies, offset = [], 0
    for index, piece in enumerate(pieces):
        size = piece.shape[0]
        copies.append(
            pltpu.make_async_copy(piece, target.at[pl.ds(offset, size)], sems.at[index])
        )
        offset += size
    return copies


def begin_lines(step, lines):
    @pl.when(step == 0)
    def _():
        for copies in lines:
            for copy in copies:
                copy.start()


def await_lines(step, lines, groups=1):
    steps = GROUPS // groups
    for index in range(steps):

        @pl.when(step == index)
        def _(index=index):
            for copies in lines:
                last = None if index == steps - 1 else (index + 1) * groups
                for copy in copies[index * groups : last]:
                    copy.wait()


def keep_rows(step, steps, pairs):
    @pl.when(step == steps - 1)
    def _():
        for copy in pairs:
            copy.start()


def await_kept(step, steps, pairs):
    @pl.when(step == steps - 1)
    def _():
        for copy in pairs:
            copy.wait()


def row_marks(marks, group, shape, axis):
    place = lax.broadcasted_iota(jnp.int32, shape, axis)
    key = jnp.zeros(shape, jnp.int32)
    for index in range(shape[axis] // BLOCK):
        began = marks[group, 3 * index]
        limit = marks[group, 3 * index + 1]
        used = marks[group, 3 * index + 2]
        inside = jnp.logical_and(place >= index * BLOCK, place < (index + 1) * BLOCK)
        last = jnp.where(used > 0, began * BLOCK + limit, 0)
        seen = jnp.where(place < last, began, -1 - axis)
        key = jnp.where(inside, seen, key)
    return place, key


def allowed_pairs(marks, group, rows):
    row, row_key = row_marks(marks, group, (rows, 1), 0)
    column, column_key = row_marks(marks, group, (1, rows), 1)
    row = jnp.broadcast_to(row, (rows, rows))
    column = jnp.broadcast_to(column, (rows, rows))
    same = jnp.broadcast_to(row_key, (rows, rows)) == jnp.broadcast_to(column_key, (rows, rows))
    return jnp.logical_or(jnp.logical_and(same, column <= row), row == column)


def placed_table(table, marks, group, rows):
    parts = []
    for index in range(rows // BLOCK):
        start = pl.multiple_of((index - marks[group, 3 * index]) * BLOCK, BLOCK)
        parts.append(table[pl.ds(start, BLOCK), :])
    return jnp.concatenate(parts, axis=0)


def rotate(values, cosine, ahead, behind):
    width = values.shape[1]
    half_rot = ROT // 2
    return (
        values * cosine
        + pltpu.roll(values, width - half_rot, 1) * ahead
        + pltpu.roll(values, half_rot, 1) * behind
    )


def head_masks(shape, heads):
    lane = lax.broadcasted_iota(jnp.int32, shape, 1)
    return [
        jnp.logical_and(lane >= index * HEAD, lane < (index + 1) * HEAD) for index in range(heads)
    ]


def softmax_of(query, key_rows, allowed):
    scores = mat_cols(query, key_rows) * HEAD ** (-0.5)
    scores = jnp.where(allowed, scores, -1e30)
    expo = jnp.exp(scores - jnp.max(scores, axis=1, keepdims=True))
    return expo / jnp.sum(expo, axis=1, keepdims=True)


def attend_forward(first, heads, rows, half, marks_ref, *refs):
    tokens = refs[0:5]
    qkv_weight, out_weight, gain, shift, bias, cos_ref, ahead_ref, behind_ref = refs[5:13]
    refs = refs[13 if first else 16 :]
    normed_ref, qkv_ref, mixed_ref, part_ref, token_rows, line_sems = refs
    step = pl.program_id(0)
    group = half * GROUPS + step
    line = line_copies(tokens, token_rows, line_sems)
    begin_lines(step, [line])
    await_lines(step, [line])
    values = token_rows[pl.ds(pl.multiple_of(step * rows, rows), rows), :].astype(f32)
    centre = values - jnp.mean(values, axis=1, keepdims=True)
    inverse = lax.rsqrt(jnp.mean(centre * centre, axis=1, keepdims=True) + eps_norm)
    normed = (centre * inverse * gain[...] + shift[...]).astype(bf16)
    normed_ref[...] = normed
    width = heads * HEAD
    qkv = mat(normed, qkv_weight[...]) + bias[...]
    tables = [placed_table(ref, marks_ref, group, rows) for ref in (cos_ref, ahead_ref, behind_ref)]
    query = rotate(qkv[:, :width], *tables).astype(bf16)
    key_rows = rotate(qkv[:, width : 2 * width], *tables).astype(bf16)
    value = qkv[:, 2 * width :].astype(bf16)
    qkv_ref[:, :width] = query
    qkv_ref[:, width : 2 * width] = key_rows
    qkv_ref[:, 2 * width :] = value
    allowed = allowed_pairs(marks_ref, group, rows)
    mixed = jnp.zeros((rows, width), f32)
    for mask in head_masks((rows, width), heads):
        probs = softmax_of(jnp.where(mask, query, 0), key_rows, allowed).astype(bf16)
        mixed = jnp.where(mask, mat(probs, value), mixed)
    mixed = mixed.astype(bf16)
    mixed_ref[...] = mixed
    part_ref[...] = mat(mixed, out_weight[...]).astype(bf16)


def feed_both(first, rows, half, *refs):
    normed, grads, weights = refs[0:5], refs[5:10], refs[10]
    refs = refs[11 if first else 15 :]
    normed_ref, grad_ref, hidden_ref, both_ref, back_ref, down_ref = refs[:6]
    normed_rows, grad_rows, gate_weight, up_weight, down_weight = refs[6:11]
    normed_sems, grad_sems, weight_sems, keep_sems = refs[11:]
    step = pl.program_id(0)
    groups = rows * GROUPS // normed_rows.shape[0]
    steps = GROUPS // groups
    place = pl.ds(half * normed_rows.shape[0], normed_rows.shape[0])
    kept = [
        pltpu.make_async_copy(normed_rows, normed_ref.at[place], keep_sems.at[0]),
        pltpu.make_async_copy(grad_rows, grad_ref.at[place], keep_sems.at[1]),
    ]
    size = gate_weight.shape[0] // LINE
    loads = [
        [
            pltpu.make_async_copy(
                weights.at[place, index],
                target.at[pl.ds(place * size, size)],
                weight_sems.at[LINE * index + place],
            )
            for place in range(LINE)
        ]
        for index, target in enumerate((gate_weight, up_weight, down_weight))
    ]
    lines = [
        line_copies(normed, normed_rows, normed_sems),
        line_copies(grads, grad_rows, grad_sems),
    ]

    @pl.when(step == 0)
    def _():
        for copy in loads[0]:
            copy.start()

    begin_lines(step, lines)

    @pl.when(step == 0)
    def _():
        for copy in loads[1] + loads[2]:
            copy.start()
        for copy in loads[0]:
            copy.wait()

    await_lines(step, lines, groups)
    keep_rows(step, steps, kept)
    here = pl.ds(pl.multiple_of(step * rows, rows), rows)
    values = normed_rows[here, :]
    gate = mat(values, gate_weight[...])

    @pl.when(step == 0)
    def _():
        for copy in loads[1] + loads[2]:
            copy.wait()

    upward = mat(values, up_weight[...])
    sigma = jax.nn.sigmoid(gate)
    gated = gate * sigma
    hidden = (gated * upward).astype(bf16)
    hidden_ref[...] = hidden
    grad_low = grad_rows[here, :]
    grad_hidden = mat(grad_low, down_weight[...])
    grad_gate = (grad_hidden * upward * sigma * (1.0 + gate * (1.0 - sigma))).astype(bf16)
    grad_up = (grad_hidden * gated).astype(bf16)
    columns = hidden.shape[1]
    both_ref[:, :columns] = grad_gate
    both_ref[:, columns:] = grad_up
    back_ref[...] = (
        mat_cols(grad_gate, gate_weight[...]) + mat_cols(grad_up, up_weight[...])
    ).astype(bf16)
    down_ref[...] = mat_cols(hidden, down_weight[...]).astype(bf16)
    await_kept(step, steps, kept)


def attend_backward(first, heads, rows, half, marks_ref, *refs):
    branch = refs[0:5]
    saved, qkv_weight, out_weight, cos_ref, ahead_ref, behind_ref = refs[5:11]
    refs = refs[11 if first else 13 :]
    branch_ref, grad_ref, early_ref, late_ref, branch_rows, line_sems, keep_sems = refs
    step = pl.program_id(0)
    group = half * GROUPS + step
    line = line_copies(branch, branch_rows, line_sems)
    place = pl.ds(half * GROUPS * rows, GROUPS * rows)
    kept = [pltpu.make_async_copy(branch_rows, branch_ref.at[place], keep_sems.at[0])]
    begin_lines(step, [line])
    await_lines(step, [line])
    keep_rows(step, GROUPS, kept)
    values = branch_rows[pl.ds(pl.multiple_of(step * rows, rows), rows), :]
    width = heads * HEAD
    factor = HEAD ** (-0.5)
    grad_mixed = mat_cols(values, out_weight[...]).astype(bf16)
    query = saved[:, :width]
    key_rows = saved[:, width : 2 * width]
    value = saved[:, 2 * width :]
    allowed = allowed_pairs(marks_ref, group, rows)
    zero = jnp.zeros((rows, width), f32)
    grad_query, grad_key, grad_value = zero, zero, zero
    for mask in head_masks((rows, width), heads):
        probs = softmax_of(jnp.where(mask, query, 0), key_rows, allowed)
        grad_probs = mat_cols(jnp.where(mask, grad_mixed, 0), value)
        inner = jnp.sum(grad_probs * probs, axis=1, keepdims=True)
        grad_scores = (probs * (grad_probs - inner)).astype(bf16)
        grad_query = jnp.where(mask, mat(grad_scores, key_rows), grad_query)
        grad_key = jnp.where(mask, mat_rows(grad_scores, query), grad_key)
        grad_value = jnp.where(mask, mat_rows(probs.astype(bf16), grad_mixed), grad_value)
    cosine, ahead, behind = (
        placed_table(ref, marks_ref, group, rows) for ref in (cos_ref, ahead_ref, behind_ref)
    )
    grads = jnp.concatenate(
        [
            rotate(grad_query * factor, cosine, -ahead, -behind),
            rotate(grad_key * factor, cosine, -ahead, -behind),
            grad_value,
        ],
        axis=1,
    ).astype(bf16)
    grad_ref[...] = grads
    part = mat_cols(grads, qkv_weight[...]).astype(bf16)

    @pl.when(step < GROUPS // 2)
    def _():
        early_ref[...] = part

    @pl.when(step >= GROUPS // 2)
    def _():
        late_ref[...] = part

    await_kept(step, GROUPS, kept)


def run_half(body, scalars, loose, blocked, whole, outputs, scratch, half, rows, prior, flops=1, steps=GROUPS, parted=0):
    loose, blocked, whole = list(loose), list(blocked), list(whole)
    kept = list(prior or [])
    out_shape, out_specs = [], []
    for width, shared, by_copy in outputs:
        total = 2 * steps if shared else steps
        offset = half * steps if shared else 0
        out_shape.append(jax.ShapeDtypeStruct((total * rows, width), bf16))
        block = pl.BlockSpec((rows, width), lambda i, *_, offset=offset: (i + offset, 0))
        out_specs.append(ANYWHERE if by_copy else block)
    if parted:
        out_shape += [jax.ShapeDtypeStruct((steps // 2 * rows, parted), bf16)] * 2
        out_specs += [
            pl.BlockSpec((rows, parted), lambda i, *_: (jnp.minimum(i, steps // 2 - 1), 0)),
            pl.BlockSpec((rows, parted), lambda i, *_: (jnp.maximum(i - steps // 2, 0), 0)),
        ]
    in_specs = [ANYWHERE] * len(loose)
    for values in blocked:
        in_specs.append(pl.BlockSpec((rows, values.shape[1]), lambda i, *_: (i + half * steps, 0)))
    for values in whole:
        in_specs.append(
            pl.BlockSpec(values.shape, lambda i, *_: (0, 0), pipeline_mode=pl.Buffered(1))
        )
    in_specs += [ANYWHERE] * len(kept)
    before = len(scalars) + len(loose) + len(blocked) + len(whole)
    return pl.pallas_call(
        body,
        grid_spec=pltpu.PrefetchScalarGridSpec(
            num_scalar_prefetch=len(scalars),
            grid=(steps,),
            in_specs=in_specs,
            out_specs=out_specs,
            scratch_shapes=scratch,
        ),
        out_shape=out_shape,
        input_output_aliases={before + index: index for index in range(len(kept))},
        compiler_params=pltpu.CompilerParams(
            dimension_semantics=("arbitrary",), vmem_limit_bytes=VMEM_BYTES
        ),
        cost_estimate=pl.CostEstimate(flops=flops, bytes_accessed=1, transcendentals=0),
    )(*scalars, *loose, *blocked, *whole, *kept)


def per_device(
    tokens,
    seq_lengths,
    block_counts,
    qkv_weight,
    qkv_bias,
    out_weight,
    norm1_gain,
    norm1_bias,
    gate_weight,
    up_weight,
    down_weight,
    norm2_gain,
    norm2_bias,
    out_grad,
):
    rows, width = tokens.shape
    share = norm1_gain.shape[0]
    bias_share = qkv_bias.shape[0]
    hidden_share = gate_weight.shape[1] // PARTS
    heads = width // HEAD // PARTS
    head_cols = heads * HEAD
    spread = lax.axis_size("s")
    iz = lax.axis_index("z")
    iy = lax.axis_index("y")
    ix = lax.axis_index("x")
    ic = lax.axis_index("c")
    me = iy * 4 + ix * 2 + ic

    def spread_gather(values, axis):
        return lax.all_gather(values, "s", axis=axis, tiled=True) if spread > 1 else values

    def spread_scatter(values, axis):
        if spread == 1:
            return values
        return lax.psum_scatter(values, "s", scatter_dimension=axis, tiled=True)

    own_marks = block_marks(seq_lengths[0], block_counts[0])
    packed = jnp.concatenate(
        [
            norm1_gain,
            norm1_bias,
            norm2_gain,
            norm2_bias,
            qkv_bias,
            seq_lengths[0].astype(bf16),
            block_counts.astype(bf16),
        ]
    )
    packed = jnp.pad(packed, (0, -packed.shape[0] % 128))[None, :]

    qkv_parts = (
        qkv_weight.reshape(share, 3 * heads, PARTS, HEAD)
        .transpose(2, 0, 1, 3)
        .reshape(PARTS, share, 3 * head_cols)
    )
    qkv_rows = exchange(pieces_for(qkv_parts, me), me, qkv_parts.shape)
    qkv_rows = spread_gather(qkv_rows, 1).reshape(-1, 3 * head_cols)
    qkv_full = gather_line(qkv_rows)
    out_full = gather_line(spread_gather(out_weight, 0))

    plane_pack = doubled(packed, "c", SWAP, ic == 1)
    plane_pack = doubled(plane_pack, "x", SWAP, ix == 1)
    plane_pack = doubled(plane_pack, "y", SWAP, iy == 1)
    all_pack = spread_gather(plane_pack[:, None], 1).reshape(PARTS * spread, -1)
    all_pack = doubled(all_pack, "z", NEAR, iz % 2 == 1)
    all_pack = doubled(all_pack, "z", FAR, iz >= 2)

    def vector(index):
        return all_pack[:, index * share : (index + 1) * share].reshape(1, width).astype(f32)

    gain_one, shift_one, gain_two, shift_two = (vector(index) for index in range(4))
    bias_full = all_pack[:, 4 * share : 4 * share + bias_share].reshape(3 * heads, PARTS, HEAD)
    bias_mine = (
        lax.dynamic_index_in_dim(bias_full, me, 1, keepdims=False)
        .reshape(1, 3 * head_cols)
        .astype(f32)
    )

    relative = [core + 4 * dy + 2 * dx for core in (0, 1) for dy in (0, 1) for dx in (0, 1)]
    marks = plane_pack[:, 4 * share + bias_share : 4 * share + bias_share + 3].astype(jnp.int32)
    marks = jnp.stack(
        [lax.dynamic_index_in_dim(marks, me ^ mask, 0, keepdims=False) for mask in relative]
    )
    marks = jax.vmap(block_marks)(marks[:, :2], marks[:, 2])
    tables = rotary_tables(rows, heads)

    mlp_parts = jnp.stack(
        [
            weight.reshape(share, PARTS, hidden_share).transpose(1, 0, 2)
            for weight in (gate_weight, up_weight, down_weight)
        ]
    )
    mlp_pieces = pieces_for(mlp_parts, me, 1)
    token_lines = gather_plane(tokens, *mlp_pieces)
    mlp_rows = spread_gather(exchange(mlp_pieces, me, mlp_parts.shape), 2)
    mlp_full = gather_line(mlp_rows.reshape(-1, hidden_share))
    mlp_full = mlp_full.reshape(LINE, 3, -1, hidden_share)

    valid = valid_rows(own_marks, rows)[:, None]
    grad_top = jnp.where(valid, out_grad.astype(f32), 0.0)
    grad_lines = gather_plane(after(grad_top.astype(bf16), token_lines[0][3], token_lines[0][4]))

    dma = pltpu.SemaphoreType.DMA
    line_rows = GROUPS * rows

    def attention(half, prior):
        return run_half(
            functools.partial(attend_forward, prior is None, heads, rows, half),
            (after(marks, mlp_rows, *grad_lines[0][:3]) if prior is None else marks,),
            token_lines[half],
            (),
            (qkv_full, out_full, gain_one, shift_one, bias_mine) + tables,
            (
                (width, True, False),
                (3 * head_cols, True, False),
                (head_cols, True, False),
                (width, False, False),
            ),
            [
                pltpu.VMEM((line_rows, width), bf16),
                dma((5,)),
            ],
            half,
            rows,
            prior,
        )

    *shared, out_sent = attention(1, None)
    normed_one, saved, mixed, out_kept = attention(0, shared)
    out_sent = after(out_sent, *grad_lines[0])
    inputs = tokens.astype(f32)
    middle = inputs + scatter_plane(out_kept, out_sent, rows)

    standard_two, inverse_two = standardize(middle)
    normed_lines = gather_plane((standard_two * gain_two + shift_two).astype(bf16))

    def feed(half, prior):
        return run_half(
            functools.partial(feed_both, prior is None, 2 * rows, half),
            (),
            normed_lines[half] + grad_lines[half] + [mlp_full],
            (),
            (),
            ((width, True, True),) * 2
            + ((hidden_share, True, False), (2 * hidden_share, True, False))
            + ((width, False, False),) * 2,
            [pltpu.VMEM((line_rows, width), bf16)] * 2
            + [pltpu.VMEM((width, hidden_share), bf16)] * 3
            + [dma((5,)), dma((5,)), dma((3 * LINE,)), dma((2,))],
            half,
            2 * rows,
            prior,
            1,
            GROUPS // 2,
        )

    *shared, back_sent, down_sent = feed(1, None)
    normed_two, grad_low, hidden, grad_both, back_kept, down_kept = feed(0, shared)
    grad_normed_two, down_part, both_part = scatter_plane(
        back_kept,
        back_sent,
        rows,
        lambda *far: mat_rows(after(grad_low, *far), hidden).astype(bf16),
        lambda *near: mat_rows(after(normed_two, *near), grad_both).astype(bf16),
    )
    down_grad = scatter_line(down_part)
    both_grad = scatter_line(both_part)

    grad_middle_norm, gain_two_grad, shift_two_grad = norm_back(
        grad_normed_two, standard_two, inverse_two, gain_two
    )
    grad_middle = grad_top + grad_middle_norm
    branch_lines = gather_plane(grad_middle.astype(bf16))

    def attention_back(half, prior, *earlier):
        return run_half(
            functools.partial(attend_backward, prior is None, heads, rows, half),
            (after(marks, *earlier),),
            branch_lines[half],
            (saved,),
            (qkv_full, out_full) + tables,
            ((width, True, True), (3 * head_cols, True, False)),
            [
                pltpu.VMEM((line_rows, width), bf16),
                dma((5,)),
                dma((1,)),
            ],
            half,
            rows,
            prior,
            13 * line_rows * width * 4 * head_cols,
            GROUPS,
            width,
        )

    backs = []

    def back_first(*far):
        backs.append(attention_back(1, None, down_grad, *far))
        return backs[0][3]

    def back_second(*near):
        backs.append(attention_back(0, backs[0][:2], *near))
        return backs[1][3]

    down, _, _ = scatter_plane(
        down_kept, after(down_sent, grad_middle), rows, back_first, back_second
    )
    layer_out = jnp.where(valid, middle + down, 0.0).astype(bf16)
    grad_branch, grad_qkv, *input_kept = backs[1]
    input_sent = backs[0][2:]
    grad_normed_one, qkv_part, out_part = scatter_plane(
        list(input_kept),
        list(input_sent),
        rows,
        lambda *far: mat_rows(after(normed_one, *far, down), grad_qkv).astype(bf16),
        lambda *near: mat_rows(after(mixed, *near, both_grad), grad_branch).astype(bf16),
    )
    qkv_grad = scatter_line(qkv_part)
    bias_part = jnp.sum(grad_qkv.astype(f32), axis=0).reshape(3 * heads, 1, HEAD)
    bias_grad = jnp.where(
        lax.broadcasted_iota(jnp.int32, (3 * heads, PARTS, HEAD), 1) == me, bias_part, 0.0
    )

    standard_one, inverse_one = standardize(inputs)
    grad_input_norm, gain_one_grad, shift_one_grad = norm_back(
        grad_normed_one, standard_one, inverse_one, gain_one
    )
    tokens_grad = (grad_middle + grad_input_norm).astype(bf16)

    devices = LINE * PARTS * spread
    small = jnp.concatenate(
        [
            part.reshape(devices, -1)
            for part in (gain_one_grad, shift_one_grad, gain_two_grad, shift_two_grad, bias_grad)
        ],
        axis=1,
    )
    small = halved(small, "z", FAR, iz >= 2)
    small = halved(small, "z", NEAR, iz % 2 == 1)
    small = halved(small, "y", SWAP, iy == 1)
    small = halved(small, "x", SWAP, ix == 1)
    small = halved(small, "c", SWAP, ic == 1)
    small = spread_scatter(small, 0)[0]

    def back_blocks(values):
        return spread_scatter(values.reshape(PARTS, -1, values.shape[1]), 1)

    columns = PARTS * hidden_share
    mlp_blocks = (back_blocks(after(down_grad, grad_normed_one)), back_blocks(both_grad))
    mlp_pieces = [
        jnp.concatenate(parts, axis=1) for parts in zip(*(pieces_for(b, me) for b in mlp_blocks))
    ]
    down_share, gate_share, up_share = exchange_columns(mlp_pieces, me, [(share, columns)] * 3)
    qkv_pieces = pieces_for(back_blocks(after(qkv_grad, *mlp_pieces)), me)
    (qkv_share,) = exchange_columns(qkv_pieces, me, [(share, 3 * width)], 3 * heads)
    out_grad_weight = scatter_line(after(out_part, qkv_grad))
    out_share = spread_scatter(out_grad_weight, 0).astype(f32)
    return (
        layer_out,
        tokens_grad,
        qkv_share,
        small[4 * share :],
        out_share,
        small[:share],
        small[share : 2 * share],
        gate_share,
        up_share,
        down_share,
        small[2 * share : 3 * share],
        small[3 * share : 4 * share],
    )


def solution(mesh):
    devices = mesh.devices.reshape(LINE, 2, 2, 2, -1)
    rows, flat = P(AXES, None), P(AXES)
    return jax.shard_map(
        per_device,
        mesh=Mesh(devices, AXES),
        in_specs=(
            rows,
            rows,
            flat,
            rows,
            flat,
            rows,
            flat,
            flat,
            rows,
            rows,
            rows,
            flat,
            flat,
            rows,
        ),
        out_specs=(rows, rows, rows, flat, rows, flat, flat, rows, rows, rows, flat, flat),
        check_vma=False,
    )
```

```python
import functools

import jax
import jax.numpy as jnp
from jax import lax
from jax.experimental import pallas as pl
from jax.experimental.pallas import tpu as pltpu
from jax.sharding import Mesh, PartitionSpec as P

HEAD = 64
ROT = 16
BLOCK = 128
PARTS = 8
CHIPS = 4
LINE = 4
GROUPS = 4

AXES = ("z", "y", "x", "c", "s")
PLANE = ("y", "x", "c")
SWAP = ((0, 1), (1, 0))
NEAR = ((0, 1), (1, 0), (2, 3), (3, 2))
FAR = ((0, 2), (1, 3), (2, 0), (3, 1))

eps_norm = 1e-05
f32 = jnp.float32
bf16 = jnp.bfloat16
VMEM_BYTES = 56 * 1024 * 1024
ANYWHERE = pl.BlockSpec(memory_space=pl.ANY)


def mat_rows(left, right):
    return lax.dot_general(left, right, (((0,), (0,)), ((), ())), preferred_element_type=f32)


def mat_cols(left, right):
    return lax.dot_general(left, right, (((1,), (1,)), ((), ())), preferred_element_type=f32)


def mat(left, right):
    return jnp.dot(left, right, preferred_element_type=f32)


def over_x(values):
    return lax.ppermute(values, "x", SWAP)


def over_y(values):
    return lax.ppermute(values, "y", SWAP)


def over_c(values):
    return lax.ppermute(values, "c", SWAP)


def gather_line(values):
    return lax.all_gather(values, "z", axis=0, tiled=True)


def scatter_line(values):
    return lax.psum_scatter(values.astype(bf16), "z", scatter_dimension=0, tiled=True)


def after(values, *earlier):
    return lax.optimization_barrier((values, *earlier))[0]


def gather_plane(values, *earlier):
    half = values.shape[0] // 2
    low, high = values[:half], values[half:]
    y_low, x_high = over_y(low), over_x(high)
    x_low, y_high = over_x(low), over_y(high)
    to_x, to_y = y_low, x_high
    if earlier:
        to_x, to_y, *_ = lax.optimization_barrier((to_x, to_y, *earlier))
    line = [low, high, x_low, x_high, y_low, y_high, over_x(to_x), over_y(to_y)]
    return line, [over_c(part) for part in line]


def gather_whole(values, *earlier):
    half = values.shape[0] // 2
    from_x, from_y = over_x(values), over_y(values)
    to_x, to_y = from_y[:half], from_x[half:]
    if earlier:
        to_x, to_y, *_ = lax.optimization_barrier((to_x, to_y, *earlier))
    line = [values, from_x, from_y, over_x(to_x), over_y(to_y)]
    return line, [over_c(part) for part in line]


def scatter_plane(kept, sent, rows, first=None, second=None, also=()):
    half = rows // 2
    kept, sent = (parts if isinstance(parts, list) else [parts] for parts in (kept, sent))
    came = [over_c(part) for part in sent]

    def rows_of(parts, low, high):
        size = parts[0].shape[0]
        return parts[low // size][low % size : low % size + high - low].astype(f32)

    def joined(low, high):
        return rows_of(kept, low, high) + rows_of(came, low, high)

    far_low = joined(3 * rows, 3 * rows + half).astype(bf16)
    far_high = joined(3 * rows + half, 4 * rows).astype(bf16)
    done = []
    if first is not None:
        done.append(first(far_low, far_high))
    low, high = over_x(far_low), over_y(far_high)
    if done:
        low, high, *_ = lax.optimization_barrier((low, high, done[0], *also))
    near_x = jnp.concatenate(
        [joined(rows, rows + half), joined(rows + half, 2 * rows) + high.astype(f32)], axis=0
    ).astype(bf16)
    near_y = jnp.concatenate(
        [joined(2 * rows, 2 * rows + half) + low.astype(f32), joined(2 * rows + half, 3 * rows)],
        axis=0,
    ).astype(bf16)
    if second is not None:
        done.append(second(near_x, near_y))
    last_x, last_y = over_x(near_x), over_y(near_y)
    if second is not None:
        last_x, last_y, _ = lax.optimization_barrier((last_x, last_y, done[-1]))
    total = joined(0, rows) + last_x.astype(f32) + last_y.astype(f32)
    return (total, *done) if done else total


def members(refs):
    return [(2 * chip + core, refs[chip].at[core]) for chip in range(CHIPS) for core in (0, 1)]


def place_pieces(me_ref, *refs):
    result = refs[CHIPS]
    for mask, piece in members(refs):
        there = jnp.bitwise_xor(me_ref[0], mask)
        if len(result.shape) == 4:
            for index in range(result.shape[0]):
                result[index, there] = piece[index]
        else:
            result[there] = piece[...]


def place_columns(chunks, me_ref, *refs):
    results, held = refs[CHIPS:-1], refs[-1]
    for mask, piece in members(refs):
        held[jnp.bitwise_xor(me_ref[0], mask)] = piece[...]
    offset = 0
    for result in results:
        size = result.shape[1] // (PARTS * chunks)
        for chunk in range(chunks):
            parts = [held[member, :, offset : offset + size] for member in range(PARTS)]
            joined = jnp.concatenate(parts, axis=1).astype(f32)
            result[:, chunk * PARTS * size : (chunk + 1) * PARTS * size] = joined
            offset += size


def send_pieces(block, me):
    chip, core = me // 2, me % 2
    to_other = jnp.stack([block((chip ^ away) * 2 + 1 - core) for away in range(CHIPS)])
    came = over_c(to_other)
    pairs = []
    for away in range(CHIPS):
        pair = jnp.stack([block((chip ^ away) * 2 + core), came[away]])
        if away:
            pair = lax.ppermute(pair, ("y", "x"), [(i, i ^ away) for i in range(CHIPS)])
        pairs.append(pair)
    return pairs


def block_of(*arrays, axis=0):
    def block(index):
        parts = [lax.dynamic_index_in_dim(a, index, axis, keepdims=False) for a in arrays]
        return parts[0] if len(parts) == 1 else jnp.concatenate(parts, axis=-1)

    return block


def collect(body, pairs, me, shapes, scratch=()):
    whole = pl.BlockSpec(memory_space=pltpu.VMEM)
    size = 3 * pairs[0].dtype.itemsize * CHIPS * pairs[0].size
    return pl.pallas_call(
        body,
        in_specs=[pl.BlockSpec(memory_space=pltpu.SMEM)] + [whole] * CHIPS,
        out_specs=[whole] * len(shapes),
        scratch_shapes=scratch,
        compiler_params=pltpu.CompilerParams(vmem_limit_bytes=24 * 1024 * 1024),
        out_shape=shapes,
        cost_estimate=pl.CostEstimate(flops=0, bytes_accessed=size, transcendentals=0),
    )(me.astype(jnp.int32).reshape(1), *pairs)


def exchange(pairs, me, shape):
    return collect(place_pieces, pairs, me, [jax.ShapeDtypeStruct(shape, pairs[0].dtype)])[0]


def exchange_columns(pairs, me, shapes, chunks=1):
    return collect(
        functools.partial(place_columns, chunks),
        pairs,
        me,
        [jax.ShapeDtypeStruct(shape, f32) for shape in shapes],
        [pltpu.VMEM((PARTS,) + pairs[0].shape[1:], pairs[0].dtype)],
    )


def doubled(values, axis, perm, upper):
    other = lax.ppermute(values, axis, perm)
    return jnp.where(
        upper,
        jnp.concatenate([other, values], axis=0),
        jnp.concatenate([values, other], axis=0),
    )


def halved(values, axis, perm, upper):
    half = values.shape[0] // 2
    low, high = values[:half], values[half:]
    came = lax.ppermute(jnp.where(upper, low, high), axis, perm)
    return jnp.where(upper, high, low) + came


def standardize(values):
    centre = values - jnp.mean(values, axis=1, keepdims=True)
    inverse = lax.rsqrt(jnp.mean(centre * centre, axis=1, keepdims=True) + eps_norm)
    return (centre * inverse, inverse)


def norm_back(grad_out, standard, inverse, gain):
    scaled = grad_out * gain
    inner = jnp.mean(scaled, axis=1, keepdims=True)
    along = jnp.mean(scaled * standard, axis=1, keepdims=True)
    return (
        inverse * (scaled - inner - standard * along),
        jnp.sum(grad_out * standard, axis=0),
        jnp.sum(grad_out, axis=0),
    )


def block_marks(lengths, used_blocks):
    index = jnp.arange(lengths.shape[0], dtype=jnp.int32)
    began = jnp.max(
        jnp.where((lengths[None, :] > 0) & (index[None, :] <= index[:, None]), index[None, :], 0),
        axis=1,
    )
    limit = jnp.sum(jnp.where(index[None, :] == began[:, None], lengths[None, :], 0), axis=1)
    return jnp.stack([began, limit, (index < used_blocks).astype(jnp.int32)], axis=1).reshape(-1)


def valid_rows(marks, row_count):
    marks = marks.reshape(-1, 3)
    row = jnp.arange(row_count, dtype=jnp.int32)
    began, limit, used = (jnp.repeat(marks[:, index], BLOCK) for index in range(3))
    return (row - began * BLOCK < limit) & (used > 0)


def rotary_tables(row_count, heads):
    half_rot = ROT // 2
    freqs = 10000.0 ** (-2.0 * jnp.arange(half_rot, dtype=f32) / ROT)
    angle = jnp.arange(row_count, dtype=f32)[:, None] * freqs[None, :]
    cosine, sine = jnp.cos(angle), jnp.sin(angle)
    zero = jnp.zeros((row_count, HEAD - ROT), f32)
    none = jnp.zeros_like(sine)
    return tuple(
        jnp.tile(jnp.concatenate(parts, axis=1), (1, heads))
        for parts in (
            [cosine, cosine, zero + 1.0],
            [-sine, none, zero],
            [none, sine, zero],
        )
    )


def line_copies(pieces, target, sems):
    copies, offset = [], 0
    for index, piece in enumerate(pieces):
        size = piece.shape[0]
        copy = pltpu.make_async_copy(piece, target.at[pl.ds(offset, size)], sems.at[index])
        copies.append((copy, offset))
        offset += size
    return copies


def begin_lines(step, lines):
    @pl.when(step == 0)
    def _():
        for copies in lines:
            for copy, _ in copies:
                copy.start()


def await_lines(step, steps, rows, lines):
    for index in range(steps):

        @pl.when(step == index)
        def _(index=index):
            for copies in lines:
                for copy, offset in copies:
                    if offset // rows == index:
                        copy.wait()


def keep_rows(step, steps, pairs):
    @pl.when(step == steps - 1)
    def _():
        for copy in pairs:
            copy.start()


def await_kept(step, steps, pairs):
    @pl.when(step == steps - 1)
    def _():
        for copy in pairs:
            copy.wait()


def row_marks(marks, group, shape, axis):
    place = lax.broadcasted_iota(jnp.int32, shape, axis)
    key = jnp.zeros(shape, jnp.int32)
    for index in range(shape[axis] // BLOCK):
        began = marks[group, 3 * index]
        limit = marks[group, 3 * index + 1]
        used = marks[group, 3 * index + 2]
        inside = jnp.logical_and(place >= index * BLOCK, place < (index + 1) * BLOCK)
        last = jnp.where(used > 0, began * BLOCK + limit, 0)
        seen = jnp.where(place < last, began, -1 - axis)
        key = jnp.where(inside, seen, key)
    return place, key


def allowed_pairs(marks, group, rows):
    row, row_key = row_marks(marks, group, (rows, 1), 0)
    column, column_key = row_marks(marks, group, (1, rows), 1)
    row = jnp.broadcast_to(row, (rows, rows))
    column = jnp.broadcast_to(column, (rows, rows))
    same = jnp.broadcast_to(row_key, (rows, rows)) == jnp.broadcast_to(column_key, (rows, rows))
    return jnp.logical_or(jnp.logical_and(same, column <= row), row == column)


def placed_table(table, marks, group, rows):
    parts = []
    for index in range(rows // BLOCK):
        start = pl.multiple_of((index - marks[group, 3 * index]) * BLOCK, BLOCK)
        parts.append(table[pl.ds(start, BLOCK), :])
    return jnp.concatenate(parts, axis=0)


def rotate(values, cosine, ahead, behind):
    width = values.shape[1]
    half_rot = ROT // 2
    return (
        values * cosine
        + pltpu.roll(values, width - half_rot, 1) * ahead
        + pltpu.roll(values, half_rot, 1) * behind
    )


def head_masks(shape, heads):
    lane = lax.broadcasted_iota(jnp.int32, shape, 1)
    return [
        jnp.logical_and(lane >= index * HEAD, lane < (index + 1) * HEAD) for index in range(heads)
    ]


def stacked(values, masks):
    return jnp.concatenate([jnp.where(mask, values, 0) for mask in masks], axis=0)


def of_heads(values, masks):
    rows = values.shape[0] // len(masks)
    result = jnp.zeros((rows, values.shape[1]), values.dtype)
    for index, mask in enumerate(masks):
        result = jnp.where(mask, values[index * rows : (index + 1) * rows], result)
    return result


def softmax_of(query_stack, key_rows, allowed):
    rows = key_rows.shape[0]
    scores = mat_cols(query_stack, key_rows).reshape(-1, rows, rows)
    scores = jnp.where(allowed[None], scores, -1e30)
    expo = jnp.exp(scores - jnp.max(scores, axis=2, keepdims=True))
    return (expo * (1.0 / jnp.sum(expo, axis=2, keepdims=True))).reshape(-1, rows)


def attend_forward(count, first, heads, rows, half, marks_ref, *refs):
    tokens, refs = refs[:count], refs[count:]
    qkv_weight, out_weight, gain, shift, bias, cos_ref, ahead_ref, behind_ref = refs[:8]
    refs = refs[8 if first else 11 :]
    normed_ref, qkv_ref, mixed_ref, part_ref, token_rows, line_sems = refs
    step = pl.program_id(0)
    group = half * GROUPS + step
    line = line_copies(tokens, token_rows, line_sems)
    begin_lines(step, [line])
    await_lines(step, GROUPS, rows, [line])
    values = token_rows[pl.ds(pl.multiple_of(step * rows, rows), rows), :].astype(f32)
    centre = values - jnp.mean(values, axis=1, keepdims=True)
    inverse = lax.rsqrt(jnp.mean(centre * centre, axis=1, keepdims=True) + eps_norm)
    normed = (centre * inverse * gain[...] + shift[...]).astype(bf16)
    normed_ref[...] = normed
    width = heads * HEAD
    qkv = mat(normed, qkv_weight[...]) + bias[...]
    tables = [placed_table(ref, marks_ref, group, rows) for ref in (cos_ref, ahead_ref, behind_ref)]
    query = rotate(qkv[:, :width], *tables).astype(bf16)
    key_rows = rotate(qkv[:, width : 2 * width], *tables).astype(bf16)
    value = qkv[:, 2 * width :].astype(bf16)
    qkv_ref[:, :width] = query
    qkv_ref[:, width : 2 * width] = key_rows
    qkv_ref[:, 2 * width :] = value
    allowed = allowed_pairs(marks_ref, group, rows)
    masks = head_masks((rows, width), heads)
    factor = jnp.asarray(HEAD ** (-0.5), bf16)
    probs = softmax_of(stacked(query * factor, masks), key_rows, allowed).astype(bf16)
    mixed = of_heads(mat(probs, value), masks).astype(bf16)
    mixed_ref[...] = mixed
    part_ref[...] = mat(mixed, out_weight[...]).astype(bf16)


def feed_both(count, first, rows, half, *refs):
    normed, refs = refs[:count], refs[count:]
    grads, refs = refs[:5], refs[5:]
    weights = refs[0]
    refs = refs[1 if first else 5 :]
    normed_ref, grad_ref, hidden_ref, both_ref, back_ref, down_ref = refs[:6]
    normed_rows, grad_rows, gate_weight, up_weight, down_weight = refs[6:11]
    normed_sems, grad_sems, weight_sems, keep_sems = refs[11:]
    step = pl.program_id(0)
    groups = rows * GROUPS // normed_rows.shape[0]
    steps = GROUPS // groups
    place = pl.ds(half * normed_rows.shape[0], normed_rows.shape[0])
    kept = [
        pltpu.make_async_copy(normed_rows, normed_ref.at[place], keep_sems.at[0]),
        pltpu.make_async_copy(grad_rows, grad_ref.at[place], keep_sems.at[1]),
    ]
    size = gate_weight.shape[0] // LINE
    loads = [
        [
            pltpu.make_async_copy(
                weights.at[place, index],
                target.at[pl.ds(place * size, size)],
                weight_sems.at[LINE * index + place],
            )
            for place in range(LINE)
        ]
        for index, target in enumerate((gate_weight, up_weight, down_weight))
    ]
    lines = [
        line_copies(normed, normed_rows, normed_sems),
        line_copies(grads, grad_rows, grad_sems),
    ]

    @pl.when(step == 0)
    def _():
        for copy in loads[0]:
            copy.start()

    begin_lines(step, lines)

    @pl.when(step == 0)
    def _():
        for copy in loads[1] + loads[2]:
            copy.start()
        for copy in loads[0]:
            copy.wait()

    await_lines(step, steps, rows, lines)
    keep_rows(step, steps, kept)
    here = pl.ds(pl.multiple_of(step * rows, rows), rows)
    values = normed_rows[here, :]
    gate = mat(values, gate_weight[...])

    @pl.when(step == 0)
    def _():
        for copy in loads[1] + loads[2]:
            copy.wait()

    upward = mat(values, up_weight[...])
    sigma = 0.5 + 0.5 * jnp.tanh(0.5 * gate)
    gated = gate * sigma
    hidden = (gated * upward).astype(bf16)
    hidden_ref[...] = hidden
    grad_low = grad_rows[here, :]
    grad_hidden = mat(grad_low, down_weight[...])
    grad_gate = (grad_hidden * upward * (sigma + gated * (1.0 - sigma))).astype(bf16)
    grad_up = (grad_hidden * gated).astype(bf16)
    columns = hidden.shape[1]
    both_ref[:, :columns] = grad_gate
    both_ref[:, columns:] = grad_up
    back_ref[...] = (
        mat_cols(grad_gate, gate_weight[...]) + mat_cols(grad_up, up_weight[...])
    ).astype(bf16)
    down_ref[...] = mat_cols(hidden, down_weight[...]).astype(bf16)
    await_kept(step, steps, kept)


def attend_backward(first, heads, rows, half, marks_ref, *refs):
    branch = refs[0:8]
    saved, qkv_weight, out_weight, cos_ref, ahead_ref, behind_ref = refs[8:14]
    refs = refs[14 if first else 16 :]
    branch_ref, grad_ref, early_ref, late_ref, branch_rows, line_sems, keep_sems = refs
    step = pl.program_id(0)
    group = half * GROUPS + step
    line = line_copies(branch, branch_rows, line_sems)
    place = pl.ds(half * GROUPS * rows, GROUPS * rows)
    kept = [pltpu.make_async_copy(branch_rows, branch_ref.at[place], keep_sems.at[0])]
    begin_lines(step, [line])
    await_lines(step, GROUPS, rows, [line])
    keep_rows(step, GROUPS, kept)
    values = branch_rows[pl.ds(pl.multiple_of(step * rows, rows), rows), :]
    width = heads * HEAD
    factor = jnp.asarray(HEAD ** (-0.5), bf16)
    grad_mixed = mat_cols(values, out_weight[...]).astype(bf16)
    query = saved[:, :width]
    key_rows = saved[:, width : 2 * width]
    value = saved[:, 2 * width :]
    allowed = allowed_pairs(marks_ref, group, rows)
    masks = head_masks((rows, width), heads)
    query_stack = stacked(query * factor, masks)
    mixed_stack = stacked(grad_mixed, masks)
    probs = softmax_of(query_stack, key_rows, allowed)
    grad_probs = mat_cols(mixed_stack, value)
    inner = jnp.sum(grad_probs * probs, axis=1, keepdims=True)
    grad_scores = (probs * (grad_probs - inner)).astype(bf16)
    grad_query = of_heads(mat(grad_scores, key_rows * factor), masks)
    grad_key = mat_rows(grad_scores, query_stack)
    grad_value = mat_rows(probs.astype(bf16), mixed_stack)
    cosine, ahead, behind = (
        placed_table(ref, marks_ref, group, rows) for ref in (cos_ref, ahead_ref, behind_ref)
    )
    grads = jnp.concatenate(
        [
            rotate(grad_query, cosine, -ahead, -behind),
            rotate(grad_key, cosine, -ahead, -behind),
            grad_value,
        ],
        axis=1,
    ).astype(bf16)
    grad_ref[...] = grads
    part = mat_cols(grads, qkv_weight[...]).astype(bf16)

    @pl.when(step < GROUPS // 2)
    def _():
        early_ref[...] = part

    @pl.when(step >= GROUPS // 2)
    def _():
        late_ref[...] = part

    await_kept(step, GROUPS, kept)


def run_half(body, scalars, loose, blocked, whole, outputs, scratch, half, rows, prior, flops=1, steps=GROUPS, parted=0):
    loose, blocked, whole = list(loose), list(blocked), list(whole)
    kept = list(prior or [])
    out_shape, out_specs = [], []
    for width, shared, by_copy in outputs:
        total = 2 * steps if shared else steps
        offset = half * steps if shared else 0
        out_shape.append(jax.ShapeDtypeStruct((total * rows, width), bf16))
        block = pl.BlockSpec((rows, width), lambda i, *_, offset=offset: (i + offset, 0))
        out_specs.append(ANYWHERE if by_copy else block)
    if parted:
        out_shape += [jax.ShapeDtypeStruct((steps // 2 * rows, parted), bf16)] * 2
        out_specs += [
            pl.BlockSpec((rows, parted), lambda i, *_: (jnp.minimum(i, steps // 2 - 1), 0)),
            pl.BlockSpec((rows, parted), lambda i, *_: (jnp.maximum(i - steps // 2, 0), 0)),
        ]
    in_specs = [ANYWHERE] * len(loose)
    for values in blocked:
        in_specs.append(pl.BlockSpec((rows, values.shape[1]), lambda i, *_: (i + half * steps, 0)))
    for values in whole:
        in_specs.append(
            pl.BlockSpec(values.shape, lambda i, *_: (0, 0), pipeline_mode=pl.Buffered(1))
        )
    in_specs += [ANYWHERE] * len(kept)
    before = len(scalars) + len(loose) + len(blocked) + len(whole)
    return pl.pallas_call(
        body,
        grid_spec=pltpu.PrefetchScalarGridSpec(
            num_scalar_prefetch=len(scalars),
            grid=(steps,),
            in_specs=in_specs,
            out_specs=out_specs,
            scratch_shapes=scratch,
        ),
        out_shape=out_shape,
        input_output_aliases={before + index: index for index in range(len(kept))},
        compiler_params=pltpu.CompilerParams(
            dimension_semantics=("arbitrary",), vmem_limit_bytes=VMEM_BYTES
        ),
        cost_estimate=pl.CostEstimate(flops=flops, bytes_accessed=1, transcendentals=0),
    )(*scalars, *loose, *blocked, *whole, *kept)


def per_device(
    tokens,
    seq_lengths,
    block_counts,
    qkv_weight,
    qkv_bias,
    out_weight,
    norm1_gain,
    norm1_bias,
    gate_weight,
    up_weight,
    down_weight,
    norm2_gain,
    norm2_bias,
    out_grad,
):
    rows, width = tokens.shape
    share = norm1_gain.shape[0]
    bias_share = qkv_bias.shape[0]
    hidden_share = gate_weight.shape[1] // PARTS
    heads = width // HEAD // PARTS
    head_cols = heads * HEAD
    spread = lax.axis_size("s")
    iz = lax.axis_index("z")
    iy = lax.axis_index("y")
    ix = lax.axis_index("x")
    ic = lax.axis_index("c")
    me = iy * 4 + ix * 2 + ic

    def spread_gather(values, axis):
        return lax.all_gather(values, "s", axis=axis, tiled=True) if spread > 1 else values

    def spread_scatter(values, axis):
        if spread == 1:
            return values
        return lax.psum_scatter(values, "s", scatter_dimension=axis, tiled=True)

    own_marks = block_marks(seq_lengths[0], block_counts[0])
    packed = jnp.concatenate(
        [
            norm1_gain,
            norm1_bias,
            norm2_gain,
            norm2_bias,
            qkv_bias,
            seq_lengths[0].astype(bf16),
            block_counts.astype(bf16),
        ]
    )
    packed = jnp.pad(packed, (0, -packed.shape[0] % 128))[None, :]

    qkv_parts = (
        qkv_weight.reshape(share, 3 * heads, PARTS, HEAD)
        .transpose(2, 0, 1, 3)
        .reshape(PARTS, share, 3 * head_cols)
    )
    qkv_rows = exchange(send_pieces(block_of(qkv_parts), me), me, qkv_parts.shape)
    qkv_rows = spread_gather(qkv_rows, 1).reshape(-1, 3 * head_cols)
    qkv_full = gather_line(qkv_rows)
    out_full = gather_line(spread_gather(out_weight, 0))

    plane_pack = doubled(packed, "c", SWAP, ic == 1)
    plane_pack = doubled(plane_pack, "x", SWAP, ix == 1)
    plane_pack = doubled(plane_pack, "y", SWAP, iy == 1)
    all_pack = spread_gather(plane_pack[:, None], 1).reshape(PARTS * spread, -1)
    all_pack = doubled(all_pack, "z", NEAR, iz % 2 == 1)
    all_pack = doubled(all_pack, "z", FAR, iz >= 2)

    def vector(index):
        return all_pack[:, index * share : (index + 1) * share].reshape(1, width).astype(f32)

    gain_one, shift_one, gain_two, shift_two = (vector(index) for index in range(4))
    bias_full = all_pack[:, 4 * share : 4 * share + bias_share].reshape(3 * heads, PARTS, HEAD)
    bias_mine = (
        lax.dynamic_index_in_dim(bias_full, me, 1, keepdims=False)
        .reshape(1, 3 * head_cols)
        .astype(f32)
    )

    relative = [core + 4 * dy + 2 * dx for core in (0, 1) for dy in (0, 1) for dx in (0, 1)]
    marks = plane_pack[:, 4 * share + bias_share : 4 * share + bias_share + 3].astype(jnp.int32)
    marks = jnp.stack(
        [lax.dynamic_index_in_dim(marks, me ^ mask, 0, keepdims=False) for mask in relative]
    )
    marks = jax.vmap(block_marks)(marks[:, :2], marks[:, 2])
    tables = rotary_tables(rows, heads)

    mlp_parts = jnp.stack(
        [
            weight.reshape(share, PARTS, hidden_share).transpose(1, 0, 2)
            for weight in (gate_weight, up_weight, down_weight)
        ]
    )
    mlp_pairs = send_pieces(block_of(mlp_parts, axis=1), me)
    token_lines = gather_whole(tokens, mlp_pairs[0])
    mlp_rows = spread_gather(exchange(mlp_pairs, me, mlp_parts.shape), 2)
    mlp_full = gather_line(mlp_rows.reshape(-1, hidden_share))
    mlp_full = mlp_full.reshape(LINE, 3, -1, hidden_share)

    valid = valid_rows(own_marks, rows)[:, None]
    grad_top = jnp.where(valid, out_grad.astype(f32), 0.0)
    grad_lines = gather_whole(after(grad_top.astype(bf16), *token_lines[0][3:]))

    dma = pltpu.SemaphoreType.DMA
    line_rows = GROUPS * rows

    def attention(half, prior):
        return run_half(
            functools.partial(attend_forward, len(token_lines[half]), prior is None, heads, rows, half),
            (after(marks, mlp_rows, *grad_lines[0][:3]) if prior is None else marks,),
            token_lines[half],
            (),
            (qkv_full, out_full, gain_one, shift_one, bias_mine) + tables,
            (
                (width, True, False),
                (3 * head_cols, True, False),
                (head_cols, True, False),
                (width, False, False),
            ),
            [
                pltpu.VMEM((line_rows, width), bf16),
                dma((8,)),
            ],
            half,
            rows,
            prior,
        )

    *shared, out_sent = attention(1, None)
    normed_one, saved, mixed, out_kept = attention(0, shared)
    out_sent = after(out_sent, *grad_lines[0])
    inputs = tokens.astype(f32)
    middle = inputs + scatter_plane(out_kept, out_sent, rows)

    standard_two, inverse_two = standardize(middle)
    normed_lines = gather_plane((standard_two * gain_two + shift_two).astype(bf16))

    def feed(half, prior):
        return run_half(
            functools.partial(feed_both, len(normed_lines[half]), prior is None, 2 * rows, half),
            (),
            normed_lines[half] + grad_lines[half] + [mlp_full],
            (),
            (),
            ((width, True, True),) * 2
            + ((hidden_share, True, False), (2 * hidden_share, True, False))
            + ((width, False, False),) * 2,
            [pltpu.VMEM((line_rows, width), bf16)] * 2
            + [pltpu.VMEM((width, hidden_share), bf16)] * 3
            + [dma((8,)), dma((8,)), dma((3 * LINE,)), dma((2,))],
            half,
            2 * rows,
            prior,
            1,
            GROUPS // 2,
        )

    *shared, back_sent, down_sent = feed(1, None)
    normed_two, grad_low, hidden, grad_both, back_kept, down_kept = feed(0, shared)
    grad_normed_two, down_part, both_part = scatter_plane(
        back_kept,
        back_sent,
        rows,
        lambda *far: mat_rows(after(grad_low, *far), hidden).astype(bf16),
        lambda *near: mat_rows(after(normed_two, *near), grad_both).astype(bf16),
    )
    down_grad = scatter_line(down_part)
    both_grad = scatter_line(both_part)

    grad_middle_norm, gain_two_grad, shift_two_grad = norm_back(
        grad_normed_two, standard_two, inverse_two, gain_two
    )
    grad_middle = grad_top + grad_middle_norm
    branch_lines = gather_plane(grad_middle.astype(bf16))

    def attention_back(half, prior, *earlier):
        return run_half(
            functools.partial(attend_backward, prior is None, heads, rows, half),
            (after(marks, *earlier),),
            branch_lines[half],
            (saved,),
            (qkv_full, out_full) + tables,
            ((width, True, True), (3 * head_cols, True, False)),
            [
                pltpu.VMEM((line_rows, width), bf16),
                dma((8,)),
                dma((1,)),
            ],
            half,
            rows,
            prior,
            11 * line_rows * width * 4 * head_cols,
            GROUPS,
            width,
        )

    backs = []

    def back_first(*far):
        backs.append(attention_back(1, None, down_grad, *far))
        return backs[0][3]

    def back_second(*near):
        backs.append(attention_back(0, backs[0][:2], *near))
        return backs[1][3]

    down, _, _ = scatter_plane(
        down_kept, after(down_sent, grad_middle), rows, back_first, back_second
    )
    layer_out = jnp.where(valid, middle + down, 0.0).astype(bf16)
    grad_branch, grad_qkv, *input_kept = backs[1]
    input_sent = backs[0][2:]
    def back_blocks(values):
        return spread_scatter(values.reshape(PARTS, -1, values.shape[1]), 1)

    columns = PARTS * hidden_share
    mlp_pairs = send_pieces(
        block_of(back_blocks(down_grad), back_blocks(both_grad)), me
    )
    down_share, gate_share, up_share = exchange_columns(mlp_pairs, me, [(share, columns)] * 3)
    column_sums = jnp.sum(grad_qkv.astype(f32), axis=0)
    norm_one_grads = []

    def qkv_work(*far):
        part = mat_rows(after(normed_one, *far), grad_qkv).astype(bf16)
        weight = qkv_full.astype(f32)
        shift_grad = jnp.sum(weight * column_sums[None, :], axis=1)
        along = jnp.sum(weight * part.astype(f32), axis=1)
        norm_one_grads.append((along - shift_one[0] * shift_grad) / gain_one[0])
        norm_one_grads.append(shift_grad)
        return part

    near_rows = []

    def out_work(*near):
        near_rows.extend(near)
        return mat_rows(after(mixed, *near), grad_branch).astype(bf16)

    grad_normed_one, qkv_part, out_part = scatter_plane(
        list(input_kept),
        list(input_sent),
        rows,
        qkv_work,
        out_work,
        (both_grad, down),
    )
    qkv_grad = scatter_line(qkv_part)
    bias_part = column_sums.reshape(3 * heads, 1, HEAD)
    bias_grad = jnp.where(
        lax.broadcasted_iota(jnp.int32, (3 * heads, PARTS, HEAD), 1) == me, bias_part, 0.0
    )

    gain_one_grad, shift_one_grad = norm_one_grads
    devices = LINE * PARTS * spread
    small = jnp.concatenate(
        [
            part.reshape(devices, -1)
            for part in (gain_one_grad, shift_one_grad, gain_two_grad, shift_two_grad, bias_grad)
        ],
        axis=1,
    )
    small = halved(after(small, *near_rows), "z", FAR, iz >= 2)
    small = halved(small, "z", NEAR, iz % 2 == 1)
    small = halved(small, "y", SWAP, iy == 1)
    small = halved(small, "x", SWAP, ix == 1)
    small = halved(small, "c", SWAP, ic == 1)
    small = spread_scatter(small, 0)[0]

    standard_one, inverse_one = standardize(inputs)
    grad_input_norm, _, _ = norm_back(
        grad_normed_one, standard_one, inverse_one, gain_one
    )
    tokens_grad = (grad_middle + grad_input_norm).astype(bf16)

    qkv_pieces = send_pieces(block_of(back_blocks(after(qkv_grad, *mlp_pairs[1:]))), me)
    (qkv_share,) = exchange_columns(qkv_pieces, me, [(share, 3 * width)], 3 * heads)
    out_grad_weight = scatter_line(after(out_part, qkv_grad))
    out_share = spread_scatter(out_grad_weight, 0).astype(f32)
    return (
        layer_out,
        tokens_grad,
        qkv_share,
        small[4 * share :],
        out_share,
        small[:share],
        small[share : 2 * share],
        gate_share,
        up_share,
        down_share,
        small[2 * share : 3 * share],
        small[3 * share : 4 * share],
    )


def solution(mesh):
    devices = mesh.devices.reshape(LINE, 2, 2, 2, -1)
    rows, flat = P(AXES, None), P(AXES)
    return jax.shard_map(
        per_device,
        mesh=Mesh(devices, AXES),
        in_specs=(
            rows,
            rows,
            flat,
            rows,
            flat,
            rows,
            flat,
            flat,
            rows,
            rows,
            rows,
            flat,
            flat,
            rows,
        ),
        out_specs=(rows, rows, rows, flat, rows, flat, flat, rows, rows, rows, flat, flat),
        check_vma=False,
    )
```

```python
import functools

import jax
import jax.numpy as jnp
from jax import lax
from jax.experimental import pallas as pl
from jax.experimental.pallas import tpu as pltpu
from jax.sharding import Mesh, PartitionSpec as P

HEAD = 64
ROT = 16
BLOCK = 128
PARTS = 8
CHIPS = 4
LINE = 4
GROUPS = 4

AXES = ("z", "y", "x", "c", "s")
PLANE = ("y", "x", "c")
SWAP = ((0, 1), (1, 0))
NEAR = ((0, 1), (1, 0), (2, 3), (3, 2))
FAR = ((0, 2), (1, 3), (2, 0), (3, 1))

eps_norm = 1e-05
f32 = jnp.float32
bf16 = jnp.bfloat16
VMEM_BYTES = 56 * 1024 * 1024
ANYWHERE = pl.BlockSpec(memory_space=pl.ANY)


def mat_rows(left, right):
    return lax.dot_general(left, right, (((0,), (0,)), ((), ())), preferred_element_type=f32)


def mat_cols(left, right):
    return lax.dot_general(left, right, (((1,), (1,)), ((), ())), preferred_element_type=f32)


def mat(left, right):
    return jnp.dot(left, right, preferred_element_type=f32)


def over_x(values):
    return lax.ppermute(values, "x", SWAP)


def over_y(values):
    return lax.ppermute(values, "y", SWAP)


def over_c(values):
    return lax.ppermute(values, "c", SWAP)


def gather_line(values):
    return lax.all_gather(values, "z", axis=0, tiled=True)


def scatter_line(values):
    return lax.psum_scatter(values.astype(bf16), "z", scatter_dimension=0, tiled=True)


def after(values, *earlier):
    return lax.optimization_barrier((values, *earlier))[0]


def gather_plane(values, *earlier):
    half = values.shape[0] // 2
    low, high = values[:half], values[half:]
    y_low, x_high = over_y(low), over_x(high)
    x_low, y_high = over_x(low), over_y(high)
    to_x, to_y = y_low, x_high
    if earlier:
        to_x, to_y, *_ = lax.optimization_barrier((to_x, to_y, *earlier))
    line = [low, high, x_low, x_high, y_low, y_high, over_x(to_x), over_y(to_y)]
    return line, [over_c(part) for part in line]


def gather_whole(values, *earlier):
    half = values.shape[0] // 2
    from_x, from_y = over_x(values), over_y(values)
    to_x, to_y = from_y[:half], from_x[half:]
    if earlier:
        to_x, to_y, *_ = lax.optimization_barrier((to_x, to_y, *earlier))
    line = [values, from_x, from_y, over_x(to_x), over_y(to_y)]
    return line, [over_c(part) for part in line]


def scatter_plane(kept, sent, rows, first=None, second=None, also=()):
    half = rows // 2
    kept, sent = (parts if isinstance(parts, list) else [parts] for parts in (kept, sent))
    came = [over_c(part) for part in sent]

    def rows_of(parts, low, high):
        size = parts[0].shape[0]
        return parts[low // size][low % size : low % size + high - low].astype(f32)

    def joined(low, high):
        return rows_of(kept, low, high) + rows_of(came, low, high)

    far_low = joined(3 * rows, 3 * rows + half).astype(bf16)
    far_high = joined(3 * rows + half, 4 * rows).astype(bf16)
    done = []
    if first is not None:
        done.append(first(far_low, far_high))
    low, high = over_x(far_low), over_y(far_high)
    if done:
        low, high, *_ = lax.optimization_barrier((low, high, done[0], *also))
    near_x = jnp.concatenate(
        [joined(rows, rows + half), joined(rows + half, 2 * rows) + high.astype(f32)], axis=0
    ).astype(bf16)
    near_y = jnp.concatenate(
        [joined(2 * rows, 2 * rows + half) + low.astype(f32), joined(2 * rows + half, 3 * rows)],
        axis=0,
    ).astype(bf16)
    if second is not None:
        done.append(second(near_x, near_y))
    last_x, last_y = over_x(near_x), over_y(near_y)
    if second is not None:
        last_x, last_y, _ = lax.optimization_barrier((last_x, last_y, done[-1]))
    total = joined(0, rows) + last_x.astype(f32) + last_y.astype(f32)
    return (total, *done) if done else total


def members(refs):
    return [(2 * chip + core, refs[chip].at[core]) for chip in range(CHIPS) for core in (0, 1)]


def place_pieces(me_ref, *refs):
    result = refs[CHIPS]
    for mask, piece in members(refs):
        there = jnp.bitwise_xor(me_ref[0], mask)
        if len(result.shape) == 4:
            for index in range(result.shape[0]):
                result[index, there] = piece[index]
        else:
            result[there] = piece[...]


def place_columns(chunks, me_ref, *refs):
    results, held = refs[CHIPS:-1], refs[-1]
    for mask, piece in members(refs):
        held[jnp.bitwise_xor(me_ref[0], mask)] = piece[...]
    offset = 0
    for result in results:
        size = result.shape[1] // (PARTS * chunks)
        for chunk in range(chunks):
            parts = [held[member, :, offset : offset + size] for member in range(PARTS)]
            joined = jnp.concatenate(parts, axis=1).astype(f32)
            result[:, chunk * PARTS * size : (chunk + 1) * PARTS * size] = joined
            offset += size


def send_pieces(block, me):
    chip, core = me // 2, me % 2
    to_other = jnp.stack([block((chip ^ away) * 2 + 1 - core) for away in range(CHIPS)])
    came = over_c(to_other)
    pairs = []
    for away in range(CHIPS):
        pair = jnp.stack([block((chip ^ away) * 2 + core), came[away]])
        if away:
            pair = lax.ppermute(pair, ("y", "x"), [(i, i ^ away) for i in range(CHIPS)])
        pairs.append(pair)
    return pairs


def block_of(*arrays, axis=0):
    def block(index):
        parts = [lax.dynamic_index_in_dim(a, index, axis, keepdims=False) for a in arrays]
        return parts[0] if len(parts) == 1 else jnp.concatenate(parts, axis=-1)

    return block


def collect(body, pairs, me, shapes, scratch=()):
    whole = pl.BlockSpec(memory_space=pltpu.VMEM)
    size = 3 * pairs[0].dtype.itemsize * CHIPS * pairs[0].size
    return pl.pallas_call(
        body,
        in_specs=[pl.BlockSpec(memory_space=pltpu.SMEM)] + [whole] * CHIPS,
        out_specs=[whole] * len(shapes),
        scratch_shapes=scratch,
        compiler_params=pltpu.CompilerParams(vmem_limit_bytes=24 * 1024 * 1024),
        out_shape=shapes,
        cost_estimate=pl.CostEstimate(flops=0, bytes_accessed=size, transcendentals=0),
    )(me.astype(jnp.int32).reshape(1), *pairs)


def exchange(pairs, me, shape):
    return collect(place_pieces, pairs, me, [jax.ShapeDtypeStruct(shape, pairs[0].dtype)])[0]


def exchange_columns(pairs, me, shapes, chunks=1):
    return collect(
        functools.partial(place_columns, chunks),
        pairs,
        me,
        [jax.ShapeDtypeStruct(shape, f32) for shape in shapes],
        [pltpu.VMEM((PARTS,) + pairs[0].shape[1:], pairs[0].dtype)],
    )


def doubled(values, axis, perm, upper):
    other = lax.ppermute(values, axis, perm)
    return jnp.where(
        upper,
        jnp.concatenate([other, values], axis=0),
        jnp.concatenate([values, other], axis=0),
    )


def halved(values, axis, perm, upper):
    half = values.shape[0] // 2
    low, high = values[:half], values[half:]
    came = lax.ppermute(jnp.where(upper, low, high), axis, perm)
    return jnp.where(upper, high, low) + came


def standardize(values):
    centre = values - jnp.mean(values, axis=1, keepdims=True)
    inverse = lax.rsqrt(jnp.mean(centre * centre, axis=1, keepdims=True) + eps_norm)
    return (centre * inverse, inverse)


def norm_back(grad_out, standard, inverse, gain):
    scaled = grad_out * gain
    inner = jnp.mean(scaled, axis=1, keepdims=True)
    along = jnp.mean(scaled * standard, axis=1, keepdims=True)
    return (
        inverse * (scaled - inner - standard * along),
        jnp.sum(grad_out * standard, axis=0),
        jnp.sum(grad_out, axis=0),
    )


def block_marks(lengths, used_blocks):
    index = jnp.arange(lengths.shape[0], dtype=jnp.int32)
    began = jnp.max(
        jnp.where((lengths[None, :] > 0) & (index[None, :] <= index[:, None]), index[None, :], 0),
        axis=1,
    )
    limit = jnp.sum(jnp.where(index[None, :] == began[:, None], lengths[None, :], 0), axis=1)
    return jnp.stack([began, limit, (index < used_blocks).astype(jnp.int32)], axis=1).reshape(-1)


def valid_rows(marks, row_count):
    marks = marks.reshape(-1, 3)
    row = jnp.arange(row_count, dtype=jnp.int32)
    began, limit, used = (jnp.repeat(marks[:, index], BLOCK) for index in range(3))
    return (row - began * BLOCK < limit) & (used > 0)


def rotary_tables(row_count, heads):
    half_rot = ROT // 2
    freqs = 10000.0 ** (-2.0 * jnp.arange(half_rot, dtype=f32) / ROT)
    angle = jnp.arange(row_count, dtype=f32)[:, None] * freqs[None, :]
    cosine, sine = jnp.cos(angle), jnp.sin(angle)
    zero = jnp.zeros((row_count, HEAD - ROT), f32)
    none = jnp.zeros_like(sine)
    return tuple(
        jnp.tile(jnp.concatenate(parts, axis=1), (1, heads))
        for parts in (
            [cosine, cosine, zero + 1.0],
            [-sine, none, zero],
            [none, sine, zero],
        )
    )


def line_copies(pieces, target, sems):
    copies, offset = [], 0
    for index, piece in enumerate(pieces):
        size = piece.shape[0]
        copy = pltpu.make_async_copy(piece, target.at[pl.ds(offset, size)], sems.at[index])
        copies.append((copy, offset))
        offset += size
    return copies


def begin_lines(step, lines):
    @pl.when(step == 0)
    def _():
        for copies in lines:
            for copy, _ in copies:
                copy.start()


def await_lines(step, steps, rows, lines):
    for index in range(steps):

        @pl.when(step == index)
        def _(index=index):
            for copies in lines:
                for copy, offset in copies:
                    if offset // rows == index:
                        copy.wait()


def keep_rows(step, steps, pairs):
    @pl.when(step == steps - 1)
    def _():
        for copy in pairs:
            copy.start()


def await_kept(step, steps, pairs):
    @pl.when(step == steps - 1)
    def _():
        for copy in pairs:
            copy.wait()


def row_marks(marks, group, shape, axis):
    place = lax.broadcasted_iota(jnp.int32, shape, axis)
    key = jnp.zeros(shape, jnp.int32)
    for index in range(shape[axis] // BLOCK):
        began = marks[group, 3 * index]
        limit = marks[group, 3 * index + 1]
        used = marks[group, 3 * index + 2]
        inside = jnp.logical_and(place >= index * BLOCK, place < (index + 1) * BLOCK)
        last = jnp.where(used > 0, began * BLOCK + limit, 0)
        seen = jnp.where(place < last, began, -1 - axis)
        key = jnp.where(inside, seen, key)
    return place, key


def allowed_pairs(marks, group, rows):
    row, row_key = row_marks(marks, group, (rows, 1), 0)
    column, column_key = row_marks(marks, group, (1, rows), 1)
    row = jnp.broadcast_to(row, (rows, rows))
    column = jnp.broadcast_to(column, (rows, rows))
    same = jnp.broadcast_to(row_key, (rows, rows)) == jnp.broadcast_to(column_key, (rows, rows))
    return jnp.logical_or(jnp.logical_and(same, column <= row), row == column)


def placed_table(table, marks, group, rows):
    parts = []
    for index in range(rows // BLOCK):
        start = pl.multiple_of((index - marks[group, 3 * index]) * BLOCK, BLOCK)
        parts.append(table[pl.ds(start, BLOCK), :])
    return jnp.concatenate(parts, axis=0)


def rotate(values, cosine, ahead, behind):
    width = values.shape[1]
    half_rot = ROT // 2
    return (
        values * cosine
        + pltpu.roll(values, width - half_rot, 1) * ahead
        + pltpu.roll(values, half_rot, 1) * behind
    )


def head_masks(shape, heads):
    lane = lax.broadcasted_iota(jnp.int32, shape, 1)
    return [
        jnp.logical_and(lane >= index * HEAD, lane < (index + 1) * HEAD) for index in range(heads)
    ]


def stacked(values, masks):
    return jnp.concatenate([jnp.where(mask, values, 0) for mask in masks], axis=0)


def of_heads(values, masks):
    rows = values.shape[0] // len(masks)
    result = jnp.zeros((rows, values.shape[1]), values.dtype)
    for index, mask in enumerate(masks):
        result = jnp.where(mask, values[index * rows : (index + 1) * rows], result)
    return result


def softmax_of(query_stack, key_rows, allowed):
    rows = key_rows.shape[0]
    scores = mat_cols(query_stack, key_rows).reshape(-1, rows, rows)
    scores = jnp.where(allowed[None], scores, -1e30)
    expo = jnp.exp(scores - jnp.max(scores, axis=2, keepdims=True))
    return (expo * (1.0 / jnp.sum(expo, axis=2, keepdims=True))).reshape(-1, rows)


def attend_forward(count, first, heads, rows, half, marks_ref, *refs):
    tokens, refs = refs[:count], refs[count:]
    qkv_weight, out_weight, gain, shift, bias, cos_ref, ahead_ref, behind_ref = refs[:8]
    refs = refs[8 if first else 11 :]
    standard_ref, qkv_ref, mixed_ref, part_ref, token_rows, line_sems = refs
    step = pl.program_id(0)
    group = half * GROUPS + step
    line = line_copies(tokens, token_rows, line_sems)
    begin_lines(step, [line])
    await_lines(step, GROUPS, rows, [line])
    values = token_rows[pl.ds(pl.multiple_of(step * rows, rows), rows), :].astype(f32)
    centre = values - jnp.mean(values, axis=1, keepdims=True)
    inverse = lax.rsqrt(jnp.mean(centre * centre, axis=1, keepdims=True) + eps_norm)
    standard = centre * inverse
    standard_ref[...] = standard.astype(bf16)
    normed = (standard * gain[...] + shift[...]).astype(bf16)
    width = heads * HEAD
    qkv = mat(normed, qkv_weight[...]) + bias[...]
    tables = [placed_table(ref, marks_ref, group, rows) for ref in (cos_ref, ahead_ref, behind_ref)]
    query = rotate(qkv[:, :width], *tables).astype(bf16)
    key_rows = rotate(qkv[:, width : 2 * width], *tables).astype(bf16)
    value = qkv[:, 2 * width :].astype(bf16)
    qkv_ref[:, :width] = query
    qkv_ref[:, width : 2 * width] = key_rows
    qkv_ref[:, 2 * width :] = value
    allowed = allowed_pairs(marks_ref, group, rows)
    masks = head_masks((rows, width), heads)
    factor = jnp.asarray(HEAD ** (-0.5), bf16)
    probs = softmax_of(stacked(query * factor, masks), key_rows, allowed).astype(bf16)
    mixed = of_heads(mat(probs, value), masks).astype(bf16)
    mixed_ref[...] = mixed
    part_ref[...] = mat(mixed, out_weight[...]).astype(bf16)


def feed_both(count, first, rows, half, *refs):
    normed, refs = refs[:count], refs[count:]
    grads, refs = refs[:5], refs[5:]
    weights = refs[0]
    refs = refs[1 if first else 5 :]
    normed_ref, grad_ref, hidden_ref, both_ref, back_ref, down_ref = refs[:6]
    normed_rows, grad_rows, gate_weight, up_weight, down_weight = refs[6:11]
    normed_sems, grad_sems, weight_sems, keep_sems = refs[11:]
    step = pl.program_id(0)
    groups = rows * GROUPS // normed_rows.shape[0]
    steps = GROUPS // groups
    place = pl.ds(half * normed_rows.shape[0], normed_rows.shape[0])
    kept = [
        pltpu.make_async_copy(normed_rows, normed_ref.at[place], keep_sems.at[0]),
        pltpu.make_async_copy(grad_rows, grad_ref.at[place], keep_sems.at[1]),
    ]
    size = gate_weight.shape[0] // LINE
    loads = [
        [
            pltpu.make_async_copy(
                weights.at[place, index],
                target.at[pl.ds(place * size, size)],
                weight_sems.at[LINE * index + place],
            )
            for place in range(LINE)
        ]
        for index, target in enumerate((gate_weight, up_weight, down_weight))
    ]
    lines = [
        line_copies(normed, normed_rows, normed_sems),
        line_copies(grads, grad_rows, grad_sems),
    ]

    @pl.when(step == 0)
    def _():
        for copy in loads[0]:
            copy.start()

    begin_lines(step, lines)

    @pl.when(step == 0)
    def _():
        for copy in loads[1] + loads[2]:
            copy.start()
        for copy in loads[0]:
            copy.wait()

    await_lines(step, steps, rows, lines)
    keep_rows(step, steps, kept)
    here = pl.ds(pl.multiple_of(step * rows, rows), rows)
    values = normed_rows[here, :]
    gate = mat(values, gate_weight[...])

    @pl.when(step == 0)
    def _():
        for copy in loads[1] + loads[2]:
            copy.wait()

    upward = mat(values, up_weight[...])
    sigma = 0.5 + 0.5 * jnp.tanh(0.5 * gate)
    gated = gate * sigma
    hidden = (gated * upward).astype(bf16)
    hidden_ref[...] = hidden
    grad_low = grad_rows[here, :]
    grad_hidden = mat(grad_low, down_weight[...])
    grad_gate = (grad_hidden * upward * (sigma + gated * (1.0 - sigma))).astype(bf16)
    grad_up = (grad_hidden * gated).astype(bf16)
    columns = hidden.shape[1]
    both_ref[:, :columns] = grad_gate
    both_ref[:, columns:] = grad_up
    back_ref[...] = (
        mat_cols(grad_gate, gate_weight[...]) + mat_cols(grad_up, up_weight[...])
    ).astype(bf16)
    down_ref[...] = mat_cols(hidden, down_weight[...]).astype(bf16)
    await_kept(step, steps, kept)


def attend_backward(first, heads, rows, half, marks_ref, *refs):
    branch = refs[0:8]
    saved, qkv_weight, out_weight, cos_ref, ahead_ref, behind_ref = refs[8:14]
    refs = refs[14 if first else 16 :]
    branch_ref, grad_ref, early_ref, late_ref, branch_rows, line_sems, keep_sems = refs
    step = pl.program_id(0)
    group = half * GROUPS + step
    line = line_copies(branch, branch_rows, line_sems)
    place = pl.ds(half * GROUPS * rows, GROUPS * rows)
    kept = [pltpu.make_async_copy(branch_rows, branch_ref.at[place], keep_sems.at[0])]
    begin_lines(step, [line])
    await_lines(step, GROUPS, rows, [line])
    keep_rows(step, GROUPS, kept)
    values = branch_rows[pl.ds(pl.multiple_of(step * rows, rows), rows), :]
    width = heads * HEAD
    factor = jnp.asarray(HEAD ** (-0.5), bf16)
    grad_mixed = mat_cols(values, out_weight[...]).astype(bf16)
    query = saved[:, :width]
    key_rows = saved[:, width : 2 * width]
    value = saved[:, 2 * width :]
    allowed = allowed_pairs(marks_ref, group, rows)
    masks = head_masks((rows, width), heads)
    query_stack = stacked(query * factor, masks)
    mixed_stack = stacked(grad_mixed, masks)
    probs = softmax_of(query_stack, key_rows, allowed)
    grad_probs = mat_cols(mixed_stack, value)
    inner = jnp.sum(grad_probs * probs, axis=1, keepdims=True)
    grad_scores = (probs * (grad_probs - inner)).astype(bf16)
    grad_query = of_heads(mat(grad_scores, key_rows * factor), masks)
    grad_key = mat_rows(grad_scores, query_stack)
    grad_value = mat_rows(probs.astype(bf16), mixed_stack)
    cosine, ahead, behind = (
        placed_table(ref, marks_ref, group, rows) for ref in (cos_ref, ahead_ref, behind_ref)
    )
    grads = jnp.concatenate(
        [
            rotate(grad_query, cosine, -ahead, -behind),
            rotate(grad_key, cosine, -ahead, -behind),
            grad_value,
        ],
        axis=1,
    ).astype(bf16)
    grad_ref[...] = grads
    part = mat_cols(grads, qkv_weight[...]).astype(bf16)

    @pl.when(step < GROUPS // 2)
    def _():
        early_ref[...] = part

    @pl.when(step >= GROUPS // 2)
    def _():
        late_ref[...] = part

    await_kept(step, GROUPS, kept)


def run_half(body, scalars, loose, blocked, whole, outputs, scratch, half, rows, prior, flops=1, steps=GROUPS, parted=0):
    loose, blocked, whole = list(loose), list(blocked), list(whole)
    kept = list(prior or [])
    out_shape, out_specs = [], []
    for width, shared, by_copy in outputs:
        total = 2 * steps if shared else steps
        offset = half * steps if shared else 0
        out_shape.append(jax.ShapeDtypeStruct((total * rows, width), bf16))
        block = pl.BlockSpec((rows, width), lambda i, *_, offset=offset: (i + offset, 0))
        out_specs.append(ANYWHERE if by_copy else block)
    if parted:
        out_shape += [jax.ShapeDtypeStruct((steps // 2 * rows, parted), bf16)] * 2
        out_specs += [
            pl.BlockSpec((rows, parted), lambda i, *_: (jnp.minimum(i, steps // 2 - 1), 0)),
            pl.BlockSpec((rows, parted), lambda i, *_: (jnp.maximum(i - steps // 2, 0), 0)),
        ]
    in_specs = [ANYWHERE] * len(loose)
    for values in blocked:
        in_specs.append(pl.BlockSpec((rows, values.shape[1]), lambda i, *_: (i + half * steps, 0)))
    for values in whole:
        in_specs.append(
            pl.BlockSpec(values.shape, lambda i, *_: (0, 0), pipeline_mode=pl.Buffered(1))
        )
    in_specs += [ANYWHERE] * len(kept)
    before = len(scalars) + len(loose) + len(blocked) + len(whole)
    return pl.pallas_call(
        body,
        grid_spec=pltpu.PrefetchScalarGridSpec(
            num_scalar_prefetch=len(scalars),
            grid=(steps,),
            in_specs=in_specs,
            out_specs=out_specs,
            scratch_shapes=scratch,
        ),
        out_shape=out_shape,
        input_output_aliases={before + index: index for index in range(len(kept))},
        compiler_params=pltpu.CompilerParams(
            dimension_semantics=("arbitrary",), vmem_limit_bytes=VMEM_BYTES
        ),
        cost_estimate=pl.CostEstimate(flops=flops, bytes_accessed=1, transcendentals=0),
    )(*scalars, *loose, *blocked, *whole, *kept)


def per_device(
    tokens,
    seq_lengths,
    block_counts,
    qkv_weight,
    qkv_bias,
    out_weight,
    norm1_gain,
    norm1_bias,
    gate_weight,
    up_weight,
    down_weight,
    norm2_gain,
    norm2_bias,
    out_grad,
):
    rows, width = tokens.shape
    share = norm1_gain.shape[0]
    bias_share = qkv_bias.shape[0]
    hidden_share = gate_weight.shape[1] // PARTS
    heads = width // HEAD // PARTS
    head_cols = heads * HEAD
    spread = lax.axis_size("s")
    iz = lax.axis_index("z")
    iy = lax.axis_index("y")
    ix = lax.axis_index("x")
    ic = lax.axis_index("c")
    me = iy * 4 + ix * 2 + ic

    def spread_gather(values, axis):
        return lax.all_gather(values, "s", axis=axis, tiled=True) if spread > 1 else values

    def spread_scatter(values, axis):
        if spread == 1:
            return values
        return lax.psum_scatter(values, "s", scatter_dimension=axis, tiled=True)

    own_marks = block_marks(seq_lengths[0], block_counts[0])
    packed = jnp.concatenate(
        [
            norm1_gain,
            norm1_bias,
            norm2_gain,
            norm2_bias,
            qkv_bias,
            seq_lengths[0].astype(bf16),
            block_counts.astype(bf16),
        ]
    )
    packed = jnp.pad(packed, (0, -packed.shape[0] % 128))[None, :]

    qkv_parts = (
        qkv_weight.reshape(share, 3 * heads, PARTS, HEAD)
        .transpose(2, 0, 1, 3)
        .reshape(PARTS, share, 3 * head_cols)
    )
    qkv_rows = exchange(send_pieces(block_of(qkv_parts), me), me, qkv_parts.shape)
    qkv_rows = spread_gather(qkv_rows, 1).reshape(-1, 3 * head_cols)
    qkv_full = gather_line(qkv_rows)
    out_full = gather_line(spread_gather(out_weight, 0))

    plane_pack = doubled(packed, "c", SWAP, ic == 1)
    plane_pack = doubled(plane_pack, "x", SWAP, ix == 1)
    plane_pack = doubled(plane_pack, "y", SWAP, iy == 1)
    all_pack = spread_gather(plane_pack[:, None], 1).reshape(PARTS * spread, -1)
    all_pack = doubled(all_pack, "z", NEAR, iz % 2 == 1)
    all_pack = doubled(all_pack, "z", FAR, iz >= 2)

    def vector(index):
        return all_pack[:, index * share : (index + 1) * share].reshape(1, width).astype(f32)

    gain_one, shift_one, gain_two, shift_two = (vector(index) for index in range(4))
    bias_full = all_pack[:, 4 * share : 4 * share + bias_share].reshape(3 * heads, PARTS, HEAD)
    bias_mine = (
        lax.dynamic_index_in_dim(bias_full, me, 1, keepdims=False)
        .reshape(1, 3 * head_cols)
        .astype(f32)
    )

    relative = [core + 4 * dy + 2 * dx for core in (0, 1) for dy in (0, 1) for dx in (0, 1)]
    marks = plane_pack[:, 4 * share + bias_share : 4 * share + bias_share + 3].astype(jnp.int32)
    marks = jnp.stack(
        [lax.dynamic_index_in_dim(marks, me ^ mask, 0, keepdims=False) for mask in relative]
    )
    marks = jax.vmap(block_marks)(marks[:, :2], marks[:, 2])
    tables = rotary_tables(rows, heads)

    mlp_parts = jnp.stack(
        [
            weight.reshape(share, PARTS, hidden_share).transpose(1, 0, 2)
            for weight in (gate_weight, up_weight, down_weight)
        ]
    )
    mlp_pairs = send_pieces(block_of(mlp_parts, axis=1), me)
    token_lines = gather_whole(tokens, mlp_pairs[0])
    mlp_rows = spread_gather(exchange(mlp_pairs, me, mlp_parts.shape), 2)
    mlp_full = gather_line(mlp_rows.reshape(-1, hidden_share))
    mlp_full = mlp_full.reshape(LINE, 3, -1, hidden_share)

    valid = valid_rows(own_marks, rows)[:, None]
    grad_top = jnp.where(valid, out_grad.astype(f32), 0.0)
    grad_lines = gather_whole(after(grad_top.astype(bf16), *token_lines[0][3:]))

    dma = pltpu.SemaphoreType.DMA
    line_rows = GROUPS * rows

    def attention(half, prior):
        return run_half(
            functools.partial(attend_forward, len(token_lines[half]), prior is None, heads, rows, half),
            (after(marks, mlp_rows, *grad_lines[0][:3]) if prior is None else marks,),
            token_lines[half],
            (),
            (qkv_full, out_full, gain_one, shift_one, bias_mine) + tables,
            (
                (width, True, False),
                (3 * head_cols, True, False),
                (head_cols, True, False),
                (width, False, False),
            ),
            [
                pltpu.VMEM((line_rows, width), bf16),
                dma((8,)),
            ],
            half,
            rows,
            prior,
        )

    *shared, out_sent = attention(1, None)
    standard_rows, saved, mixed, out_kept = attention(0, shared)
    out_sent = after(out_sent, *grad_lines[0])
    inputs = tokens.astype(f32)
    middle = inputs + scatter_plane(out_kept, out_sent, rows)

    standard_two, inverse_two = standardize(middle)
    normed_lines = gather_plane((standard_two * gain_two + shift_two).astype(bf16))

    def feed(half, prior):
        return run_half(
            functools.partial(feed_both, len(normed_lines[half]), prior is None, 2 * rows, half),
            (),
            normed_lines[half] + grad_lines[half] + [mlp_full],
            (),
            (),
            ((width, True, True),) * 2
            + ((hidden_share, True, False), (2 * hidden_share, True, False))
            + ((width, False, False),) * 2,
            [pltpu.VMEM((line_rows, width), bf16)] * 2
            + [pltpu.VMEM((width, hidden_share), bf16)] * 3
            + [dma((8,)), dma((8,)), dma((3 * LINE,)), dma((2,))],
            half,
            2 * rows,
            prior,
            1,
            GROUPS // 2,
        )

    *shared, back_sent, down_sent = feed(1, None)
    normed_two, grad_low, hidden, grad_both, back_kept, down_kept = feed(0, shared)
    grad_normed_two, down_part, both_part = scatter_plane(
        back_kept,
        back_sent,
        rows,
        lambda *far: mat_rows(after(grad_low, *far), hidden).astype(bf16),
        lambda *near: mat_rows(after(normed_two, *near), grad_both).astype(bf16),
    )
    down_grad = scatter_line(down_part)
    both_grad = scatter_line(both_part)

    grad_middle_norm, gain_two_grad, shift_two_grad = norm_back(
        grad_normed_two, standard_two, inverse_two, gain_two
    )
    grad_middle = grad_top + grad_middle_norm
    branch_lines = gather_plane(grad_middle.astype(bf16))

    def attention_back(half, prior, *earlier):
        return run_half(
            functools.partial(attend_backward, prior is None, heads, rows, half),
            (after(marks, *earlier),),
            branch_lines[half],
            (saved,),
            (qkv_full, out_full) + tables,
            ((width, True, True), (3 * head_cols, True, False)),
            [
                pltpu.VMEM((line_rows, width), bf16),
                dma((8,)),
                dma((1,)),
            ],
            half,
            rows,
            prior,
            11 * line_rows * width * 4 * head_cols,
            GROUPS,
            width,
        )

    backs = []

    def back_first(*far):
        backs.append(attention_back(1, None, down_grad, *far))
        return backs[0][3]

    def back_second(*near):
        backs.append(attention_back(0, backs[0][:2], *near))
        return backs[1][3]

    down, _, _ = scatter_plane(
        down_kept, after(down_sent, grad_middle), rows, back_first, back_second
    )
    layer_out = jnp.where(valid, middle + down, 0.0).astype(bf16)
    grad_branch, grad_qkv, *input_kept = backs[1]
    input_sent = backs[0][2:]
    def back_blocks(values):
        return spread_scatter(values.reshape(PARTS, -1, values.shape[1]), 1)

    columns = PARTS * hidden_share
    mlp_pairs = send_pieces(
        block_of(back_blocks(down_grad), back_blocks(both_grad)), me
    )
    down_share, gate_share, up_share = exchange_columns(mlp_pairs, me, [(share, columns)] * 3)
    column_sums = jnp.sum(grad_qkv.astype(f32), axis=0)
    norm_one_grads = []

    def qkv_work(*far):
        along = mat_rows(after(standard_rows, *far), grad_qkv).astype(bf16).astype(f32)
        weight = qkv_full.astype(f32)
        norm_one_grads.append(jnp.sum(weight * along, axis=1))
        norm_one_grads.append(jnp.sum(weight * column_sums[None, :], axis=1))
        return (gain_one.T * along + shift_one.T * column_sums[None, :]).astype(bf16)

    near_rows = []

    def out_work(*near):
        near_rows.extend(near)
        return mat_rows(after(mixed, *near), grad_branch).astype(bf16)

    grad_normed_one, qkv_part, out_part = scatter_plane(
        list(input_kept),
        list(input_sent),
        rows,
        qkv_work,
        out_work,
        (both_grad, down),
    )
    qkv_grad = scatter_line(qkv_part)
    bias_part = column_sums.reshape(3 * heads, 1, HEAD)
    bias_grad = jnp.where(
        lax.broadcasted_iota(jnp.int32, (3 * heads, PARTS, HEAD), 1) == me, bias_part, 0.0
    )

    gain_one_grad, shift_one_grad = norm_one_grads
    devices = LINE * PARTS * spread
    small = jnp.concatenate(
        [
            part.reshape(devices, -1)
            for part in (gain_one_grad, shift_one_grad, gain_two_grad, shift_two_grad, bias_grad)
        ],
        axis=1,
    )
    small = halved(after(small, *near_rows), "z", FAR, iz >= 2)
    small = halved(small, "z", NEAR, iz % 2 == 1)
    small = halved(small, "y", SWAP, iy == 1)
    small = halved(small, "x", SWAP, ix == 1)
    small = halved(small, "c", SWAP, ic == 1)
    small = spread_scatter(small, 0)[0]

    standard_one, inverse_one = standardize(inputs)
    grad_input_norm, _, _ = norm_back(
        grad_normed_one, standard_one, inverse_one, gain_one
    )
    tokens_grad = (grad_middle + grad_input_norm).astype(bf16)

    qkv_pieces = send_pieces(block_of(back_blocks(after(qkv_grad, *mlp_pairs[1:]))), me)
    (qkv_share,) = exchange_columns(qkv_pieces, me, [(share, 3 * width)], 3 * heads)
    out_grad_weight = scatter_line(after(out_part, qkv_grad))
    out_share = spread_scatter(out_grad_weight, 0).astype(f32)
    return (
        layer_out,
        tokens_grad,
        qkv_share,
        small[4 * share :],
        out_share,
        small[:share],
        small[share : 2 * share],
        gate_share,
        up_share,
        down_share,
        small[2 * share : 3 * share],
        small[3 * share : 4 * share],
    )


def solution(mesh):
    devices = mesh.devices.reshape(LINE, 2, 2, 2, -1)
    rows, flat = P(AXES, None), P(AXES)
    return jax.shard_map(
        per_device,
        mesh=Mesh(devices, AXES),
        in_specs=(
            rows,
            rows,
            flat,
            rows,
            flat,
            rows,
            flat,
            flat,
            rows,
            rows,
            rows,
            flat,
            flat,
            rows,
        ),
        out_specs=(rows, rows, rows, flat, rows, flat, flat, rows, rows, rows, flat, flat),
        check_vma=False,
    )
```
